32 devices in a mesh: dp: 4 (over x, core), fsdp: 8 (over z, y).
Axes of the slice: x: 2, y: 2, z: 4, core: 2. Of those that a mesh axis runs over, the one named last changes fastest.
Arguments:
- tokens: bfloat16 [4, 1024, 768], P('dp', 'fsdp'), may hold values from -6 to 6
- ln1_gain: bfloat16 [768], P('fsdp'), may hold values from 0.099609375 to 1.8984375
- ln1_bias: bfloat16 [768], P('fsdp'), may hold values from -1.75 to 1.75
- ln2_gain: bfloat16 [768], P('fsdp'), may hold values from 0.099609375 to 1.8984375
- ln2_bias: bfloat16 [768], P('fsdp'), may hold values from -1.75 to 1.75
- qkv_weight: bfloat16 [768, 2304], P('fsdp'), may hold values from -0.21875 to 0.21875
- qkv_bias: bfloat16 [2304], P('fsdp'), may hold values from -3 to 3
- out_weight: bfloat16 [768, 768], P('fsdp'), may hold values from -1.75 to 1.75
- out_bias: bfloat16 [768], P('fsdp'), may hold values from -3 to 3
- up_weight: bfloat16 [768, 3072], P('fsdp'), may hold values from -0.21875 to 0.21875
- up_bias: bfloat16 [3072], P('fsdp'), may hold values from -3 to 3
- down_weight: bfloat16 [3072, 768], P('fsdp'), may hold values from -0.109375 to 0.109375
- down_bias: bfloat16 [768], P('fsdp'), may hold values from -3 to 3
- cotangent: bfloat16 [4, 1024, 768], P('dp', 'fsdp'), may hold values from -6 to 6
Outputs:
- layer_output: bfloat16 [4, 1024, 768], P('dp', 'fsdp')
- input_grad: float32 [4, 1024, 768], P('dp', 'fsdp')
- grad_ln1_gain: float32 [768], P('fsdp')
- grad_ln1_bias: float32 [768], P('fsdp')
- grad_ln2_gain: float32 [768], P('fsdp')
- grad_ln2_bias: float32 [768], P('fsdp')
- grad_qkv_weight: float32 [768, 2304], P('fsdp')
- grad_qkv_bias: float32 [2304], P('fsdp')
- grad_out_weight: float32 [768, 768], P('fsdp')
- grad_out_bias: float32 [768], P('fsdp')
- grad_up_weight: float32 [768, 3072], P('fsdp')
- grad_up_bias: float32 [3072], P('fsdp')
- grad_down_weight: float32 [3072, 768], P('fsdp')
- grad_down_bias: float32 [768], P('fsdp')
The draws below stay inside these ranges and needn't reach their ends.
All inputs are finite; a program needn't handle non-finite values.
Results may differ from the reference program's by a relative error of at most 0.018.
Values may be sent and summed in bfloat16 or wider, within the bound.
A program may use at most 128 MiB of HBM per device.

```python
import jax
import jax.numpy as jnp
from jax import lax

D = 768
HEADS = 12
HEAD = 64
ROT = 16
FF = 3072
SEQS = 4
LEN = 1024


def shard_levels(own_key, shape, cuts, least, top_value):
    def one(axis_at, blocks):
        heights = jax.random.uniform(jax.random.fold_in(jax.random.fold_in(own_key, 6), axis_at), (blocks,), jnp.float32, least / len(cuts), top_value / len(cuts))
        return jnp.repeat(jnp.exp(heights), shape[axis_at] // blocks).reshape((-1,) + (1,) * (len(shape) - axis_at - 1))

    level = one(*cuts[0])
    for cut in cuts[1:]:
        level = level * one(*cut)
    return level


def centred(key, shape, deviation, bound, shards=(), kind=jnp.bfloat16):
    values = deviation * jax.random.normal(key, shape, jnp.float32)
    if shards:
        values = values * shard_levels(key, shape, shards, -0.22, 0.18)
    return jnp.clip(values, -bound, bound).astype(kind)


def setup_inputs(seed: int = 0) -> dict:
    arg_keys = jax.random.split(jax.random.key(seed), 15)
    return {
        "tokens": centred(arg_keys[0], (SEQS, LEN, D), 1.0, 6.0, ((0, 4), (1, 8))),
        "ln1_gain": jnp.clip(1.0 + 0.18 * jax.random.normal(arg_keys[1], (D,), jnp.float32), 0.099609375, 1.8984375).astype(jnp.bfloat16),
        "ln1_bias": centred(arg_keys[2], (D,), 0.3, 1.75, ((0, 8),)),
        "ln2_gain": jnp.clip(1.0 + 0.18 * jax.random.normal(arg_keys[3], (D,), jnp.float32), 0.099609375, 1.8984375).astype(jnp.bfloat16),
        "ln2_bias": centred(arg_keys[4], (D,), 0.3, 1.75, ((0, 8),)),
        "qkv_weight": centred(arg_keys[5], (D, 3 * D), D ** -0.5, 0.21875, ((0, 8),)),
        "qkv_bias": centred(arg_keys[6], (3 * D,), 0.5, 3.0, ((0, 8),)),
        "out_weight": centred(arg_keys[7], (D, D), (max(1, D // 64)) ** -0.5, 1.75, ((0, 8),)),
        "out_bias": centred(arg_keys[8], (D,), 0.5, 3.0, ((0, 8),)),
        "up_weight": centred(arg_keys[9], (D, FF), D ** -0.5, 0.21875, ((0, 8),)),
        "up_bias": centred(arg_keys[10], (FF,), 0.5, 3.0, ((0, 8),)),
        "down_weight": centred(arg_keys[11], (FF, D), FF ** -0.5, 0.109375, ((0, 8),)),
        "down_bias": centred(arg_keys[12], (D,), 0.5, 3.0, ((0, 8),)),
        "cotangent": centred(arg_keys[13], (SEQS, LEN, D), 1.0, 6.0, ((0, 4), (1, 8))),
    }


@jax.custom_vjp
def low(v):
    return lax.optimization_barrier(v.astype(jnp.bfloat16)).astype(jnp.float32)

@jax.custom_vjp
def low_back(v):
    return v

def low_keep(v):
    return (low(v), None)

def low_pass(kept, grad):
    return (grad,)

def back_keep(v):
    return (v, None)

def back_low(kept, grad):
    return (low(grad),)
low.defvjp(low_keep, low_pass)
low_back.defvjp(back_keep, back_low)
highest = lax.Precision.HIGHEST

def product(left, right):
    return jnp.dot(left, right, precision=highest)

def norm_layer(inputs, gain, shift):
    center = inputs - lax.optimization_barrier(jnp.mean(inputs, axis=-1, keepdims=True))
    spread = lax.optimization_barrier(jnp.mean(center * center, axis=-1, keepdims=True))
    return center * lax.rsqrt(spread + 1e-05) * gain + shift

def rotate(tensor, places):
    half = ROT // 2
    inverse = 10000.0 ** (-(jnp.arange(half, dtype=jnp.float32) * 2.0) / ROT)
    angle = places[:, None] * inverse[None, :]
    cosine = jnp.cos(angle)[:, None, :]
    sine = jnp.sin(angle)[:, None, :]
    first = tensor[..., :half]
    second = tensor[..., half:ROT]
    return jnp.concatenate([first * cosine - second * sine, second * cosine + first * sine, tensor[..., ROT:]], axis=-1)

def layer_fwd(inputs, gain_first, bias_first, gain_second, bias_second, w_qkv, b_qkv, w_out, b_out, w_up, b_up, w_down, b_down):
    length = inputs.shape[0]
    first_norm = low(norm_layer(inputs, gain_first, bias_first))
    second_norm = low(norm_layer(inputs, gain_second, bias_second))
    projected = low_back(product(first_norm, w_qkv) + b_qkv)
    places = jnp.arange(length, dtype=jnp.float32)
    queries = low(rotate(projected[:, :D].reshape(length, HEADS, HEAD), places) * 0.125)
    keys_all = low(rotate(projected[:, D:2 * D].reshape(length, HEADS, HEAD), places))
    values_all = low(projected[:, 2 * D:].reshape(length, HEADS, HEAD))
    query_rows = min(512, length)
    count = length // query_rows

    def attend_rows(pieces):
        query_block, start = pieces
        scores = jnp.einsum('qhd,khd->hqk', query_block, keys_all, precision=highest)
        scores = low_back(scores)
        query_places = start + jnp.arange(query_rows, dtype=jnp.int32)
        key_places = jnp.arange(length, dtype=jnp.int32)
        visible = key_places[None, :] <= query_places[:, None]
        scores = jnp.where(visible[None], scores, -1e+30)
        probs = jax.nn.softmax(scores, axis=-1)
        return jnp.einsum('hqk,khd->qhd', low(probs), values_all, precision=highest)
    starts = jnp.arange(count, dtype=jnp.int32) * query_rows
    attended = lax.map(jax.checkpoint(attend_rows), (queries.reshape(count, query_rows, HEADS, HEAD), starts))
    attended = low(low_back(attended.reshape(length, D)))
    branch_attn = product(attended, w_out) + b_out
    hidden_pre = low_back(product(second_norm, w_up) + b_up)
    hidden = low(jax.nn.gelu(hidden_pre, approximate=False))
    branch_mlp = product(hidden, w_down) + b_down
    return inputs + branch_attn + branch_mlp

def reference(tokens, ln1_gain, ln1_bias, ln2_gain, ln2_bias, qkv_weight, qkv_bias, out_weight, out_bias, up_weight, up_bias, down_weight, down_bias, cotangent):
    params = tuple((member.astype(jnp.float32) for member in (ln1_gain, ln1_bias, ln2_gain, ln2_bias, qkv_weight, qkv_bias, out_weight, out_bias, up_weight, up_bias, down_weight, down_bias)))

    def one_sequence(totals, pieces):
        seq_tokens, seq_grad = pieces
        result, pullback = jax.vjp(layer_fwd, seq_tokens.astype(jnp.float32), *params)
        grads = pullback(seq_grad.astype(jnp.float32))
        totals = tuple((summed + addend for summed, addend in zip(totals, grads[1:])))
        return (totals, (result.astype(jnp.bfloat16), grads[0]))
    initial = tuple((jnp.zeros(member.shape, jnp.float32) for member in params))
    totals, (outputs, input_grads) = lax.scan(one_sequence, initial, (tokens, cotangent))
    return (outputs, input_grads, totals[0], totals[1], totals[2], totals[3], totals[4], totals[5], totals[6], totals[7], totals[8], totals[9], totals[10], totals[11])
```

```python
import functools
import math

import jax
import jax.numpy as jnp
from jax import lax
from jax.experimental import pallas as pl
from jax.experimental.pallas import tpu as pltpu
from jax.sharding import PartitionSpec as P

HEADS = 12
HEAD = 64
ROT = 16

epsilon = 1e-05
inv_root_two = 1.0 / math.sqrt(2.0)
inv_root_twopi = 1.0 / math.sqrt(2.0 * math.pi)
bf16 = jnp.bfloat16
f32 = jnp.float32


def rotary(tensor, cosine, sine, direction):
    half = ROT // 2
    first = tensor[..., :half]
    second = tensor[..., half:ROT]
    return jnp.concatenate(
        [
            first * cosine - direction * second * sine,
            second * cosine + direction * first * sine,
            tensor[..., ROT:],
        ],
        axis=-1,
    )


def dot(a, b, dims):
    return lax.dot_general(a, b, ((dims[0], dims[1]), ((), ())), preferred_element_type=f32)


NN = ((1,), (0,))
NT = ((1,), (1,))
TN = ((0,), (0,))


def gather_rows(arrays):
    return [lax.all_gather(a, "fsdp", axis=0, tiled=True) for a in arrays]


def scatter_rows(a):
    F = lax.axis_size("fsdp")
    got = lax.all_to_all(a, "fsdp", 0, 0, tiled=True)
    return jnp.sum(got.reshape((F, a.shape[0] // F) + a.shape[1:]).astype(f32), axis=0)


def spread_weights(blocks):
    return lax.all_to_all(blocks, "fsdp", 0, 0, tiled=True)


def return_grads(blocks, own):
    n = lax.axis_size("dp")
    F, W, C = blocks.shape
    R, D = own.shape
    parts = jnp.swapaxes(blocks.reshape(F, n, W // n, C), 0, 1).reshape(n, F * (W // n), C)
    own_parts = own.reshape(n, R // n, D)
    if C == D:
        both = jnp.concatenate([parts, own_parts], axis=1)
        both = jnp.sum(lax.all_to_all(both, "dp", 0, 0, tiled=True).astype(f32), axis=0)
        part, own_part = both[: F * (W // n)].astype(bf16), both[F * (W // n) :].astype(bf16)
    else:
        part = jnp.sum(lax.all_to_all(parts, "dp", 0, 0, tiled=True).astype(f32), axis=0)
        own_part = jnp.sum(lax.all_to_all(own_parts, "dp", 0, 0, tiled=True).astype(f32), axis=0)
        part, own_part = part.astype(bf16), own_part.astype(bf16)
    part = lax.all_to_all(part, "fsdp", 0, 0, tiled=True)
    if C == D:
        whole = lax.all_gather(jnp.concatenate([part, own_part], axis=0), "dp", axis=0)
        part_all, own_all = whole[:, : F * (W // n)], whole[:, F * (W // n) :]
    else:
        part_all = lax.all_gather(part, "dp", axis=0)
        own_all = lax.all_gather(own_part, "dp", axis=0)
    part_all = jnp.swapaxes(part_all.reshape(n, F, W // n, C), 0, 1).reshape(F, W, C)
    return part_all, own_all.reshape(R, D)


def body(
    tokens,
    ln1_gain,
    ln1_bias,
    ln2_gain,
    ln2_bias,
    qkv_weight,
    qkv_bias,
    out_weight,
    out_bias,
    up_weight,
    up_bias,
    down_weight,
    down_bias,
    cotangent,
):
    rank = lax.axis_index("fsdp")
    F = lax.axis_size("fsdp")
    rows, D = tokens.shape[1:]
    W = D // F
    FFW = down_weight.shape[0]
    NH = max(-(-((g * W) % HEAD + W) // HEAD) for g in range(F))
    WIN = NH * HEAD
    starts = [min(g * W // HEAD, HEADS - NH) * HEAD for g in range(F)]
    start = jnp.minimum(rank * W // HEAD, HEADS - NH) * HEAD
    off = rank * W - start
    S = rows * F

    qkv3 = qkv_weight.reshape(W, 3, D)
    blocks = jnp.stack(
        [
            jnp.concatenate(
                [
                    qkv3[:, 0, s : s + WIN],
                    qkv3[:, 1, s : s + WIN],
                    qkv3[:, 2, s : s + WIN],
                    up_weight[:, g * FFW : (g + 1) * FFW],
                ],
                axis=1,
            )
            for g, s in enumerate(starts)
        ]
    )
    smalls = jnp.concatenate(
        [ln1_gain, ln1_bias, ln2_gain, ln2_bias, out_bias, down_bias, qkv_bias]
    )
    extra = -(-smalls.shape[0] // (16 * D)) * 16
    smalls = jnp.concatenate([smalls, jnp.zeros(extra * D - smalls.shape[0], bf16)])
    (both_all,) = gather_rows([jnp.concatenate([tokens[0], smalls.reshape(extra, D)], axis=0)])
    both_all = both_all.reshape(F, rows + extra, D)
    x_low = both_all[:, :rows].reshape(S, D)
    small_all = both_all[:, rows:].reshape(F, extra * D)
    wall = spread_weights(blocks).reshape(D, 3 * WIN + FFW)
    w_qkv = wall[:, : 3 * WIN]
    w_up = wall[:, 3 * WIN :]
    up_ring = [(i, (i + 1) % F) for i in range(F)]
    down_ring = [(i, (i - 1) % F) for i in range(F)]
    out_prev = lax.ppermute(out_weight, "fsdp", up_ring)
    out_next = lax.ppermute(out_weight, "fsdp", down_ring)
    (grad_out,) = gather_rows([cotangent[0]])
    out_three = jnp.concatenate(
        [out_prev, out_weight, out_next, jnp.zeros((WIN, D), bf16)], axis=0
    )
    w_out_win = lax.dynamic_slice_in_dim(out_three, W - off, WIN, 0)
    win_col = jnp.arange(WIN, dtype=jnp.int32)
    mine = (win_col >= off) & (win_col < off + W)
    small_all = small_all.astype(f32)
    gain_one, bias_one, gain_two, bias_two, b_out, b_down = [
        small_all[:, i * W : (i + 1) * W].reshape(D) for i in range(6)
    ]
    b_qkv = small_all[:, 6 * W : 9 * W].reshape(3, D)
    b_qkv = lax.dynamic_slice_in_dim(b_qkv, start, WIN, 1).reshape(3 * WIN)
    b_up = up_bias.astype(f32)

    x = x_low.astype(f32)
    center = x - jnp.mean(x, axis=-1, keepdims=True)
    inverse = lax.rsqrt(jnp.mean(center * center, axis=-1, keepdims=True) + epsilon)
    normed = center * inverse
    first_low = (normed * gain_one + bias_one).astype(bf16)
    second_low = (normed * gain_two + bias_two).astype(bf16)

    places = jnp.arange(S, dtype=f32)
    half = ROT // 2
    freq = 10000.0 ** (-(jnp.arange(half, dtype=f32) * 2.0) / ROT)
    angle = places[:, None] * freq[None, :]
    cosine = jnp.cos(angle)[:, None, :]
    sine = jnp.sin(angle)[:, None, :]

    proj = dot(first_low, w_qkv, NN) + b_qkv
    queries = (rotary(proj[:, :WIN].reshape(S, NH, HEAD), cosine, sine, 1.0) * 0.125).astype(bf16)
    keys = rotary(proj[:, WIN : 2 * WIN].reshape(S, NH, HEAD), cosine, sine, 1.0).astype(bf16)
    vals = proj[:, 2 * WIN :].astype(bf16).reshape(S, NH, HEAD)
    q_place = jnp.arange(S, dtype=jnp.int32)
    visible = (q_place[None, :] <= q_place[:, None])[None]
    scores = jnp.einsum("qhd,khd->hqk", queries, keys, preferred_element_type=f32)
    masked = jnp.where(visible, scores, -1e30)
    top = jnp.max(masked, axis=-1, keepdims=True)
    lse = top + jnp.log(jnp.sum(jnp.exp(masked - top), axis=-1, keepdims=True))
    probs = jnp.exp(masked - lse)
    probs_low = probs.astype(bf16)
    attended = jnp.einsum("hqk,khd->qhd", probs_low, vals, preferred_element_type=f32)
    att_low = jnp.where(mine, attended.reshape(S, WIN), 0.0).astype(bf16)

    hidden_pre = dot(second_low, w_up, NN) + b_up
    cdf = 0.5 * (1.0 + lax.erf(hidden_pre * inv_root_two))
    hidden_low = (hidden_pre * cdf).astype(bf16)
    part = dot(att_low, w_out_win, NN) + dot(hidden_low, down_weight, NN)
    branch = scatter_rows(part.astype(bf16))

    grad_hidden = dot(grad_out, down_weight, NT)
    slope = cdf + hidden_pre * jnp.exp(-0.5 * hidden_pre * hidden_pre) * inv_root_twopi
    grad_pre = (grad_hidden * slope).astype(bf16)
    grad_w_down = dot(hidden_low, grad_out, TN)
    grad_w_out_win = dot(att_low, grad_out, TN)
    grad_w_out = lax.dynamic_slice_in_dim(grad_w_out_win, off, W, 0)
    bias_total = jnp.sum(grad_out.astype(f32), axis=0)
    grad_b_up = jnp.sum(grad_pre.astype(f32), axis=0)
    grad_att = dot(grad_out, w_out_win, NT).astype(bf16).reshape(S, NH, HEAD)
    delta = jnp.transpose(jnp.sum(grad_att.astype(f32) * attended, axis=-1))[:, :, None]
    grad_probs = jnp.einsum("qhd,khd->hqk", grad_att, vals, preferred_element_type=f32)
    grad_scores = (probs * (grad_probs - delta)).astype(bf16)
    grad_q = jnp.einsum("hqk,khd->qhd", grad_scores, keys, preferred_element_type=f32)
    grad_k = jnp.einsum("hqk,qhd->khd", grad_scores, queries, preferred_element_type=f32)
    grad_v = jnp.einsum("hqk,qhd->khd", probs_low, grad_att, preferred_element_type=f32)
    grad_proj = jnp.stack(
        [
            rotary(grad_q * 0.125, cosine, sine, -1.0).reshape(S, WIN),
            rotary(grad_k, cosine, sine, -1.0).reshape(S, WIN),
            grad_v.reshape(S, WIN),
        ],
        axis=1,
    )
    grad_proj = jnp.where(mine, grad_proj, 0.0).astype(bf16).reshape(S, 3 * WIN)
    grad_w_qkv = dot(first_low, grad_proj, TN)
    grad_w_up = dot(second_low, grad_pre, TN)
    grad_b_qkv = jnp.sum(grad_proj.astype(f32), axis=0).reshape(3, WIN)
    grad_first = dot(grad_proj, w_qkv, NT)
    grad_second = dot(grad_pre, w_up, NT)
    vectors = [
        jnp.sum(grad_first * normed, axis=0),
        jnp.sum(grad_first, axis=0),
        jnp.sum(grad_second * normed, axis=0),
        jnp.sum(grad_second, axis=0),
    ]
    mixed = grad_first * gain_one + grad_second * gain_two
    b_full = lax.dynamic_update_slice_in_dim(jnp.zeros((3, D), f32), grad_b_qkv, start, 1)
    small_part = jnp.concatenate(
        [v.reshape(F, W) for v in vectors] + [b_full.reshape(F, 3 * W)], axis=1
    )
    mixed_mine = scatter_rows(mixed.astype(bf16))
    small_mine = scatter_rows(small_part)[0]
    own_small = jnp.concatenate(
        [small_mine, lax.dynamic_slice_in_dim(bias_total, rank * W, W, 0), grad_b_up]
    )
    pad = 8 * lax.axis_size("dp")
    own_rows = -(-(W + FFW + -(-own_small.shape[0] // D)) // pad) * pad
    n_small = own_rows - W - FFW
    own_small = jnp.concatenate([own_small, jnp.zeros(n_small * D - own_small.shape[0], f32)])

    grad_blocks = jnp.concatenate([grad_w_qkv, grad_w_up], axis=1).astype(bf16)
    grad_blocks = grad_blocks.reshape(F, W, 3 * WIN + FFW)
    own = jnp.concatenate(
        [grad_w_out, grad_w_down, own_small.reshape(n_small, D)], axis=0
    ).astype(bf16)
    returned, own = return_grads(grad_blocks, own)
    returned = returned.astype(f32)
    own = own.astype(f32)
    own_small = own[W + FFW :].reshape(n_small * D)
    pieces = [
        [returned[g, :, i * WIN + g * W - s : i * WIN + g * W - s + W] for g, s in enumerate(starts)]
        for i in range(3)
    ]
    out_w_qkv = jnp.concatenate(pieces[0] + pieces[1] + pieces[2], axis=1)
    out_w_up = jnp.concatenate([returned[g, :, 3 * WIN :] for g in range(F)], axis=1)

    here = rank * rows
    x_own = tokens[0].astype(f32)
    c_own = x_own - jnp.mean(x_own, axis=-1, keepdims=True)
    i_own = lax.rsqrt(jnp.mean(c_own * c_own, axis=-1, keepdims=True) + epsilon)
    n_own = c_own * i_own
    layer_output = (x_own + branch + b_out + b_down).astype(bf16)
    input_grad = cotangent[0].astype(f32) + i_own * (
        mixed_mine
        - jnp.mean(mixed_mine, axis=-1, keepdims=True)
        - n_own * jnp.mean(mixed_mine * n_own, axis=-1, keepdims=True)
    )
    g = [own_small[i * W : (i + 1) * W] for i in range(4)]
    bias_mine = own_small[7 * W : 8 * W]
    return (
        layer_output[None],
        input_grad[None],
        g[0],
        g[1],
        g[2],
        g[3],
        out_w_qkv,
        own_small[4 * W : 7 * W],
        own[:W],
        bias_mine,
        out_w_up,
        own_small[8 * W : 8 * W + FFW],
        own[W : W + FFW],
        bias_mine,
    )


class Copies:
    def __init__(self):
        self.later = []

    def send(self, src, dst, send_sem, recv_sem, when=None, **to):
        copy = pltpu.make_async_remote_copy(
            src_ref=src,
            dst_ref=dst,
            send_sem=send_sem,
            recv_sem=recv_sem,
            device_id=to,
            device_id_type=pl.DeviceIdType.MESH,
        )
        if when is None:
            copy.start()
        else:
            pl.when(when)(copy.start)
        self.later.append((copy, when))

    def drain(self):
        for copy, when in self.later:
            if when is None:
                copy.wait_send()
            else:
                pl.when(when)(copy.wait_send)
        self.later = []


def arrived(dst, recv_sem, **to):
    pltpu.make_async_remote_copy(
        src_ref=dst,
        dst_ref=dst,
        send_sem=recv_sem,
        recv_sem=recv_sem,
        device_id=to,
        device_id_type=pl.DeviceIdType.MESH,
    ).wait_recv()


def meet(peers):
    barrier = pltpu.get_barrier_semaphore()
    for to in peers:
        pl.semaphore_signal(barrier, inc=1, device_id=to, device_id_type=pl.DeviceIdType.MESH)
    pl.semaphore_wait(barrier, len(peers))


class Spread:
    def __init__(self, copies, buf, send_sem, recv_sem, Z, z, y):
        self.copies, self.buf, self.ss, self.rs = copies, buf, send_sem, recv_sem
        self.Z, self.z, self.y = Z, z, y

    def push(self, src, way, when=None):
        to = {0: src * 0 + (self.z * 2 + self.y + 2), 1: self.z * 2 + self.y - 2, 2: self.z * 2 + 1 - self.y}[way]
        self.copies.send(
            self.buf.at[src], self.buf.at[src], self.ss.at[way, src], self.rs.at[src], when, fsdp=to
        )

    def first(self):
        me = self.z * 2 + self.y
        self.push(me, 0, self.z + 1 < self.Z)
        self.push(me, 1, self.z > 0)
        self.push(me, 2)

    def got(self, src, when=None):
        def wait():
            arrived(self.buf.at[src], self.rs.at[src], fsdp=self.z * 2 + 1 - self.y)

        if when is None:
            wait()
        else:
            pl.when(when)(wait)

    def step(self, k):
        z, y = self.z, self.y
        low, high = jnp.maximum(z - k, 0) * 2 + y, jnp.minimum(z + k, self.Z - 1) * 2 + y
        has_low, has_high = z - k >= 0, z + k < self.Z
        self.got(low, has_low)
        self.push(low, 0, has_low & (z + 1 < self.Z))
        self.push(low, 2, has_low)
        self.got(high, has_high)
        self.push(high, 1, has_high & (z > 0))
        self.push(high, 2, has_high)

    def finish(self):
        for k in range(self.Z):
            self.got(k * 2 + 1 - self.y)


def gather_kernel(
    F, tok, cot, small, qkv, up, outw, xall, gall, sall, wall, outwin, wblk, sx, rx, sg, rg, s_small, r_small,
    s_w, r_w, s_o, r_o,
):
    me, d = lax.axis_index("fsdp"), lax.axis_index("dp")
    Z, z, y, x, c = F // 2, me // 2, me % 2, d // 2, d % 2
    W, D = outw.shape
    C = wall.shape[3]
    half = W // 2
    others = [lax.rem(me + k, F) for k in range(1, F)]
    xn, cn = d + 2 - 4 * x, d + 1 - 2 * c
    meet([{"fsdp": o} for o in others] + [{"dp": xn}, {"dp": cn}])
    copies = Copies()

    xall[me] = tok[...]
    tokens = Spread(copies, xall, sx, rx, Z, z, y)
    tokens.first()

    row = lax.broadcasted_iota(jnp.int32, (256, 128), 0)
    col = lax.broadcasted_iota(jnp.int32, (256, 128), 1)
    shift = (row == col + HEAD).astype(bf16)
    for g in range(F):
        s = g * W // HEAD * HEAD
        for i in range(3):
            at = i * D + s
            if s % 128 == 0:
                piece = qkv[:, at : at + 128]
            else:
                piece = dot(qkv[:, at - 64 : at + 192], shift, NN).astype(bf16)
            wblk[0, g, :, i * 128 : (i + 1) * 128] = piece
        wblk[1, g] = up[:, g * C : (g + 1) * C]
    mine = pl.ds(pl.multiple_of(c * half, half), half)
    for k, o in enumerate(others):
        copies.send(wblk.at[x, o, mine], wall.at[x, me, mine], s_w.at[0, k], r_w.at[0, me], fsdp=o)
    wall[:, me] = wblk[:, me]
    outwin[pl.ds(pl.multiple_of(32 * y, 32), W), :] = outw[...]
    copies.send(
        outw.at[pl.ds(pl.multiple_of((W - 32) * (1 - y), 32), 32)],
        outwin.at[pl.ds(pl.multiple_of(W * y, 32), 32)],
        s_o, r_o, fsdp=z * 2 + 1 - y,
    )
    sall[me] = small[...]
    for k, o in enumerate(others):
        copies.send(small, sall.at[me], s_small.at[k], r_small.at[me], fsdp=o)
    gall[me] = cot[...]
    grads = Spread(copies, gall, sg, rg, Z, z, y)

    tokens.step(1)
    for k, o in enumerate(others):
        src = lax.rem(me + F - k - 1, F)
        piece = wall.at[x, src, mine]
        arrived(piece, r_w.at[0, src], fsdp=o)
        copies.send(piece, piece, s_w.at[1, k], r_w.at[1, src], dp=xn)
        copies.send(piece, piece, s_w.at[2, k], r_w.at[2, src], dp=cn)
    for k in range(2, Z):
        tokens.step(k)
    grads.first()
    for k, o in enumerate(others):
        src = lax.rem(me + F - k - 1, F)
        piece = wall.at[1 - x, src, mine]
        arrived(piece, r_w.at[1, src], dp=xn)
        copies.send(piece, piece, s_w.at[3, k], r_w.at[3, src], dp=cn)
    for k in range(1, Z):
        grads.step(k)
    theirs = pl.ds(pl.multiple_of((1 - c) * half, half), half)
    for k, o in enumerate(others):
        src = lax.rem(me + F - k - 1, F)
        arrived(wall.at[x, src, theirs], r_w.at[2, src], dp=cn)
        arrived(wall.at[1 - x, src, theirs], r_w.at[3, src], dp=cn)
        arrived(sall.at[src], r_small.at[src], fsdp=o)
    arrived(outwin.at[pl.ds(pl.multiple_of(W * (1 - y), 32), 32)], r_o, fsdp=z * 2 + 1 - y)
    tokens.finish()
    grads.finish()
    copies.drain()


def vmem():
    return pl.BlockSpec(memory_space=pltpu.VMEM)


def gather_all(F, tok, cot, small, qkv, up, outw):
    rows, D = tok.shape
    W, FF = up.shape
    C = FF // F
    dma = pltpu.SemaphoreType.DMA
    return pl.pallas_call(
        functools.partial(gather_kernel, F),
        out_shape=(
            jax.ShapeDtypeStruct((F, rows, D), bf16),
            jax.ShapeDtypeStruct((F, rows, D), bf16),
            jax.ShapeDtypeStruct((F,) + small.shape, bf16),
            jax.ShapeDtypeStruct((2, F, W, C), bf16),
            jax.ShapeDtypeStruct((128, D), bf16),
        ),
        in_specs=[vmem()] * 6,
        out_specs=(vmem(),) * 5,
        scratch_shapes=[
            pltpu.VMEM((2, F, W, C), bf16),
            dma((3, F)), dma((F,)), dma((3, F)), dma((F,)), dma((F,)), dma((F,)),
            dma((4, F)), dma((4, F)), dma, dma,
        ],
        compiler_params=pltpu.CompilerParams(
            collective_id=0, has_side_effects=True, vmem_limit_bytes=56 * 2**20
        ),
        name="gather_all",
    )(tok, cot, small, qkv, up, outw)


def add_rows(out, parts):
    step = 16
    for r in range(0, out.shape[0], step):
        total = parts[0][r : r + step].astype(f32)
        for p in parts[1:]:
            total = total + p[r : r + step].astype(f32)
        out[r : r + step] = total.astype(out.dtype)


class Collect:
    def __init__(self, copies, part, yb, ub, db, sb, sems, out, Z, z, y):
        self.__dict__.update(copies=copies, part=part, yb=yb, ub=ub, db=db, sb=sb, out=out, Z=Z, z=z, y=y)
        self.sy, self.ry, self.sz, self.ru, self.rd = [sems.at[i] for i in range(5)]
        self.order = [jnp.where(z < Z // 2, Z - 1 - j, j) for j in range(Z)]

    def first(self):
        for t in self.order:
            self.copies.send(
                self.part.at[t * 2 + 1 - self.y], self.yb.at[t], self.sy.at[t], self.ry.at[t],
                fsdp=self.z * 2 + 1 - self.y,
            )

    def chain(self, t, buf, recv, more, to, active):
        z, y = self.z, self.y

        @pl.when(active & more)
        def _():
            arrived(buf.at[t], recv.at[t], fsdp=z * 2 + 1 - y)
            add_rows(self.sb.at[t], [self.part.at[t * 2 + y], self.yb.at[t], buf.at[t]])

        @pl.when(active & jnp.logical_not(more))
        def _():
            add_rows(self.sb.at[t], [self.part.at[t * 2 + y], self.yb.at[t]])

        self.copies.send(self.sb.at[t], buf.at[t], self.sz.at[t], recv.at[t], active, fsdp=to)

    def step(self, j):
        z, y, Z = self.z, self.y, self.Z
        t = self.order[j]

        @pl.when(t != z)
        def _():
            arrived(self.yb.at[t], self.ry.at[t], fsdp=z * 2 + 1 - y)

        self.chain(t, self.ub, self.ru, z > 0, jnp.minimum(z + 1, Z - 1) * 2 + y, t > z)
        self.chain(t, self.db, self.rd, z < Z - 1, jnp.maximum(z - 1, 0) * 2 + y, t < z)

    def finish(self):
        z, y, Z = self.z, self.y, self.Z
        to = z * 2 + 1 - y
        arrived(self.yb.at[z], self.ry.at[z], fsdp=to)
        base = [self.part.at[z * 2 + y], self.yb.at[z]]

        @pl.when(z > 0)
        def _():
            arrived(self.ub.at[z], self.ru.at[z], fsdp=to)

        @pl.when(z < Z - 1)
        def _():
            arrived(self.db.at[z], self.rd.at[z], fsdp=to)

        @pl.when(z == 0)
        def _():
            add_rows(self.out, base + [self.db.at[z]])

        @pl.when(z == Z - 1)
        def _():
            add_rows(self.out, base + [self.ub.at[z]])

        @pl.when((z > 0) & (z < Z - 1))
        def _():
            add_rows(self.out, base + [self.ub.at[z], self.db.at[z]])


def collect_kernel(
    F, half, part, mixed, grad, vecs, own_vec, branch, mixed_own, ret, vec_sum,
    yb, ub, db, sb, cbuf, hbuf, xbuf, qbuf, vbuf, vtot, wbuf, sems, s_c, r_c, s_x, r_x, s_w, r_w, s_own, r_own,
    s_v, r_v, s_d, r_d,
):
    me, d = lax.axis_index("fsdp"), lax.axis_index("dp")
    Z, z, y, x, c = F // 2, me // 2, me % 2, d // 2, d % 2
    others = [lax.rem(me + k, F) for k in range(1, F)]
    xn, cn, dn = d + 2 - 4 * x, d + 1 - 2 * c, (1 - x) * 2 + 1 - c
    meet([{"fsdp": o} for o in others] + [{"dp": xn}, {"dp": cn}, {"dp": dn}])
    copies = Copies()
    for i in range(2):
        copies.send(grad.at[i, 1 - c], cbuf.at[i], s_c.at[i], r_c.at[i], dp=cn)
    vbuf[me] = vecs[me]
    for k, o in enumerate(others):
        copies.send(vecs.at[o], vbuf.at[me], s_v.at[k], r_v.at[me], fsdp=o)
    first = Collect(copies, part, yb.at[0], ub.at[0], db.at[0], sb.at[0], sems.at[0], branch, Z, z, y)
    second = Collect(copies, mixed, yb.at[1], ub.at[1], db.at[1], sb.at[1], sems.at[1], mixed_own, Z, z, y)
    first.first()
    second.first()
    GR = F * half
    own_rows = pl.ds(GR, grad.shape[2] - GR)

    arrived(cbuf.at[1 - x], r_c.at[1 - x], dp=cn)
    add_rows(hbuf, [grad.at[1 - x, c], cbuf.at[1 - x]])
    copies.send(hbuf, xbuf, s_x, r_x, dp=xn)
    arrived(cbuf.at[x], r_c.at[x], dp=cn)
    for j in range(Z):
        first.step(j)
    arrived(xbuf, r_x, dp=xn)
    add_rows(qbuf, [grad.at[x, c], cbuf.at[x], xbuf])
    for k, o in enumerate(others):
        piece = pl.ds(pl.multiple_of(o * half, half), half)
        copies.send(qbuf.at[piece], wbuf.at[me], s_w.at[0, k], r_w.at[0, me], fsdp=o)
    ret[x, c, own_rows] = qbuf[own_rows]
    owner = ret.at[x, c, own_rows]
    copies.send(owner, owner, s_own.at[0], r_own.at[0], dp=xn)
    copies.send(owner, owner, s_own.at[1], r_own.at[1], dp=cn)
    total = vbuf[me]
    for k, o in enumerate(others):
        src = lax.rem(me + F - k - 1, F)
        arrived(vbuf.at[src], r_v.at[src], fsdp=o)
    total = vbuf[0]
    for g in range(1, F):
        total = total + vbuf[g]
    vtot[d, :8] = total
    vtot[d, 8:] = own_vec[...]
    for k, to in enumerate((xn, cn, dn)):
        copies.send(vtot.at[d], vtot.at[d], s_d.at[k], r_d.at[d], dp=to)
    first.finish()
    mine = pl.ds(pl.multiple_of(me * half, half), half)
    ret[x, c, mine] = qbuf[mine]
    piece = ret.at[x, c, mine]
    copies.send(piece, piece, s_w.at[1, 7], r_w.at[1, me], dp=xn)
    copies.send(piece, piece, s_w.at[2, 7], r_w.at[2, me], dp=cn)

    def pass_on(k):
        src = lax.rem(me + F - k - 1, F)
        rows = pl.ds(pl.multiple_of(src * half, half), half)
        arrived(wbuf.at[src], r_w.at[0, src], fsdp=others[k])
        ret[x, c, rows] = wbuf[src]
        piece = ret.at[x, c, rows]
        copies.send(piece, piece, s_w.at[1, k], r_w.at[1, src], dp=xn)
        copies.send(piece, piece, s_w.at[2, k], r_w.at[2, src], dp=cn)

    for k in range(F - 1):
        pass_on(k)
    for j in range(Z):
        second.step(j)
    arrived(ret.at[1 - x, c, own_rows], r_own.at[0], dp=xn)
    copies.send(ret.at[1 - x, c, own_rows], ret.at[1 - x, c, own_rows], s_own.at[2], r_own.at[2], dp=cn)
    for g in range(F):
        rows = pl.ds(g * half, half)
        piece = ret.at[1 - x, c, rows]
        arrived(piece, r_w.at[1, g], dp=xn)
        copies.send(piece, piece, s_w.at[3, g], r_w.at[3, g], dp=cn)
    second.finish()
    for k, to in enumerate((xn, cn, dn)):
        arrived(vtot.at[to], r_d.at[to], dp=to)
    vec_sum[...] = vtot[0] + vtot[1] + vtot[2] + vtot[3]
    arrived(ret.at[x, 1 - c, own_rows], r_own.at[1], dp=cn)
    arrived(ret.at[1 - x, 1 - c, own_rows], r_own.at[2], dp=cn)
    for g in range(F):
        rows = pl.ds(g * half, half)
        arrived(ret.at[x, 1 - c, rows], r_w.at[2, g], dp=cn)
        arrived(ret.at[1 - x, 1 - c, rows], r_w.at[3, g], dp=cn)
    copies.drain()


def collect_all(F, half, part, mixed, grad, vecs, own_vec):
    _, rows, D = part.shape
    GR, C = grad.shape[2:]
    Z = F // 2
    dma = pltpu.SemaphoreType.DMA
    block = pltpu.VMEM((2, Z, rows, D), bf16)
    return pl.pallas_call(
        functools.partial(collect_kernel, F, half),
        out_shape=(
            jax.ShapeDtypeStruct((rows, D), f32),
            jax.ShapeDtypeStruct((rows, D), f32),
            jax.ShapeDtypeStruct(grad.shape, bf16),
            jax.ShapeDtypeStruct((16, 128), f32),
        ),
        in_specs=[vmem()] * 5,
        out_specs=(vmem(),) * 4,
        scratch_shapes=[
            block, block, block, block,
            pltpu.VMEM((2, GR, C), bf16),
            pltpu.VMEM((GR, C), bf16),
            pltpu.VMEM((GR, C), bf16),
            pltpu.VMEM((GR, C), bf16),
            pltpu.VMEM((F, 8, 128), f32),
            pltpu.VMEM((4, 16, 128), f32),
            pltpu.VMEM((F, half, C), bf16),
            dma((2, 5, Z)),
            dma((2,)), dma((2,)), dma, dma, dma((4, F)), dma((4, F)), dma((3,)), dma((3,)),
            dma((F,)), dma((F,)), dma((3,)), dma((4,)),
        ],
        compiler_params=pltpu.CompilerParams(
            collective_id=1, has_side_effects=True, vmem_limit_bytes=56 * 2**20
        ),
        name="collect_all",
    )(part, mixed, grad, vecs, own_vec)


def fast_body(
    tokens,
    ln1_gain,
    ln1_bias,
    ln2_gain,
    ln2_bias,
    qkv_weight,
    qkv_bias,
    out_weight,
    out_bias,
    up_weight,
    up_bias,
    down_weight,
    down_bias,
    cotangent,
):
    rank = lax.axis_index("fsdp")
    F = lax.axis_size("fsdp")
    rows, D = tokens.shape[1:]
    W = D // F
    FFW = down_weight.shape[0]
    NH = max(-(-((g * W) % HEAD + W) // HEAD) for g in range(F))
    WIN = NH * HEAD
    starts = [min(g * W // HEAD, HEADS - NH) * HEAD for g in range(F)]
    start = jnp.minimum(rank * W // HEAD, HEADS - NH) * HEAD
    off = rank * W - start
    S = rows * F

    c = W // 2
    small = jnp.stack([ln1_gain, ln1_bias, ln2_gain, ln2_bias, out_bias, down_bias])
    small = jnp.concatenate([small, qkv_bias.reshape(3, W)], axis=0)
    small = jnp.pad(small, ((0, 7), (0, 128 - W)))
    x_low, grad_out, small_all, wall, w_out_win = gather_all(
        F, tokens[0], cotangent[0], small, qkv_weight, up_weight, out_weight
    )
    x_low = x_low.reshape(S, D)
    grad_out = grad_out.reshape(S, D)
    w_qkv = wall[0].reshape(D, 3 * WIN)
    w_up = wall[1].reshape(D, FFW)
    win_col = jnp.arange(WIN, dtype=jnp.int32)
    mine = (win_col >= off) & (win_col < off + W)
    small_all = small_all[:, :9, :W].astype(f32)
    gain_one, bias_one, gain_two, bias_two, b_out, b_down = [
        small_all[:, i].reshape(D) for i in range(6)
    ]
    b_qkv = small_all[:, 6:].reshape(3, D)
    b_qkv = lax.dynamic_slice_in_dim(b_qkv, start, WIN, 1).reshape(3 * WIN)
    b_up = up_bias.astype(f32)

    x = x_low.astype(f32)
    center = x - jnp.mean(x, axis=-1, keepdims=True)
    inverse = lax.rsqrt(jnp.mean(center * center, axis=-1, keepdims=True) + epsilon)
    normed = center * inverse
    first_low = (normed * gain_one + bias_one).astype(bf16)
    second_low = (normed * gain_two + bias_two).astype(bf16)

    places = jnp.arange(S, dtype=f32)
    half = ROT // 2
    freq = 10000.0 ** (-(jnp.arange(half, dtype=f32) * 2.0) / ROT)
    angle = places[:, None] * freq[None, :]
    cosine = jnp.cos(angle)[:, None, :]
    sine = jnp.sin(angle)[:, None, :]

    proj = dot(first_low, w_qkv, NN) + b_qkv
    queries = (rotary(proj[:, :WIN].reshape(S, NH, HEAD), cosine, sine, 1.0) * 0.125).astype(bf16)
    keys = rotary(proj[:, WIN : 2 * WIN].reshape(S, NH, HEAD), cosine, sine, 1.0).astype(bf16)
    vals = proj[:, 2 * WIN :].astype(bf16).reshape(S, NH, HEAD)
    q_place = jnp.arange(S, dtype=jnp.int32)
    visible = (q_place[None, :] <= q_place[:, None])[None]
    scores = jnp.einsum("qhd,khd->hqk", queries, keys, preferred_element_type=f32)
    masked = jnp.where(visible, scores, -1e30)
    top = jnp.max(masked, axis=-1, keepdims=True)
    lse = top + jnp.log(jnp.sum(jnp.exp(masked - top), axis=-1, keepdims=True))
    probs = jnp.exp(masked - lse)
    probs_low = probs.astype(bf16)
    attended = jnp.einsum("hqk,khd->qhd", probs_low, vals, preferred_element_type=f32)
    att_low = jnp.where(mine, attended.reshape(S, WIN), 0.0).astype(bf16)

    hidden_pre = dot(second_low, w_up, NN) + b_up
    cdf = 0.5 * (1.0 + lax.erf(hidden_pre * inv_root_two))
    hidden_low = (hidden_pre * cdf).astype(bf16)
    part = dot(att_low, w_out_win, NN) + dot(hidden_low, down_weight, NN)

    grad_hidden = dot(grad_out, down_weight, NT)
    slope = cdf + hidden_pre * jnp.exp(-0.5 * hidden_pre * hidden_pre) * inv_root_twopi
    grad_pre = (grad_hidden * slope).astype(bf16)
    grad_w_down = dot(hidden_low, grad_out, TN)
    grad_w_out_win = dot(att_low, grad_out, TN)
    grad_w_out = lax.dynamic_slice_in_dim(grad_w_out_win, off, W, 0)
    bias_total = jnp.sum(grad_out.astype(f32), axis=0)
    grad_b_up = jnp.sum(grad_pre.astype(f32), axis=0)
    grad_att = dot(grad_out, w_out_win, NT).astype(bf16).reshape(S, NH, HEAD)
    delta = jnp.transpose(jnp.sum(grad_att.astype(f32) * attended, axis=-1))[:, :, None]
    grad_probs = jnp.einsum("qhd,khd->hqk", grad_att, vals, preferred_element_type=f32)
    grad_scores = (probs * (grad_probs - delta)).astype(bf16)
    grad_q = jnp.einsum("hqk,khd->qhd", grad_scores, keys, preferred_element_type=f32)
    grad_k = jnp.einsum("hqk,qhd->khd", grad_scores, queries, preferred_element_type=f32)
    grad_v = jnp.einsum("hqk,qhd->khd", probs_low, grad_att, preferred_element_type=f32)
    grad_proj = jnp.stack(
        [
            rotary(grad_q * 0.125, cosine, sine, -1.0).reshape(S, WIN),
            rotary(grad_k, cosine, sine, -1.0).reshape(S, WIN),
            grad_v.reshape(S, WIN),
        ],
        axis=1,
    )
    grad_proj = jnp.where(mine, grad_proj, 0.0).astype(bf16).reshape(S, 3 * WIN)
    grad_w_qkv = dot(first_low, grad_proj, TN)
    grad_w_up = dot(second_low, grad_pre, TN)
    grad_b_qkv = jnp.sum(grad_proj.astype(f32), axis=0).reshape(3, WIN)
    grad_first = dot(grad_proj, w_qkv, NT)
    grad_second = dot(grad_pre, w_up, NT)
    vectors = [
        jnp.sum(grad_first * normed, axis=0),
        jnp.sum(grad_first, axis=0),
        jnp.sum(grad_second * normed, axis=0),
        jnp.sum(grad_second, axis=0),
    ]
    mixed = grad_first * gain_one + grad_second * gain_two
    b_full = lax.dynamic_update_slice_in_dim(jnp.zeros((3, D), f32), grad_b_qkv, start, 1)
    vecs = jnp.concatenate(
        [jnp.stack([v.reshape(F, W) for v in vectors], axis=1), b_full.reshape(F, 3, W)], axis=1
    )
    vecs = jnp.pad(vecs, ((0, 0), (0, 1), (0, 128 - W)))
    own_vec = jnp.concatenate(
        [
            jnp.pad(lax.dynamic_slice_in_dim(bias_total, rank * W, W, 0), (0, 128 - W))[None],
            grad_b_up.reshape(FFW // 128, 128),
        ]
    )
    own_vec = jnp.pad(own_vec, ((0, 8 - own_vec.shape[0]), (0, 0)))
    C = FFW
    half = W // 2
    grad_own = jnp.concatenate([grad_w_out, grad_w_down], axis=0).astype(bf16)
    own_rows = grad_own.shape[0] // 2
    grad_own = grad_own.reshape(2, own_rows, 2, C).transpose(2, 0, 1, 3)
    grad_blocks = jnp.stack([grad_w_qkv, grad_w_up]).astype(bf16)
    grad_blocks = grad_blocks.reshape(2, F, 2, half, C).transpose(0, 2, 1, 3, 4)
    grad = jnp.concatenate([grad_blocks.reshape(2, 2, F * half, C), grad_own], axis=2)
    branch, mixed_mine, returned, vec_sum = collect_all(
        F,
        half,
        part.astype(bf16).reshape(F, rows, D),
        mixed.astype(bf16).reshape(F, rows, D),
        grad,
        vecs,
        own_vec,
    )
    own = returned[:, :, F * half :].transpose(1, 2, 0, 3).reshape(W + FFW, D).astype(f32)
    returned = returned[:, :, : F * half].reshape(2, 2, F, half, C).transpose(0, 2, 1, 3, 4)
    returned = returned.reshape(2, F, W, C)
    src_col = jnp.arange(F * WIN, dtype=jnp.int32)[:, None]
    dst_col = jnp.arange(D, dtype=jnp.int32)[None, :]
    src_win = src_col // WIN
    place = (src_win * W // HEAD * HEAD + src_col % WIN == dst_col) & (dst_col // W == src_win)
    qkv_all = returned[0].reshape(F, W, 3, WIN).transpose(2, 1, 0, 3).reshape(3 * W, F * WIN)
    out_w_qkv = dot(qkv_all, place.astype(bf16), NN).reshape(3, W, D)
    out_w_qkv = jnp.concatenate([out_w_qkv[0], out_w_qkv[1], out_w_qkv[2]], axis=1)
    out_w_up = returned[1].transpose(1, 0, 2).reshape(W, F * FFW).astype(f32)

    here = rank * rows
    x_own = tokens[0].astype(f32)
    c_own = x_own - jnp.mean(x_own, axis=-1, keepdims=True)
    i_own = lax.rsqrt(jnp.mean(c_own * c_own, axis=-1, keepdims=True) + epsilon)
    n_own = c_own * i_own
    layer_output = (x_own + branch + b_out + b_down).astype(bf16)
    input_grad = cotangent[0].astype(f32) + i_own * (
        mixed_mine
        - jnp.mean(mixed_mine, axis=-1, keepdims=True)
        - n_own * jnp.mean(mixed_mine * n_own, axis=-1, keepdims=True)
    )
    g = [vec_sum[i, :W] for i in range(4)]
    bias_mine = vec_sum[8, :W]
    return (
        layer_output[None],
        input_grad[None],
        g[0],
        g[1],
        g[2],
        g[3],
        out_w_qkv,
        vec_sum[4:7, :W].reshape(3 * W),
        own[:W],
        bias_mine,
        out_w_up,
        vec_sum[9 : 9 + FFW // 128].reshape(FFW),
        own[W : W + FFW],
        bias_mine,
    )


def solution(mesh):
    row = P("fsdp", None)
    vec = P("fsdp")
    act = P("dp", "fsdp", None)
    fast = mesh.shape["fsdp"] == 8 and mesh.shape["dp"] == 4
    return jax.shard_map(
        fast_body if fast else body,
        mesh=mesh,
        in_specs=(act, vec, vec, vec, vec, row, vec, row, vec, row, vec, row, vec, act),
        out_specs=(act, act, vec, vec, vec, vec, row, vec, row, vec, row, vec, row, vec),
        check_vma=False,
    )
```

```python
import functools
import math

import jax
import jax.numpy as jnp
import numpy as np
from jax import lax
from jax.experimental import pallas as pl
from jax.experimental.pallas import tpu as pltpu
from jax.sharding import PartitionSpec as P

HEADS = 12
HEAD = 64
ROT = 16

epsilon = 1e-05
inv_root_two = 1.0 / math.sqrt(2.0)
inv_root_twopi = 1.0 / math.sqrt(2.0 * math.pi)
bf16 = jnp.bfloat16
f32 = jnp.float32


def rotary(tensor, cosine, sine, direction):
    half = ROT // 2
    first = tensor[..., :half]
    second = tensor[..., half:ROT]
    return jnp.concatenate(
        [
            first * cosine - direction * second * sine,
            second * cosine + direction * first * sine,
            tensor[..., ROT:],
        ],
        axis=-1,
    )


def dot(a, b, dims):
    return lax.dot_general(a, b, ((dims[0], dims[1]), ((), ())), preferred_element_type=f32)


NN = ((1,), (0,))
NT = ((1,), (1,))
TN = ((0,), (0,))


def gather_rows(arrays):
    return [lax.all_gather(a, "fsdp", axis=0, tiled=True) for a in arrays]


def scatter_rows(a):
    F = lax.axis_size("fsdp")
    got = lax.all_to_all(a, "fsdp", 0, 0, tiled=True)
    return jnp.sum(got.reshape((F, a.shape[0] // F) + a.shape[1:]).astype(f32), axis=0)


def spread_weights(blocks):
    return lax.all_to_all(blocks, "fsdp", 0, 0, tiled=True)


def return_grads(blocks, own):
    n = lax.axis_size("dp")
    F, W, C = blocks.shape
    R, D = own.shape
    parts = jnp.swapaxes(blocks.reshape(F, n, W // n, C), 0, 1).reshape(n, F * (W // n), C)
    own_parts = own.reshape(n, R // n, D)
    if C == D:
        both = jnp.concatenate([parts, own_parts], axis=1)
        both = jnp.sum(lax.all_to_all(both, "dp", 0, 0, tiled=True).astype(f32), axis=0)
        part, own_part = both[: F * (W // n)].astype(bf16), both[F * (W // n) :].astype(bf16)
    else:
        part = jnp.sum(lax.all_to_all(parts, "dp", 0, 0, tiled=True).astype(f32), axis=0)
        own_part = jnp.sum(lax.all_to_all(own_parts, "dp", 0, 0, tiled=True).astype(f32), axis=0)
        part, own_part = part.astype(bf16), own_part.astype(bf16)
    part = lax.all_to_all(part, "fsdp", 0, 0, tiled=True)
    if C == D:
        whole = lax.all_gather(jnp.concatenate([part, own_part], axis=0), "dp", axis=0)
        part_all, own_all = whole[:, : F * (W // n)], whole[:, F * (W // n) :]
    else:
        part_all = lax.all_gather(part, "dp", axis=0)
        own_all = lax.all_gather(own_part, "dp", axis=0)
    part_all = jnp.swapaxes(part_all.reshape(n, F, W // n, C), 0, 1).reshape(F, W, C)
    return part_all, own_all.reshape(R, D)


def body(
    tokens,
    ln1_gain,
    ln1_bias,
    ln2_gain,
    ln2_bias,
    qkv_weight,
    qkv_bias,
    out_weight,
    out_bias,
    up_weight,
    up_bias,
    down_weight,
    down_bias,
    cotangent,
):
    rank = lax.axis_index("fsdp")
    F = lax.axis_size("fsdp")
    rows, D = tokens.shape[1:]
    W = D // F
    FFW = down_weight.shape[0]
    NH = max(-(-((g * W) % HEAD + W) // HEAD) for g in range(F))
    WIN = NH * HEAD
    starts = [min(g * W // HEAD, HEADS - NH) * HEAD for g in range(F)]
    start = jnp.minimum(rank * W // HEAD, HEADS - NH) * HEAD
    off = rank * W - start
    S = rows * F

    qkv3 = qkv_weight.reshape(W, 3, D)
    blocks = jnp.stack(
        [
            jnp.concatenate(
                [
                    qkv3[:, 0, s : s + WIN],
                    qkv3[:, 1, s : s + WIN],
                    qkv3[:, 2, s : s + WIN],
                    up_weight[:, g * FFW : (g + 1) * FFW],
                ],
                axis=1,
            )
            for g, s in enumerate(starts)
        ]
    )
    smalls = jnp.concatenate(
        [ln1_gain, ln1_bias, ln2_gain, ln2_bias, out_bias, down_bias, qkv_bias]
    )
    extra = -(-smalls.shape[0] // (16 * D)) * 16
    smalls = jnp.concatenate([smalls, jnp.zeros(extra * D - smalls.shape[0], bf16)])
    (both_all,) = gather_rows([jnp.concatenate([tokens[0], smalls.reshape(extra, D)], axis=0)])
    both_all = both_all.reshape(F, rows + extra, D)
    x_low = both_all[:, :rows].reshape(S, D)
    small_all = both_all[:, rows:].reshape(F, extra * D)
    wall = spread_weights(blocks).reshape(D, 3 * WIN + FFW)
    w_qkv = wall[:, : 3 * WIN]
    w_up = wall[:, 3 * WIN :]
    up_ring = [(i, (i + 1) % F) for i in range(F)]
    down_ring = [(i, (i - 1) % F) for i in range(F)]
    out_prev = lax.ppermute(out_weight, "fsdp", up_ring)
    out_next = lax.ppermute(out_weight, "fsdp", down_ring)
    (grad_out,) = gather_rows([cotangent[0]])
    out_three = jnp.concatenate(
        [out_prev, out_weight, out_next, jnp.zeros((WIN, D), bf16)], axis=0
    )
    w_out_win = lax.dynamic_slice_in_dim(out_three, W - off, WIN, 0)
    win_col = jnp.arange(WIN, dtype=jnp.int32)
    mine = (win_col >= off) & (win_col < off + W)
    small_all = small_all.astype(f32)
    gain_one, bias_one, gain_two, bias_two, b_out, b_down = [
        small_all[:, i * W : (i + 1) * W].reshape(D) for i in range(6)
    ]
    b_qkv = small_all[:, 6 * W : 9 * W].reshape(3, D)
    b_qkv = lax.dynamic_slice_in_dim(b_qkv, start, WIN, 1).reshape(3 * WIN)
    b_up = up_bias.astype(f32)

    x = x_low.astype(f32)
    center = x - jnp.mean(x, axis=-1, keepdims=True)
    inverse = lax.rsqrt(jnp.mean(center * center, axis=-1, keepdims=True) + epsilon)
    normed = center * inverse
    first_low = (normed * gain_one + bias_one).astype(bf16)
    second_low = (normed * gain_two + bias_two).astype(bf16)

    places = jnp.arange(S, dtype=f32)
    half = ROT // 2
    freq = 10000.0 ** (-(jnp.arange(half, dtype=f32) * 2.0) / ROT)
    angle = places[:, None] * freq[None, :]
    cosine = jnp.cos(angle)[:, None, :]
    sine = jnp.sin(angle)[:, None, :]

    proj = dot(first_low, w_qkv, NN) + b_qkv
    queries = (rotary(proj[:, :WIN].reshape(S, NH, HEAD), cosine, sine, 1.0) * 0.125).astype(bf16)
    keys = rotary(proj[:, WIN : 2 * WIN].reshape(S, NH, HEAD), cosine, sine, 1.0).astype(bf16)
    vals = proj[:, 2 * WIN :].astype(bf16).reshape(S, NH, HEAD)
    q_place = jnp.arange(S, dtype=jnp.int32)
    visible = (q_place[None, :] <= q_place[:, None])[None]
    scores = jnp.einsum("qhd,khd->hqk", queries, keys, preferred_element_type=f32)
    masked = jnp.where(visible, scores, -1e30)
    top = jnp.max(masked, axis=-1, keepdims=True)
    lse = top + jnp.log(jnp.sum(jnp.exp(masked - top), axis=-1, keepdims=True))
    probs = jnp.exp(masked - lse)
    probs_low = probs.astype(bf16)
    attended = jnp.einsum("hqk,khd->qhd", probs_low, vals, preferred_element_type=f32)
    att_low = jnp.where(mine, attended.reshape(S, WIN), 0.0).astype(bf16)

    hidden_pre = dot(second_low, w_up, NN) + b_up
    cdf = 0.5 * (1.0 + lax.erf(hidden_pre * inv_root_two))
    hidden_low = (hidden_pre * cdf).astype(bf16)
    part = dot(att_low, w_out_win, NN) + dot(hidden_low, down_weight, NN)
    branch = scatter_rows(part.astype(bf16))

    grad_hidden = dot(grad_out, down_weight, NT)
    slope = cdf + hidden_pre * jnp.exp(-0.5 * hidden_pre * hidden_pre) * inv_root_twopi
    grad_pre = (grad_hidden * slope).astype(bf16)
    grad_w_down = dot(hidden_low, grad_out, TN)
    grad_w_out_win = dot(att_low, grad_out, TN)
    grad_w_out = lax.dynamic_slice_in_dim(grad_w_out_win, off, W, 0)
    bias_total = jnp.sum(grad_out.astype(f32), axis=0)
    grad_b_up = jnp.sum(grad_pre.astype(f32), axis=0)
    grad_att = dot(grad_out, w_out_win, NT).astype(bf16).reshape(S, NH, HEAD)
    delta = jnp.transpose(jnp.sum(grad_att.astype(f32) * attended, axis=-1))[:, :, None]
    grad_probs = jnp.einsum("qhd,khd->hqk", grad_att, vals, preferred_element_type=f32)
    grad_scores = (probs * (grad_probs - delta)).astype(bf16)
    grad_q = jnp.einsum("hqk,khd->qhd", grad_scores, keys, preferred_element_type=f32)
    grad_k = jnp.einsum("hqk,qhd->khd", grad_scores, queries, preferred_element_type=f32)
    grad_v = jnp.einsum("hqk,qhd->khd", probs_low, grad_att, preferred_element_type=f32)
    grad_proj = jnp.stack(
        [
            rotary(grad_q * 0.125, cosine, sine, -1.0).reshape(S, WIN),
            rotary(grad_k, cosine, sine, -1.0).reshape(S, WIN),
            grad_v.reshape(S, WIN),
        ],
        axis=1,
    )
    grad_proj = jnp.where(mine, grad_proj, 0.0).astype(bf16).reshape(S, 3 * WIN)
    grad_w_qkv = dot(first_low, grad_proj, TN)
    grad_w_up = dot(second_low, grad_pre, TN)
    grad_b_qkv = jnp.sum(grad_proj.astype(f32), axis=0).reshape(3, WIN)
    grad_first = dot(grad_proj, w_qkv, NT)
    grad_second = dot(grad_pre, w_up, NT)
    vectors = [
        jnp.sum(grad_first * normed, axis=0),
        jnp.sum(grad_first, axis=0),
        jnp.sum(grad_second * normed, axis=0),
        jnp.sum(grad_second, axis=0),
    ]
    mixed = grad_first * gain_one + grad_second * gain_two
    b_full = lax.dynamic_update_slice_in_dim(jnp.zeros((3, D), f32), grad_b_qkv, start, 1)
    small_part = jnp.concatenate(
        [v.reshape(F, W) for v in vectors] + [b_full.reshape(F, 3 * W)], axis=1
    )
    mixed_mine = scatter_rows(mixed.astype(bf16))
    small_mine = scatter_rows(small_part)[0]
    own_small = jnp.concatenate(
        [small_mine, lax.dynamic_slice_in_dim(bias_total, rank * W, W, 0), grad_b_up]
    )
    pad = 8 * lax.axis_size("dp")
    own_rows = -(-(W + FFW + -(-own_small.shape[0] // D)) // pad) * pad
    n_small = own_rows - W - FFW
    own_small = jnp.concatenate([own_small, jnp.zeros(n_small * D - own_small.shape[0], f32)])

    grad_blocks = jnp.concatenate([grad_w_qkv, grad_w_up], axis=1).astype(bf16)
    grad_blocks = grad_blocks.reshape(F, W, 3 * WIN + FFW)
    own = jnp.concatenate(
        [grad_w_out, grad_w_down, own_small.reshape(n_small, D)], axis=0
    ).astype(bf16)
    returned, own = return_grads(grad_blocks, own)
    returned = returned.astype(f32)
    own = own.astype(f32)
    own_small = own[W + FFW :].reshape(n_small * D)
    pieces = [
        [returned[g, :, i * WIN + g * W - s : i * WIN + g * W - s + W] for g, s in enumerate(starts)]
        for i in range(3)
    ]
    out_w_qkv = jnp.concatenate(pieces[0] + pieces[1] + pieces[2], axis=1)
    out_w_up = jnp.concatenate([returned[g, :, 3 * WIN :] for g in range(F)], axis=1)

    here = rank * rows
    x_own = tokens[0].astype(f32)
    c_own = x_own - jnp.mean(x_own, axis=-1, keepdims=True)
    i_own = lax.rsqrt(jnp.mean(c_own * c_own, axis=-1, keepdims=True) + epsilon)
    n_own = c_own * i_own
    layer_output = (x_own + branch + b_out + b_down).astype(bf16)
    input_grad = cotangent[0].astype(f32) + i_own * (
        mixed_mine
        - jnp.mean(mixed_mine, axis=-1, keepdims=True)
        - n_own * jnp.mean(mixed_mine * n_own, axis=-1, keepdims=True)
    )
    g = [own_small[i * W : (i + 1) * W] for i in range(4)]
    bias_mine = own_small[7 * W : 8 * W]
    return (
        layer_output[None],
        input_grad[None],
        g[0],
        g[1],
        g[2],
        g[3],
        out_w_qkv,
        own_small[4 * W : 7 * W],
        own[:W],
        bias_mine,
        out_w_up,
        own_small[8 * W : 8 * W + FFW],
        own[W : W + FFW],
        bias_mine,
    )


class Copies:
    def __init__(self):
        self.later = []

    def send(self, src, dst, send_sem, recv_sem, when=None, **to):
        copy = pltpu.make_async_remote_copy(
            src_ref=src,
            dst_ref=dst,
            send_sem=send_sem,
            recv_sem=recv_sem,
            device_id=to,
            device_id_type=pl.DeviceIdType.MESH,
        )
        if when is None:
            copy.start()
        else:
            pl.when(when)(copy.start)
        self.later.append((copy, when))

    def drain(self):
        for copy, when in self.later:
            if when is None:
                copy.wait_send()
            else:
                pl.when(when)(copy.wait_send)
        self.later = []


def arrived(dst, recv_sem, **to):
    pltpu.make_async_remote_copy(
        src_ref=dst,
        dst_ref=dst,
        send_sem=recv_sem,
        recv_sem=recv_sem,
        device_id=to,
        device_id_type=pl.DeviceIdType.MESH,
    ).wait_recv()


def meet(peers):
    barrier = pltpu.get_barrier_semaphore()
    for to in peers:
        pl.semaphore_signal(barrier, inc=1, device_id=to, device_id_type=pl.DeviceIdType.MESH)
    pl.semaphore_wait(barrier, len(peers))


class Spread:
    def __init__(self, copies, buf, send_sem, recv_sem, Z, z, y):
        self.copies, self.buf, self.ss, self.rs = copies, buf, send_sem, recv_sem
        self.Z, self.z, self.y = Z, z, y

    def push(self, src, way, when=None):
        to = {0: src * 0 + (self.z * 2 + self.y + 2), 1: self.z * 2 + self.y - 2, 2: self.z * 2 + 1 - self.y}[way]
        self.copies.send(
            self.buf.at[src], self.buf.at[src], self.ss.at[way, src], self.rs.at[src], when, fsdp=to
        )

    def first(self):
        me = self.z * 2 + self.y
        self.push(me, 0, self.z + 1 < self.Z)
        self.push(me, 1, self.z > 0)
        self.push(me, 2)

    def got(self, src, when=None):
        def wait():
            arrived(self.buf.at[src], self.rs.at[src], fsdp=self.z * 2 + 1 - self.y)

        if when is None:
            wait()
        else:
            pl.when(when)(wait)

    def step(self, k):
        z, y = self.z, self.y
        low, high = jnp.maximum(z - k, 0) * 2 + y, jnp.minimum(z + k, self.Z - 1) * 2 + y
        has_low, has_high = z - k >= 0, z + k < self.Z
        self.got(low, has_low)
        self.push(low, 0, has_low & (z + 1 < self.Z))
        self.push(low, 2, has_low)
        self.got(high, has_high)
        self.push(high, 1, has_high & (z > 0))
        self.push(high, 2, has_high)

    def finish(self):
        for k in range(self.Z):
            self.got(k * 2 + 1 - self.y)


def vmem():
    return pl.BlockSpec(memory_space=pltpu.VMEM)


def add_rows(out, parts):
    step = 16
    for r in range(0, out.shape[0], step):
        total = parts[0][r : r + step].astype(f32)
        for p in parts[1:]:
            total = total + p[r : r + step].astype(f32)
        out[r : r + step] = total.astype(out.dtype)


class Collect:
    def __init__(self, copies, part, yb, ub, db, sb, sems, out, Z, z, y):
        self.__dict__.update(copies=copies, part=part, yb=yb, ub=ub, db=db, sb=sb, out=out, Z=Z, z=z, y=y)
        self.sy, self.ry, self.sz, self.ru, self.rd = [sems.at[i] for i in range(5)]
        self.order = [jnp.where(z < Z // 2, Z - 1 - j, j) for j in range(Z)]

    def first(self):
        for t in self.order:
            self.copies.send(
                self.part.at[t * 2 + 1 - self.y], self.yb.at[t], self.sy.at[t], self.ry.at[t],
                fsdp=self.z * 2 + 1 - self.y,
            )

    def chain(self, t, buf, recv, more, to, active):
        z, y = self.z, self.y

        @pl.when(active & more)
        def _():
            arrived(buf.at[t], recv.at[t], fsdp=z * 2 + 1 - y)
            add_rows(self.sb.at[t], [self.part.at[t * 2 + y], self.yb.at[t], buf.at[t]])

        @pl.when(active & jnp.logical_not(more))
        def _():
            add_rows(self.sb.at[t], [self.part.at[t * 2 + y], self.yb.at[t]])

        self.copies.send(self.sb.at[t], buf.at[t], self.sz.at[t], recv.at[t], active, fsdp=to)

    def step(self, j):
        z, y, Z = self.z, self.y, self.Z
        t = self.order[j]

        @pl.when(t != z)
        def _():
            arrived(self.yb.at[t], self.ry.at[t], fsdp=z * 2 + 1 - y)

        self.chain(t, self.ub, self.ru, z > 0, jnp.minimum(z + 1, Z - 1) * 2 + y, t > z)
        self.chain(t, self.db, self.rd, z < Z - 1, jnp.maximum(z - 1, 0) * 2 + y, t < z)

    def finish(self):
        z, y, Z = self.z, self.y, self.Z
        to = z * 2 + 1 - y
        arrived(self.yb.at[z], self.ry.at[z], fsdp=to)
        base = [self.part.at[z * 2 + y], self.yb.at[z]]

        @pl.when(z > 0)
        def _():
            arrived(self.ub.at[z], self.ru.at[z], fsdp=to)

        @pl.when(z < Z - 1)
        def _():
            arrived(self.db.at[z], self.rd.at[z], fsdp=to)

        @pl.when(z == 0)
        def _():
            add_rows(self.out, base + [self.db.at[z]])

        @pl.when(z == Z - 1)
        def _():
            add_rows(self.out, base + [self.ub.at[z]])

        @pl.when((z > 0) & (z < Z - 1))
        def _():
            add_rows(self.out, base + [self.ub.at[z], self.db.at[z]])


def ln_rows(xall, normed, scale, b):
    x = xall[pl.ds(2 * b, 2)].reshape(RB, xall.shape[2]).astype(f32)
    center = x - jnp.mean(x, axis=-1, keepdims=True)
    inverse = lax.rsqrt(jnp.mean(center * center, axis=-1, keepdims=True) + epsilon)
    normed[block(b)] = center * inverse


RB = 256


def block(b):
    return pl.ds(pl.multiple_of(b * RB, RB), RB)


def turn(t, cosine, low_sine, high_sine):
    return t * cosine + pltpu.roll(t, 120, 1) * low_sine + pltpu.roll(t, 8, 1) * high_sine


def place_matrix(W, at, D):
    row = lax.broadcasted_iota(jnp.int32, (128, D), 0)
    col = lax.broadcasted_iota(jnp.int32, (128, D), 1)
    return ((col - at == row) & (row < W)).astype(f32)


def exact(a, b, dims):
    return lax.dot_general(
        a, b, ((dims[0], dims[1]), ((), ())), preferred_element_type=f32, precision=lax.Precision.HIGHEST
    )


def layer_kernel(
    F,
    tok, cot, small, qkv, up, outw, downw, b_up, freq,
    branch_out, mixed_out, ret, ret_own, vec_sum, full,
    xall, gall, sall, wall, outwin, wblk, placed,
    tabs, normed, first, second, q_s, k_s, v_s, probs, att, att_low, hidden, slope, part, gpre, gatt, gsec, mixed,
    gproj, gq, gk, gv, gout_win, g_mat, g_own, vec, vecs, own_vec,
    yb, ub, db, sb, cbuf, hbuf, xbuf, co_buf, ho_buf, xo_buf, vbuf, vtot,
    sx, rx, sg, rg, s_small, r_small, s_w, r_w, s_o, r_o, sems,
    s_c, r_c, s_x, r_x, s_a, r_a, s_cc, r_cc, s_co, r_co, s_xo, r_xo, s_fo, r_fo, s_v, r_v, s_d, r_d,
):
    me, d = lax.axis_index("fsdp"), lax.axis_index("dp")
    Z, z, y, x, c = F // 2, me // 2, me % 2, d // 2, d % 2
    W, D = outw.shape
    C = wall.shape[3]
    S = normed.shape[0]
    NB = S // RB
    half = W // 2
    others = [lax.rem(me + k, F) for k in range(1, F)]
    sources = [lax.rem(me + F - k, F) for k in range(1, F)]
    xn, cn, dn = d + 2 - 4 * x, d + 1 - 2 * c, (1 - x) * 2 + 1 - c
    meet([{"fsdp": o} for o in others] + [{"dp": xn}, {"dp": cn}, {"dp": dn}])
    copies = Copies()

    xall[me] = tok[...]
    tokens = Spread(copies, xall, sx, rx, Z, z, y)
    tokens.first()
    row = lax.broadcasted_iota(jnp.int32, (256, 128), 0)
    col = lax.broadcasted_iota(jnp.int32, (256, 128), 1)
    shift = (row == col + HEAD).astype(bf16)
    for g in range(F):
        s = g * W // HEAD * HEAD
        for i in range(3):
            at = i * D + s
            if s % 128 == 0:
                piece = qkv[:, at : at + 128]
            else:
                piece = dot(qkv[:, at - 64 : at + 192], shift, NN).astype(bf16)
            wblk[0, g, :, i * 128 : (i + 1) * 128] = piece
        wblk[1, g] = up[:, g * C : (g + 1) * C]
    mine_rows = pl.ds(pl.multiple_of(c * half, half), half)
    for k, o in enumerate(others):
        copies.send(wblk.at[x, o, mine_rows], wall.at[x, me, mine_rows], s_w.at[0, k], r_w.at[0, me], fsdp=o)
    wall[:, me] = wblk[:, me]
    outwin[pl.ds(pl.multiple_of(32 * y, 32), W), :] = outw[...]
    copies.send(
        outw.at[pl.ds(pl.multiple_of((W - 32) * (1 - y), 32), 32)],
        outwin.at[pl.ds(pl.multiple_of(W * y, 32), 32)],
        s_o, r_o, fsdp=z * 2 + 1 - y,
    )
    sall[me] = small[...]
    for k, o in enumerate(others):
        copies.send(small, sall.at[me], s_small.at[k], r_small.at[me], fsdp=o)
    gall[me] = cot[...]
    grads = Spread(copies, gall, sg, rg, Z, z, y)

    tokens.step(1)
    for k, src in enumerate(sources):
        piece = wall.at[x, src, mine_rows]
        arrived(piece, r_w.at[0, src], dp=xn)
        copies.send(piece, piece, s_w.at[1, k], r_w.at[1, src], dp=xn)
        copies.send(piece, piece, s_w.at[2, k], r_w.at[2, src], dp=cn)
    for k in range(2, Z):
        tokens.step(k)
    grads.first()

    lane = lax.broadcasted_iota(jnp.int32, (RB, 128), 1)
    part_lane = lane % HEAD

    def tables(b, _):
        place = (lax.broadcasted_iota(jnp.int32, (RB, 128), 0) + b * RB).astype(f32)
        angle = place * freq[0:1]
        sine = jnp.sin(angle)
        tabs[0, block(b)] = jnp.where(part_lane < ROT, jnp.cos(angle), 1.0)
        tabs[1, block(b)] = jnp.where(part_lane < ROT // 2, -sine, 0.0)
        tabs[2, block(b)] = jnp.where((part_lane >= ROT // 2) & (part_lane < ROT), sine, 0.0)
        return 0

    lax.fori_loop(0, NB, tables, 0)
    for k, src in enumerate(sources):
        piece = wall.at[1 - x, src, mine_rows]
        arrived(piece, r_w.at[1, src], dp=xn)
        copies.send(piece, piece, s_w.at[3, k], r_w.at[3, src], dp=cn)
    for src in sources:
        arrived(sall.at[src], r_small.at[src], dp=xn)
    for b in range(F):
        placed[b, 0:6] = sall[b, 0:6]
        for i in range(3):
            m = F * i + b
            placed[b, 6 + i : 7 + i] = sall[m // 3, 6 + m % 3 : 7 + m % 3]
        placed[b, 9:16] = jnp.zeros((7, 128), f32)
    total = jnp.zeros((16, D), f32)
    for b in range(F):
        total = total + dot(placed[b].astype(bf16), place_matrix(W, b * W, D).astype(bf16), NN)
    full[...] = total
    start = (me // 2) * (3 * HEAD) + HEAD * y
    window = (
        lax.broadcasted_iota(jnp.int32, (D, 128), 0) - start == lax.broadcasted_iota(jnp.int32, (D, 128), 1)
    ).astype(f32)
    b_qkv = dot(total.astype(bf16), window.astype(bf16), NN)
    gain_one, bias_one, gain_two, bias_two = [total[i : i + 1] for i in range(4)]
    off = 32 * y
    mine = ((lane >= off) & (lane < off + W))[0:1]
    tokens.finish()

    def norm(b, _):
        ln_rows(xall, normed, None, b)
        n = normed[block(b)]
        first[block(b)] = (n * gain_one + bias_one).astype(bf16)
        second[block(b)] = (n * gain_two + bias_two).astype(bf16)
        return 0

    lax.fori_loop(0, NB, norm, 0)
    other_rows = pl.ds(pl.multiple_of((1 - c) * half, half), half)
    for src in sources:
        arrived(wall.at[x, src, other_rows], r_w.at[2, src], dp=cn)
        arrived(wall.at[1 - x, src, other_rows], r_w.at[3, src], dp=cn)
    arrived(outwin.at[pl.ds(pl.multiple_of(W * (1 - y), 32), 32)], r_o, fsdp=z * 2 + 1 - y)
    grads.step(1)

    head = [lane // HEAD == h for h in range(2)]

    def project(b, _):
        p = dot(first[block(b)], wall[0].reshape(D, C), NN)
        ct, s1, s2 = tabs[0, block(b)], tabs[1, block(b)], tabs[2, block(b)]
        q = turn(p[:, :128] + b_qkv[6:7], ct, s1, s2) * 0.125
        q_s[block(b)] = q.astype(bf16)
        k_s[block(b)] = turn(p[:, 128:256] + b_qkv[7:8], ct, s1, s2).astype(bf16)
        v_s[block(b)] = (p[:, 256:] + b_qkv[8:9]).astype(bf16)
        u = dot(second[block(b)], wall[1].reshape(D, C), NN) + b_up[...].astype(f32)
        cdf = 0.5 * (1.0 + lax.erf(u * inv_root_two))
        hidden[block(b)] = (u * cdf).astype(bf16)
        slope[block(b)] = cdf + u * jnp.exp(-0.5 * u * u) * inv_root_twopi
        return 0

    lax.fori_loop(0, NB // 2, project, 0)
    grads.step(2)
    lax.fori_loop(NB // 2, NB, project, 0)

    def seen():
        r = lax.broadcasted_iota(jnp.int32, (RB, RB), 0)
        return lax.broadcasted_iota(jnp.int32, (RB, RB), 1) <= r

    def attend(b):
        kv = (b + 1) * RB
        rows = slice(b * RB, kv)
        halves = []
        for h in range(2):
            q = jnp.where(head[h], q_s[rows], jnp.zeros((), bf16))
            s = dot(q, k_s[:kv], NT)
            last = jnp.where(seen(), s[:, kv - RB :], -1e30)
            top = jnp.max(last, axis=-1, keepdims=True)
            if b:
                top = jnp.maximum(top, jnp.max(s[:, : kv - RB], axis=-1, keepdims=True))
            e_last = jnp.exp(last - top)
            norm = jnp.sum(e_last, axis=-1, keepdims=True)
            if b:
                e_rest = jnp.exp(s[:, : kv - RB] - top)
                norm = norm + jnp.sum(e_rest, axis=-1, keepdims=True)
            inv = 1.0 / norm
            probs[h, rows, kv - RB : kv] = (e_last * inv).astype(bf16)
            if b:
                probs[h, rows, : kv - RB] = (e_rest * inv).astype(bf16)
            halves.append(dot(probs[h, rows, :kv], v_s[:kv], NN))
        a = jnp.where(head[0], halves[0], halves[1])
        att[rows] = a
        att_low[rows] = jnp.where(mine, a, 0.0).astype(bf16)
        p = dot(att_low[rows], outwin[...], NN) + dot(hidden[rows], downw[...], NN)
        part[2 * b : 2 * b + 2] = p.astype(bf16).reshape(2, RB // 2, D)

    attend(0)
    attend(1)
    grads.step(3)
    attend(2)
    attend(3)

    one = Collect(copies, part, yb.at[0], ub.at[0], db.at[0], sb.at[0], sems.at[0], branch_out, Z, z, y)
    one.first()
    grads.finish()
    vec[...] = jnp.zeros_like(vec)

    def back(b, _):
        g = gall[pl.ds(2 * b, 2)].reshape(RB, D)
        gp = (dot(g, downw[...], NT) * slope[block(b)]).astype(bf16)
        gpre[block(b)] = gp
        gatt[block(b)] = dot(g, outwin[...], NT).astype(bf16)
        gs = dot(gp, wall[1].reshape(D, C), NT)
        n = normed[block(b)]
        vec[2:3] += jnp.sum(gs * n, axis=0, keepdims=True)
        vec[3:4] += jnp.sum(gs, axis=0, keepdims=True)
        vec[7:8] += jnp.sum(g.astype(f32), axis=0, keepdims=True)
        gsec[block(b)] = gs * gain_two
        sums = jnp.sum(gp.astype(f32), axis=0, keepdims=True)
        for i in range(C // 128):
            own_vec[1 + i : 2 + i] += sums[:, i * 128 : (i + 1) * 128]
        return 0

    own_vec[...] = jnp.zeros_like(own_vec)
    lax.fori_loop(0, NB // 2, back, 0)
    one.step(0)
    lax.fori_loop(NB // 2, NB, back, 0)
    one.step(1)

    g_flat = gall[...].reshape(S, D)
    down_grad = dot(hidden[...], g_flat, TN).astype(bf16)
    q4 = C // 2
    for i in range(2):
        for j in range(2):
            g_own[i, j, half:] = down_grad[j * q4 : (j + 1) * q4, i * C : (i + 1) * C]
    gout_win[...] = dot(att_low[...], g_flat, TN).astype(bf16)
    for i in range(2):
        for j in range(2):
            g_own[i, j, :half] = gout_win[pl.ds(pl.multiple_of(off + j * half, 16), half), i * C : (i + 1) * C]
    for i in range(2):
        copies.send(g_own.at[i, 1 - c], co_buf.at[i], s_co.at[i], r_co.at[i], dp=cn)

    def matrix(m, left, right):
        g = dot(left[...], right[...], TN).astype(bf16).reshape(F, 2, half, C)
        for j in range(2):
            g_mat[m, j] = g[:, j].reshape(F * half, C)
        copies.send(g_mat.at[m, 1 - c], cbuf.at[m], s_c.at[m], r_c.at[m], dp=cn)

    def matrix_x(m):
        arrived(cbuf.at[m], r_c.at[m], dp=cn)
        add_rows(hbuf.at[m], [g_mat.at[m, c], cbuf.at[m]])
        copies.send(hbuf.at[m], xbuf.at[m], s_x.at[m], r_x.at[m], x != m, dp=xn)

    def matrix_spread(m):
        own = x == m

        @pl.when(own)
        def _():
            arrived(xbuf.at[m], r_x.at[m], dp=xn)
            add_rows(hbuf.at[m], [hbuf.at[m], xbuf.at[m]])
            here = pl.ds(pl.multiple_of(me * half, half), half)
            ret[m, c, here] = hbuf[m, here]

        for k, o in enumerate(others):
            there = pl.ds(pl.multiple_of(o * half, half), half)
            here = pl.ds(pl.multiple_of(me * half, half), half)
            copies.send(hbuf.at[m, there], ret.at[m, c, here], s_a.at[m, k], r_a.at[m, me], own, fsdp=o)

    def matrix_share(m):
        own = x == m
        for k, src in enumerate([me] + sources):
            piece = ret.at[m, c, pl.ds(pl.multiple_of(src * half, half), half)]
            if k == 0:

                @pl.when(jnp.logical_not(own))
                def _():
                    arrived(piece, r_a.at[m, src], dp=xn)
            else:
                arrived(piece, r_a.at[m, src], dp=xn)
            copies.send(piece, piece, s_cc.at[m, 0, k], r_a.at[m, src], own, dp=xn)
            copies.send(piece, piece, s_cc.at[m, 1, k], r_cc.at[m, src], dp=cn)

    matrix(1, second, gpre)
    for i in range(2):
        arrived(co_buf.at[i], r_co.at[i], dp=cn)
        add_rows(ho_buf.at[i], [g_own.at[i, c], co_buf.at[i]])
    copies.send(ho_buf.at[1 - x], xo_buf, s_xo, r_xo, dp=xn)
    matrix_x(1)
    one.step(2)

    def attend_back(b):
        kv = (b + 1) * RB
        rows = slice(b * RB, kv)
        ga, a = gatt[rows], att[rows]
        prod = ga.astype(f32) * a
        q_grad = None
        for h in range(2):
            delta = jnp.sum(jnp.where(head[h], prod, 0.0), axis=-1, keepdims=True)
            gah = jnp.where(head[h], ga, jnp.zeros((), bf16))
            qh = jnp.where(head[h], q_s[rows], jnp.zeros((), bf16))
            p = probs[h, rows, :kv]
            gp = dot(gah, v_s[:kv], NT)
            gs_f = p.astype(f32) * (gp - delta)
            last = jnp.where(seen(), gs_f[:, kv - RB :], 0.0).astype(bf16)
            gs = jnp.concatenate([gs_f[:, : kv - RB].astype(bf16), last], axis=1) if b else last
            dq = dot(gs, k_s[:kv], NN)
            q_grad = dq if h == 0 else jnp.where(head[0], q_grad, dq)
            gk[:kv] += dot(gs, qh, TN)
            gv[:kv] += dot(p, gah, TN)
        gq[rows] = q_grad

    gk[...] = jnp.zeros_like(gk)
    gv[...] = jnp.zeros_like(gv)
    attend_back(3)
    one.step(3)
    arrived(xo_buf, r_xo, dp=xn)
    owner = ret_own.at[x, c]
    add_rows(owner, [ho_buf.at[x], xo_buf])
    copies.send(owner, owner, s_fo.at[0], r_fo.at[0], dp=xn)
    copies.send(owner, owner, s_fo.at[1], r_fo.at[1], dp=cn)
    matrix_spread(1)
    attend_back(2)
    one.finish()
    attend_back(1)
    attend_back(0)

    def back_project(b, _):
        ct, s1, s2 = tabs[0, block(b)], tabs[1, block(b)], tabs[2, block(b)]
        dq = turn(gq[block(b)] * 0.125, ct, -s1, -s2)
        dk = turn(gk[block(b)], ct, -s1, -s2)
        for i, t in enumerate((dq, dk, gv[block(b)])):
            low = jnp.where(mine, t, 0.0).astype(bf16)
            gproj[block(b), i * 128 : (i + 1) * 128] = low
            own_vec[8 + i : 9 + i] += jnp.sum(low.astype(f32), axis=0, keepdims=True)
        gf = dot(gproj[block(b)], wall[0].reshape(D, C), NT)
        n = normed[block(b)]
        vec[0:1] += jnp.sum(gf * n, axis=0, keepdims=True)
        vec[1:2] += jnp.sum(gf, axis=0, keepdims=True)
        mixed[pl.ds(2 * b, 2)] = (gf * gain_one + gsec[block(b)]).astype(bf16).reshape(2, RB // 2, D)
        return 0

    lax.fori_loop(0, NB, back_project, 0)
    two = Collect(copies, mixed, yb.at[1], ub.at[1], db.at[1], sb.at[1], sems.at[1], mixed_out, Z, z, y)
    two.first()
    matrix(0, first, gproj)
    matrix_share(1)
    two.step(0)
    matrix_x(0)

    vec[4:7] = exact(own_vec[8:16], window, NT)[0:3]
    pieces = [exact(vec[...], place_matrix(W, b * W, D), NT) for b in range(F)]
    for b in range(F):
        vecs[b, 0:4] = pieces[b][0:4]
        for j in range(3):
            m = 3 * b + j
            vecs[b, 4 + j : 5 + j] = pieces[m % F][4 + m // F : 5 + m // F]
        vecs[b, 7:8] = jnp.zeros((1, 128), f32)
    own_vec[0:1] = exact(vec[...], place_matrix(W, me * W, D), NT)[7:8]
    vbuf[me] = vecs[me]
    for k, o in enumerate(others):
        copies.send(vecs.at[o], vbuf.at[me], s_v.at[k], r_v.at[me], fsdp=o)
    two.step(1)
    matrix_spread(0)
    for src in sources:
        arrived(vbuf.at[src], r_v.at[src], dp=xn)
    total = vbuf[0]
    for g in range(1, F):
        total = total + vbuf[g]
    vtot[d, :8] = total
    vtot[d, 8:] = own_vec[0:8]
    for k, to in enumerate((xn, cn, dn)):
        copies.send(vtot.at[d], vtot.at[d], s_d.at[k], r_d.at[d], dp=to)
    two.step(2)
    two.step(3)
    matrix_share(0)
    arrived(ret_own.at[1 - x, c], r_fo.at[0], dp=xn)
    copies.send(ret_own.at[1 - x, c], ret_own.at[1 - x, c], s_fo.at[2], r_fo.at[2], dp=cn)
    two.finish()
    for to in (xn, cn, dn):
        arrived(vtot.at[to], r_d.at[to], dp=to)
    vec_sum[...] = vtot[0] + vtot[1] + vtot[2] + vtot[3]
    arrived(ret_own.at[x, 1 - c], r_fo.at[1], dp=cn)
    arrived(ret_own.at[1 - x, 1 - c], r_fo.at[2], dp=cn)
    for m in range(2):
        for g in range(F):
            arrived(ret.at[m, 1 - c, pl.ds(g * half, half)], r_cc.at[m, g], dp=cn)
    copies.drain()


def layer(F, tok, cot, small, qkv, up, outw, downw, b_up, freq):
    rows, D = tok.shape
    W, FF = up.shape
    C = FF // F
    S, Z, half = rows * F, F // 2, W // 2
    own = (W + C) // 2
    dma = pltpu.SemaphoreType.DMA
    low = lambda *s: pltpu.VMEM(s, bf16)
    wide = lambda *s: pltpu.VMEM(s, f32)
    return pl.pallas_call(
        functools.partial(layer_kernel, F),
        out_shape=(
            jax.ShapeDtypeStruct((rows, D), f32),
            jax.ShapeDtypeStruct((rows, D), f32),
            jax.ShapeDtypeStruct((2, 2, F * half, C), bf16),
            jax.ShapeDtypeStruct((2, 2, own, C), bf16),
            jax.ShapeDtypeStruct((16, 128), f32),
            jax.ShapeDtypeStruct((16, D), f32),
        ),
        in_specs=[vmem()] * 9,
        out_specs=(vmem(),) * 6,
        scratch_shapes=[
            low(F, rows, D), low(F, rows, D), wide(F, 16, 128), low(2, F, W, C), low(128, D), low(2, F, W, C),
            wide(F, 16, 128),
            wide(3, S, 128), wide(S, D), low(S, D), low(S, D), low(S, 128), low(S, 128), low(S, 128), low(2, S, S),
            wide(S, 128), low(S, 128), low(S, C), wide(S, C), low(F, rows, D), low(S, C), low(S, 128), wide(S, D),
            low(F, rows, D),
            low(S, 3 * 128), wide(S, 128), wide(S, 128), wide(S, 128), low(128, D), low(2, 2, F * half, C),
            low(2, 2, own, C), wide(8, D), wide(F, 8, 128), wide(16, 128),
            low(2, Z, rows, D), low(2, Z, rows, D), low(2, Z, rows, D), low(2, Z, rows, D),
            low(2, F * half, C), low(2, F * half, C), low(2, F * half, C),
            low(2, own, C), low(2, own, C), low(own, C), wide(F, 8, 128), wide(4, 16, 128),
            dma((3, F)), dma((F,)), dma((3, F)), dma((F,)), dma((F,)), dma((F,)), dma((4, F)), dma((4, F)), dma, dma,
            dma((2, 5, Z)),
            dma((2,)), dma((2,)), dma((2,)), dma((2,)), dma((2, F)), dma((2, F)), dma((2, 2, F)), dma((2, F)),
            dma((2,)), dma((2,)), dma, dma, dma((3,)), dma((3,)), dma((F,)), dma((F,)), dma((3,)), dma((4,)),
        ],
        compiler_params=pltpu.CompilerParams(
            collective_id=0, has_side_effects=True, vmem_limit_bytes=60 * 2**20
        ),
        name="layer",
    )(tok, cot, small, qkv, up, outw, downw, b_up, freq)


def finish_kernel(F, tok, cot, branch, mixed, ret, ret_own, full, out, igrad, g_qkv, g_out, g_up, g_down):
    W, D = g_out.shape
    C = ret.shape[3]
    half = W // 2
    x = tok[...].astype(f32)
    center = x - jnp.mean(x, axis=-1, keepdims=True)
    inverse = lax.rsqrt(jnp.mean(center * center, axis=-1, keepdims=True) + epsilon)
    n = center * inverse
    out[...] = (x + branch[...] + full[4:5] + full[5:6]).astype(bf16)
    m = mixed[...]
    m = m - jnp.mean(m, axis=-1, keepdims=True) - n * jnp.mean(m * n, axis=-1, keepdims=True)
    igrad[...] = cot[...].astype(f32) + inverse * m
    row = lax.broadcasted_iota(jnp.int32, (128, D), 0)
    col = lax.broadcasted_iota(jnp.int32, (128, D), 1)
    for j in range(2):
        rows = slice(j * half, (j + 1) * half)
        for i in range(2):
            columns = slice(i * C, (i + 1) * C)
            g_out[rows, columns] = ret_own[i, j, :half].astype(f32)
            g_down[j * (C // 2) : (j + 1) * (C // 2), columns] = ret_own[i, j, half:].astype(f32)
        for g in range(F):
            g_up[rows, g * C : (g + 1) * C] = ret[1, j, g * half : (g + 1) * half].astype(f32)
    for i in range(3):
        total = jnp.zeros((W, D), f32)
        for g in range(F):
            s = g * W // HEAD * HEAD
            place = ((row + s == col) & (col >= g * W) & (col < (g + 1) * W)).astype(bf16)
            piece = jnp.concatenate(
                [ret[0, j, g * half : (g + 1) * half, i * 128 : (i + 1) * 128] for j in range(2)], axis=0
            )
            total = total + dot(piece, place, NN)
        g_qkv[:, i * D : (i + 1) * D] = total


def finish(F, tok, cot, branch, mixed, ret, ret_own, full):
    rows, D = tok.shape
    W = D // F
    C = ret.shape[3]
    return pl.pallas_call(
        functools.partial(finish_kernel, F),
        out_shape=(
            jax.ShapeDtypeStruct((rows, D), bf16),
            jax.ShapeDtypeStruct((rows, D), f32),
            jax.ShapeDtypeStruct((W, 3 * D), f32),
            jax.ShapeDtypeStruct((W, D), f32),
            jax.ShapeDtypeStruct((W, F * C), f32),
            jax.ShapeDtypeStruct((C, D), f32),
        ),
        in_specs=[vmem()] * 7,
        out_specs=(vmem(),) * 6,
        compiler_params=pltpu.CompilerParams(vmem_limit_bytes=40 * 2**20),
        name="finish",
    )(tok, cot, branch, mixed, ret, ret_own, full)


def fast_body(
    tokens, ln1_gain, ln1_bias, ln2_gain, ln2_bias, qkv_weight, qkv_bias, out_weight, out_bias, up_weight, up_bias,
    down_weight, down_bias, cotangent,
):
    F = lax.axis_size("fsdp")
    W, FF = up_weight.shape
    C = FF // F
    small = jnp.stack([ln1_gain, ln1_bias, ln2_gain, ln2_bias, out_bias, down_bias])
    small = jnp.concatenate([small, qkv_bias.reshape(3, W)], axis=0)
    small = jnp.pad(small, ((0, 7), (0, 128 - W))).astype(f32)
    lane = np.arange(128) % HEAD % (ROT // 2)
    freq = np.broadcast_to(np.float32(10000.0) ** (-(lane.astype(np.float32) * 2.0) / ROT), (8, 128))
    branch, mixed, ret, ret_own, vec_sum, full = layer(
        F, tokens[0], cotangent[0], small, qkv_weight, up_weight, out_weight, down_weight, up_bias[None],
        jnp.asarray(freq, f32),
    )
    out, igrad, g_qkv, g_out, g_up, g_down = finish(
        F, tokens[0], cotangent[0], branch, mixed, ret, ret_own, full
    )
    bias = vec_sum[8, :W]
    return (
        out[None], igrad[None], vec_sum[0, :W], vec_sum[1, :W], vec_sum[2, :W], vec_sum[3, :W],
        g_qkv, vec_sum[4:7, :W].reshape(3 * W), g_out, bias, g_up, vec_sum[9 : 9 + C // 128].reshape(C), g_down, bias,
    )


def solution(mesh):
    row = P("fsdp", None)
    vec = P("fsdp")
    act = P("dp", "fsdp", None)
    fast = mesh.shape["fsdp"] == 8 and mesh.shape["dp"] == 4
    return jax.shard_map(
        fast_body if fast else body,
        mesh=mesh,
        in_specs=(act, vec, vec, vec, vec, row, vec, row, vec, row, vec, row, vec, act),
        out_specs=(act, act, vec, vec, vec, vec, row, vec, row, vec, row, vec, row, vec),
        check_vma=False,
    )
```

```python
import functools
import math

import jax
import jax.numpy as jnp
from jax import lax
from jax.experimental import pallas as pl
from jax.experimental.pallas import tpu as pltpu
from jax.sharding import PartitionSpec as P

HEADS = 12
HEAD = 64
ROT = 16

epsilon = 1e-05
inv_root_two = 1.0 / math.sqrt(2.0)
inv_root_twopi = 1.0 / math.sqrt(2.0 * math.pi)
bf16 = jnp.bfloat16
f32 = jnp.float32


def rotary(tensor, cosine, sine, direction):
    half = ROT // 2
    first = tensor[..., :half]
    second = tensor[..., half:ROT]
    return jnp.concatenate(
        [
            first * cosine - direction * second * sine,
            second * cosine + direction * first * sine,
            tensor[..., ROT:],
        ],
        axis=-1,
    )


def dot(a, b, dims):
    return lax.dot_general(a, b, ((dims[0], dims[1]), ((), ())), preferred_element_type=f32)


NN = ((1,), (0,))
NT = ((1,), (1,))
TN = ((0,), (0,))


def gather_rows(arrays):
    return [lax.all_gather(a, "fsdp", axis=0, tiled=True) for a in arrays]


def scatter_rows(a):
    F = lax.axis_size("fsdp")
    got = lax.all_to_all(a, "fsdp", 0, 0, tiled=True)
    return jnp.sum(got.reshape((F, a.shape[0] // F) + a.shape[1:]).astype(f32), axis=0)


def spread_weights(blocks):
    return lax.all_to_all(blocks, "fsdp", 0, 0, tiled=True)


def return_grads(blocks, own):
    n = lax.axis_size("dp")
    F, W, C = blocks.shape
    R, D = own.shape
    parts = jnp.swapaxes(blocks.reshape(F, n, W // n, C), 0, 1).reshape(n, F * (W // n), C)
    own_parts = own.reshape(n, R // n, D)
    if C == D:
        both = jnp.concatenate([parts, own_parts], axis=1)
        both = jnp.sum(lax.all_to_all(both, "dp", 0, 0, tiled=True).astype(f32), axis=0)
        part, own_part = both[: F * (W // n)].astype(bf16), both[F * (W // n) :].astype(bf16)
    else:
        part = jnp.sum(lax.all_to_all(parts, "dp", 0, 0, tiled=True).astype(f32), axis=0)
        own_part = jnp.sum(lax.all_to_all(own_parts, "dp", 0, 0, tiled=True).astype(f32), axis=0)
        part, own_part = part.astype(bf16), own_part.astype(bf16)
    part = lax.all_to_all(part, "fsdp", 0, 0, tiled=True)
    if C == D:
        whole = lax.all_gather(jnp.concatenate([part, own_part], axis=0), "dp", axis=0)
        part_all, own_all = whole[:, : F * (W // n)], whole[:, F * (W // n) :]
    else:
        part_all = lax.all_gather(part, "dp", axis=0)
        own_all = lax.all_gather(own_part, "dp", axis=0)
    part_all = jnp.swapaxes(part_all.reshape(n, F, W // n, C), 0, 1).reshape(F, W, C)
    return part_all, own_all.reshape(R, D)


def body(
    tokens,
    ln1_gain,
    ln1_bias,
    ln2_gain,
    ln2_bias,
    qkv_weight,
    qkv_bias,
    out_weight,
    out_bias,
    up_weight,
    up_bias,
    down_weight,
    down_bias,
    cotangent,
):
    rank = lax.axis_index("fsdp")
    F = lax.axis_size("fsdp")
    rows, D = tokens.shape[1:]
    W = D // F
    FFW = down_weight.shape[0]
    NH = max(-(-((g * W) % HEAD + W) // HEAD) for g in range(F))
    WIN = NH * HEAD
    starts = [min(g * W // HEAD, HEADS - NH) * HEAD for g in range(F)]
    start = jnp.minimum(rank * W // HEAD, HEADS - NH) * HEAD
    off = rank * W - start
    S = rows * F

    qkv3 = qkv_weight.reshape(W, 3, D)
    blocks = jnp.stack(
        [
            jnp.concatenate(
                [
                    qkv3[:, 0, s : s + WIN],
                    qkv3[:, 1, s : s + WIN],
                    qkv3[:, 2, s : s + WIN],
                    up_weight[:, g * FFW : (g + 1) * FFW],
                ],
                axis=1,
            )
            for g, s in enumerate(starts)
        ]
    )
    smalls = jnp.concatenate(
        [ln1_gain, ln1_bias, ln2_gain, ln2_bias, out_bias, down_bias, qkv_bias]
    )
    extra = -(-smalls.shape[0] // (16 * D)) * 16
    smalls = jnp.concatenate([smalls, jnp.zeros(extra * D - smalls.shape[0], bf16)])
    (both_all,) = gather_rows([jnp.concatenate([tokens[0], smalls.reshape(extra, D)], axis=0)])
    both_all = both_all.reshape(F, rows + extra, D)
    x_low = both_all[:, :rows].reshape(S, D)
    small_all = both_all[:, rows:].reshape(F, extra * D)
    wall = spread_weights(blocks).reshape(D, 3 * WIN + FFW)
    w_qkv = wall[:, : 3 * WIN]
    w_up = wall[:, 3 * WIN :]
    up_ring = [(i, (i + 1) % F) for i in range(F)]
    down_ring = [(i, (i - 1) % F) for i in range(F)]
    out_prev = lax.ppermute(out_weight, "fsdp", up_ring)
    out_next = lax.ppermute(out_weight, "fsdp", down_ring)
    (grad_out,) = gather_rows([cotangent[0]])
    out_three = jnp.concatenate(
        [out_prev, out_weight, out_next, jnp.zeros((WIN, D), bf16)], axis=0
    )
    w_out_win = lax.dynamic_slice_in_dim(out_three, W - off, WIN, 0)
    win_col = jnp.arange(WIN, dtype=jnp.int32)
    mine = (win_col >= off) & (win_col < off + W)
    small_all = small_all.astype(f32)
    gain_one, bias_one, gain_two, bias_two, b_out, b_down = [
        small_all[:, i * W : (i + 1) * W].reshape(D) for i in range(6)
    ]
    b_qkv = small_all[:, 6 * W : 9 * W].reshape(3, D)
    b_qkv = lax.dynamic_slice_in_dim(b_qkv, start, WIN, 1).reshape(3 * WIN)
    b_up = up_bias.astype(f32)

    x = x_low.astype(f32)
    center = x - jnp.mean(x, axis=-1, keepdims=True)
    inverse = lax.rsqrt(jnp.mean(center * center, axis=-1, keepdims=True) + epsilon)
    normed = center * inverse
    first_low = (normed * gain_one + bias_one).astype(bf16)
    second_low = (normed * gain_two + bias_two).astype(bf16)

    places = jnp.arange(S, dtype=f32)
    half = ROT // 2
    freq = 10000.0 ** (-(jnp.arange(half, dtype=f32) * 2.0) / ROT)
    angle = places[:, None] * freq[None, :]
    cosine = jnp.cos(angle)[:, None, :]
    sine = jnp.sin(angle)[:, None, :]

    proj = dot(first_low, w_qkv, NN) + b_qkv
    queries = (rotary(proj[:, :WIN].reshape(S, NH, HEAD), cosine, sine, 1.0) * 0.125).astype(bf16)
    keys = rotary(proj[:, WIN : 2 * WIN].reshape(S, NH, HEAD), cosine, sine, 1.0).astype(bf16)
    vals = proj[:, 2 * WIN :].astype(bf16).reshape(S, NH, HEAD)
    q_place = jnp.arange(S, dtype=jnp.int32)
    visible = (q_place[None, :] <= q_place[:, None])[None]
    scores = jnp.einsum("qhd,khd->hqk", queries, keys, preferred_element_type=f32)
    masked = jnp.where(visible, scores, -1e30)
    top = jnp.max(masked, axis=-1, keepdims=True)
    lse = top + jnp.log(jnp.sum(jnp.exp(masked - top), axis=-1, keepdims=True))
    probs = jnp.exp(masked - lse)
    probs_low = probs.astype(bf16)
    attended = jnp.einsum("hqk,khd->qhd", probs_low, vals, preferred_element_type=f32)
    att_low = jnp.where(mine, attended.reshape(S, WIN), 0.0).astype(bf16)

    hidden_pre = dot(second_low, w_up, NN) + b_up
    cdf = 0.5 * (1.0 + lax.erf(hidden_pre * inv_root_two))
    hidden_low = (hidden_pre * cdf).astype(bf16)
    part = dot(att_low, w_out_win, NN) + dot(hidden_low, down_weight, NN)
    branch = scatter_rows(part.astype(bf16))

    grad_hidden = dot(grad_out, down_weight, NT)
    slope = cdf + hidden_pre * jnp.exp(-0.5 * hidden_pre * hidden_pre) * inv_root_twopi
    grad_pre = (grad_hidden * slope).astype(bf16)
    grad_w_down = dot(hidden_low, grad_out, TN)
    grad_w_out_win = dot(att_low, grad_out, TN)
    grad_w_out = lax.dynamic_slice_in_dim(grad_w_out_win, off, W, 0)
    bias_total = jnp.sum(grad_out.astype(f32), axis=0)
    grad_b_up = jnp.sum(grad_pre.astype(f32), axis=0)
    grad_att = dot(grad_out, w_out_win, NT).astype(bf16).reshape(S, NH, HEAD)
    delta = jnp.transpose(jnp.sum(grad_att.astype(f32) * attended, axis=-1))[:, :, None]
    grad_probs = jnp.einsum("qhd,khd->hqk", grad_att, vals, preferred_element_type=f32)
    grad_scores = (probs * (grad_probs - delta)).astype(bf16)
    grad_q = jnp.einsum("hqk,khd->qhd", grad_scores, keys, preferred_element_type=f32)
    grad_k = jnp.einsum("hqk,qhd->khd", grad_scores, queries, preferred_element_type=f32)
    grad_v = jnp.einsum("hqk,qhd->khd", probs_low, grad_att, preferred_element_type=f32)
    grad_proj = jnp.stack(
        [
            rotary(grad_q * 0.125, cosine, sine, -1.0).reshape(S, WIN),
            rotary(grad_k, cosine, sine, -1.0).reshape(S, WIN),
            grad_v.reshape(S, WIN),
        ],
        axis=1,
    )
    grad_proj = jnp.where(mine, grad_proj, 0.0).astype(bf16).reshape(S, 3 * WIN)
    grad_w_qkv = dot(first_low, grad_proj, TN)
    grad_w_up = dot(second_low, grad_pre, TN)
    grad_b_qkv = jnp.sum(grad_proj.astype(f32), axis=0).reshape(3, WIN)
    grad_first = dot(grad_proj, w_qkv, NT)
    grad_second = dot(grad_pre, w_up, NT)
    vectors = [
        jnp.sum(grad_first * normed, axis=0),
        jnp.sum(grad_first, axis=0),
        jnp.sum(grad_second * normed, axis=0),
        jnp.sum(grad_second, axis=0),
    ]
    mixed = grad_first * gain_one + grad_second * gain_two
    b_full = lax.dynamic_update_slice_in_dim(jnp.zeros((3, D), f32), grad_b_qkv, start, 1)
    small_part = jnp.concatenate(
        [v.reshape(F, W) for v in vectors] + [b_full.reshape(F, 3 * W)], axis=1
    )
    mixed_mine = scatter_rows(mixed.astype(bf16))
    small_mine = scatter_rows(small_part)[0]
    own_small = jnp.concatenate(
        [small_mine, lax.dynamic_slice_in_dim(bias_total, rank * W, W, 0), grad_b_up]
    )
    pad = 8 * lax.axis_size("dp")
    own_rows = -(-(W + FFW + -(-own_small.shape[0] // D)) // pad) * pad
    n_small = own_rows - W - FFW
    own_small = jnp.concatenate([own_small, jnp.zeros(n_small * D - own_small.shape[0], f32)])

    grad_blocks = jnp.concatenate([grad_w_qkv, grad_w_up], axis=1).astype(bf16)
    grad_blocks = grad_blocks.reshape(F, W, 3 * WIN + FFW)
    own = jnp.concatenate(
        [grad_w_out, grad_w_down, own_small.reshape(n_small, D)], axis=0
    ).astype(bf16)
    returned, own = return_grads(grad_blocks, own)
    returned = returned.astype(f32)
    own = own.astype(f32)
    own_small = own[W + FFW :].reshape(n_small * D)
    pieces = [
        [returned[g, :, i * WIN + g * W - s : i * WIN + g * W - s + W] for g, s in enumerate(starts)]
        for i in range(3)
    ]
    out_w_qkv = jnp.concatenate(pieces[0] + pieces[1] + pieces[2], axis=1)
    out_w_up = jnp.concatenate([returned[g, :, 3 * WIN :] for g in range(F)], axis=1)

    here = rank * rows
    x_own = tokens[0].astype(f32)
    c_own = x_own - jnp.mean(x_own, axis=-1, keepdims=True)
    i_own = lax.rsqrt(jnp.mean(c_own * c_own, axis=-1, keepdims=True) + epsilon)
    n_own = c_own * i_own
    layer_output = (x_own + branch + b_out + b_down).astype(bf16)
    input_grad = cotangent[0].astype(f32) + i_own * (
        mixed_mine
        - jnp.mean(mixed_mine, axis=-1, keepdims=True)
        - n_own * jnp.mean(mixed_mine * n_own, axis=-1, keepdims=True)
    )
    g = [own_small[i * W : (i + 1) * W] for i in range(4)]
    bias_mine = own_small[7 * W : 8 * W]
    return (
        layer_output[None],
        input_grad[None],
        g[0],
        g[1],
        g[2],
        g[3],
        out_w_qkv,
        own_small[4 * W : 7 * W],
        own[:W],
        bias_mine,
        out_w_up,
        own_small[8 * W : 8 * W + FFW],
        own[W : W + FFW],
        bias_mine,
    )


class Copies:
    def __init__(self):
        self.later = []

    def send(self, src, dst, send_sem, recv_sem, when=None, **to):
        copy = pltpu.make_async_remote_copy(
            src_ref=src,
            dst_ref=dst,
            send_sem=send_sem,
            recv_sem=recv_sem,
            device_id=to,
            device_id_type=pl.DeviceIdType.MESH,
        )
        if when is None:
            copy.start()
        else:
            pl.when(when)(copy.start)
        self.later.append((copy, when))

    def drain(self):
        for copy, when in self.later:
            if when is None:
                copy.wait_send()
            else:
                pl.when(when)(copy.wait_send)
        self.later = []


def arrived(dst, recv_sem, **to):
    pltpu.make_async_remote_copy(
        src_ref=dst,
        dst_ref=dst,
        send_sem=recv_sem,
        recv_sem=recv_sem,
        device_id=to,
        device_id_type=pl.DeviceIdType.MESH,
    ).wait_recv()


def meet(peers):
    barrier = pltpu.get_barrier_semaphore()
    for to in peers:
        pl.semaphore_signal(barrier, inc=1, device_id=to, device_id_type=pl.DeviceIdType.MESH)
    pl.semaphore_wait(barrier, len(peers))


class Spread:
    def __init__(self, copies, buf, send_sem, recv_sem, Z, z, y):
        self.copies, self.buf, self.ss, self.rs = copies, buf, send_sem, recv_sem
        self.Z, self.z, self.y = Z, z, y

    def push(self, src, way, when=None):
        to = {0: src * 0 + (self.z * 2 + self.y + 2), 1: self.z * 2 + self.y - 2, 2: self.z * 2 + 1 - self.y}[way]
        self.copies.send(
            self.buf.at[src], self.buf.at[src], self.ss.at[way, src], self.rs.at[src], when, fsdp=to
        )

    def first(self):
        me = self.z * 2 + self.y
        self.push(me, 0, self.z + 1 < self.Z)
        self.push(me, 1, self.z > 0)
        self.push(me, 2)

    def got(self, src, when=None):
        def wait():
            arrived(self.buf.at[src], self.rs.at[src], fsdp=self.z * 2 + 1 - self.y)

        if when is None:
            wait()
        else:
            pl.when(when)(wait)

    def step(self, k):
        z, y = self.z, self.y
        low, high = jnp.maximum(z - k, 0) * 2 + y, jnp.minimum(z + k, self.Z - 1) * 2 + y
        has_low, has_high = z - k >= 0, z + k < self.Z
        self.got(low, has_low)
        self.push(low, 0, has_low & (z + 1 < self.Z))
        self.push(low, 2, has_low)
        self.got(high, has_high)
        self.push(high, 1, has_high & (z > 0))
        self.push(high, 2, has_high)

    def finish(self):
        for k in range(self.Z):
            self.got(k * 2 + 1 - self.y)


def vmem():
    return pl.BlockSpec(memory_space=pltpu.VMEM)


def add_rows(out, parts):
    step = 16
    for r in range(0, out.shape[0], step):
        total = parts[0][r : r + step].astype(f32)
        for p in parts[1:]:
            total = total + p[r : r + step].astype(f32)
        out[r : r + step] = total.astype(out.dtype)


class Collect:
    def __init__(self, copies, part, yb, zb, sb, sems, out, Z, z, y):
        self.__dict__.update(copies=copies, part=part, yb=yb, zb=zb, sb=sb, out=out, Z=Z, z=z, y=y)
        self.sy, self.ry, self.sz, self.rz = [sems.at[i] for i in range(4)]
        zb[z] = jnp.zeros(zb.shape[1:], zb.dtype)

    def push(self, t):
        self.copies.send(
            self.part.at[t * 2 + 1 - self.y], self.yb.at[t], self.sy.at[t], self.ry.at[t],
            fsdp=self.z * 2 + 1 - self.y,
        )

    def step(self, t):
        z, y = self.z, self.y
        away = t != z

        @pl.when(away)
        def _():
            arrived(self.yb.at[t], self.ry.at[t], fsdp=z * 2 + 1 - y)
            add_rows(self.sb.at[t], [self.part.at[t * 2 + y], self.yb.at[t]])

        self.copies.send(self.sb.at[t], self.zb.at[z], self.sz.at[t], self.rz.at[z], away, fsdp=t * 2 + y)

    def finish(self):
        z, y, Z = self.z, self.y, self.Z
        to = z * 2 + 1 - y
        arrived(self.yb.at[z], self.ry.at[z], fsdp=to)
        for k in range(1, Z):
            src = lax.rem(z + k, Z)
            arrived(self.zb.at[src], self.rz.at[src], fsdp=to)
        add_rows(self.out, [self.part.at[z * 2 + y], self.yb.at[z]] + [self.zb.at[k] for k in range(Z)])


def ln_rows(xall, normed, scale, b):
    x = xall[pl.ds(2 * b, 2)].reshape(RB, xall.shape[2]).astype(f32)
    center = x - jnp.mean(x, axis=-1, keepdims=True)
    inverse = lax.rsqrt(jnp.mean(center * center, axis=-1, keepdims=True) + epsilon)
    normed[block(b)] = center * inverse


RB = 256


def block(b):
    return pl.ds(pl.multiple_of(b * RB, RB), RB)


def turn(t, cosine, low_sine, high_sine):
    return t * cosine + pltpu.roll(t, 120, 1) * low_sine + pltpu.roll(t, 8, 1) * high_sine


def place_matrix(W, at, D):
    row = lax.broadcasted_iota(jnp.int32, (128, D), 0)
    col = lax.broadcasted_iota(jnp.int32, (128, D), 1)
    return ((col - at == row) & (row < W)).astype(f32)


def exact(a, b, dims):
    return lax.dot_general(
        a, b, ((dims[0], dims[1]), ((), ())), preferred_element_type=f32, precision=lax.Precision.HIGHEST
    )


def layer_kernel(
    F,
    tok, cot, qkv_in, up_in, outw_in, downw_in, v0, v1, v2, v3, v4, v5, qkv_bias, b_up,
    branch_out, mixed_out, ret, ret_own, vec_sum, full,
    xall, gall, sall, wall, outwin, wblk, placed,
    tabs, normed, first, second, q_s, k_s, v_s, probs, att, att_low, hidden, slope, part, gpre, gatt, gsec, mixed,
    gproj, gq, gk, gv, gout_win, g_mat, g_own, vec, vecs, own_vec,
    qkv, up, outw, downw, small, yb, zb, sb, cbuf, hbuf, xbuf, co_buf, ho_buf, xo_buf, vbuf, vtot,
    sx, rx, sg, rg, s_small, r_small, s_w, r_w, s_o, r_o, sems,
    s_c, r_c, s_x, r_x, s_a, r_a, s_cc, r_cc, s_co, r_co, s_xo, r_xo, s_fo, r_fo, s_v, r_v, s_d, r_d, s_in,
):
    me, d = lax.axis_index("fsdp"), lax.axis_index("dp")
    Z, z, y, x, c = F // 2, me // 2, me % 2, d // 2, d % 2
    W, D = outw.shape
    C = wall.shape[3]
    S = normed.shape[0]
    NB = S // RB
    half = W // 2
    others = [lax.rem(me + k, F) for k in range(1, F)]
    sources = [lax.rem(me + F - k, F) for k in range(1, F)]
    xn, cn, dn = d + 2 - 4 * x, d + 1 - 2 * c, (1 - x) * 2 + 1 - c
    fetches = [
        pltpu.make_async_copy(src, dst, s_in.at[i])
        for i, (src, dst) in enumerate(
            (
                (tok, xall.at[me]), (qkv_in, qkv), (up_in, up), (outw_in, outw), (cot, gall.at[me]), (downw_in, downw)
            )
        )
    ]
    for fetch in fetches:
        fetch.start()
    small[...] = jnp.zeros_like(small)
    for i, v in enumerate((v0, v1, v2, v3, v4, v5)):
        small[i : i + 1, :W] = v[...].astype(f32).reshape(1, W)
    shifts = qkv_bias[...].astype(f32).reshape(1, 3 * W)
    for i in range(3):
        small[6 + i : 7 + i, :W] = shifts[:, i * W : (i + 1) * W]
    meet([{"fsdp": o} for o in others] + [{"dp": xn}, {"dp": cn}, {"dp": dn}])
    copies = Copies()

    fetches[0].wait()
    tokens = Spread(copies, xall, sx, rx, Z, z, y)
    tokens.first()
    sall[me] = small[...]
    for k, o in enumerate(others):
        copies.send(small, sall.at[me], s_small.at[k], r_small.at[me], fsdp=o)
    for fetch in fetches[1:4]:
        fetch.wait()
    row = lax.broadcasted_iota(jnp.int32, (256, 128), 0)
    col = lax.broadcasted_iota(jnp.int32, (256, 128), 1)
    shift = (row == col + HEAD).astype(bf16)
    for g in range(F):
        s = g * W // HEAD * HEAD
        for i in range(3):
            at = i * D + s
            if s % 128 == 0:
                piece = qkv[:, at : at + 128]
            else:
                piece = dot(qkv[:, at - 64 : at + 192], shift, NN).astype(bf16)
            wblk[0, g, :, i * 128 : (i + 1) * 128] = piece
        wblk[1, g] = up[:, g * C : (g + 1) * C]
    mine_rows = pl.ds(pl.multiple_of(c * half, half), half)
    for k, o in enumerate(others):
        copies.send(wblk.at[x, o, mine_rows], wall.at[x, me, mine_rows], s_w.at[0, k], r_w.at[0, me], fsdp=o)
    wall[:, me] = wblk[:, me]
    outwin[pl.ds(pl.multiple_of(32 * y, 32), W), :] = outw[...]
    copies.send(
        outw.at[pl.ds(pl.multiple_of((W - 32) * (1 - y), 32), 32)],
        outwin.at[pl.ds(pl.multiple_of(W * y, 32), 32)],
        s_o, r_o, fsdp=z * 2 + 1 - y,
    )
    for fetch in fetches[4:]:
        fetch.wait()
    grads = Spread(copies, gall, sg, rg, Z, z, y)

    near = []
    for j in range(Z):
        at = jnp.int32(0)
        for i in range(Z):
            ranked = sorted(range(Z), key=lambda t: abs(t - i))
            at = jnp.where(z == i, ranked[j], at)
        near.append(at)
    tokens.step(1)
    tokens.step(2)
    for k, src in enumerate(sources):
        piece = wall.at[x, src, mine_rows]
        arrived(piece, r_w.at[0, src], dp=xn)
        copies.send(piece, piece, s_w.at[1, k], r_w.at[1, src], dp=xn)
        copies.send(piece, piece, s_w.at[2, k], r_w.at[2, src], dp=cn)
    grads.first()
    for k in range(3, Z):
        tokens.step(k)

    lane = lax.broadcasted_iota(jnp.int32, (RB, 128), 1)
    part_lane = lane % HEAD
    exponent = (part_lane[0:1] % (ROT // 2)).astype(f32) * (-2.0 * math.log(10000.0) / ROT)
    freq = jnp.exp(exponent)

    def tables(b, _):
        place = (lax.broadcasted_iota(jnp.int32, (RB, 128), 0) + b * RB).astype(f32)
        angle = place * freq
        sine = jnp.sin(angle)
        tabs[0, block(b)] = jnp.where(part_lane < ROT, jnp.cos(angle), 1.0)
        tabs[1, block(b)] = jnp.where(part_lane < ROT // 2, -sine, 0.0)
        tabs[2, block(b)] = jnp.where((part_lane >= ROT // 2) & (part_lane < ROT), sine, 0.0)
        return 0

    lax.fori_loop(0, NB, tables, 0)
    for k, src in enumerate(sources):
        piece = wall.at[1 - x, src, mine_rows]
        arrived(piece, r_w.at[1, src], dp=xn)
        copies.send(piece, piece, s_w.at[3, k], r_w.at[3, src], dp=cn)
    for src in sources:
        arrived(sall.at[src], r_small.at[src], dp=xn)
    for b in range(F):
        placed[b, 0:6] = sall[b, 0:6]
        for i in range(3):
            m = F * i + b
            placed[b, 6 + i : 7 + i] = sall[m // 3, 6 + m % 3 : 7 + m % 3]
        placed[b, 9:16] = jnp.zeros((7, 128), f32)
    total = jnp.zeros((16, D), f32)
    for b in range(F):
        total = total + dot(placed[b].astype(bf16), place_matrix(W, b * W, D).astype(bf16), NN)
    full[...] = total
    start = (me // 2) * (3 * HEAD) + HEAD * y
    window = (
        lax.broadcasted_iota(jnp.int32, (D, 128), 0) - start == lax.broadcasted_iota(jnp.int32, (D, 128), 1)
    ).astype(f32)
    b_qkv = dot(total.astype(bf16), window.astype(bf16), NN)
    gain_one, bias_one, gain_two, bias_two = [total[i : i + 1] for i in range(4)]
    off = 32 * y
    mine = ((lane >= off) & (lane < off + W))[0:1]

    def norm(b):
        ln_rows(xall, normed, None, b)
        n = normed[block(b)]
        first[block(b)] = (n * gain_one + bias_one).astype(bf16)
        second[block(b)] = (n * gain_two + bias_two).astype(bf16)

    up_shift = b_up[...].astype(f32).reshape(1, C)
    head = [lane // HEAD == h for h in range(2)]

    def project(b):
        p = dot(first[block(b)], wall[0].reshape(D, C), NN)
        ct, s1, s2 = tabs[0, block(b)], tabs[1, block(b)], tabs[2, block(b)]
        q = turn(p[:, :128] + b_qkv[6:7], ct, s1, s2) * 0.125
        q_s[block(b)] = q.astype(bf16)
        k_s[block(b)] = turn(p[:, 128:256] + b_qkv[7:8], ct, s1, s2).astype(bf16)
        v_s[block(b)] = (p[:, 256:] + b_qkv[8:9]).astype(bf16)
        u = dot(second[block(b)], wall[1].reshape(D, C), NN) + up_shift
        cdf = 0.5 * (1.0 + lax.erf(u * inv_root_two))
        hidden[block(b)] = (u * cdf).astype(bf16)
        slope[block(b)] = cdf + u * jnp.exp(-0.5 * u * u) * inv_root_twopi

    other_rows = pl.ds(pl.multiple_of((1 - c) * half, half), half)
    for j, b in enumerate(near):
        tokens.got(2 * b + 1 - y)
        norm(b)
        if j == 1:
            grads.step(1)
            for src in sources:
                arrived(wall.at[x, src, other_rows], r_w.at[2, src], dp=cn)
                arrived(wall.at[1 - x, src, other_rows], r_w.at[3, src], dp=cn)
            arrived(outwin.at[pl.ds(pl.multiple_of(W * (1 - y), 32), 32)], r_o, fsdp=z * 2 + 1 - y)
            project(near[0])
        if j:
            project(b)
    grads.step(2)

    def seen():
        r = lax.broadcasted_iota(jnp.int32, (RB, RB), 0)
        return lax.broadcasted_iota(jnp.int32, (RB, RB), 1) <= r

    def attend(b):
        kv = (b + 1) * RB
        rows = slice(b * RB, kv)
        halves = []
        for h in range(2):
            q = jnp.where(head[h], q_s[rows], jnp.zeros((), bf16))
            s = dot(q, k_s[:kv], NT)
            last = jnp.where(seen(), s[:, kv - RB :], -1e30)
            top = jnp.max(last, axis=-1, keepdims=True)
            if b:
                top = jnp.maximum(top, jnp.max(s[:, : kv - RB], axis=-1, keepdims=True))
            e_last = jnp.exp(last - top)
            norm = jnp.sum(e_last, axis=-1, keepdims=True)
            if b:
                e_rest = jnp.exp(s[:, : kv - RB] - top)
                norm = norm + jnp.sum(e_rest, axis=-1, keepdims=True)
            inv = 1.0 / norm
            probs[h, rows, kv - RB : kv] = (e_last * inv).astype(bf16)
            if b:
                probs[h, rows, : kv - RB] = (e_rest * inv).astype(bf16)
            halves.append(dot(probs[h, rows, :kv], v_s[:kv], NN))
        a = jnp.where(head[0], halves[0], halves[1])
        att[rows] = a
        att_low[rows] = jnp.where(mine, a, 0.0).astype(bf16)
        p = dot(att_low[rows], outwin[...], NN) + dot(hidden[rows], downw[...], NN)
        part[2 * b : 2 * b + 2] = p.astype(bf16).reshape(2, RB // 2, D)

    one = Collect(copies, part, yb.at[0], zb.at[0], sb.at[0], sems.at[0], branch_out, Z, z, y)
    for b in (0, 3, 1, 2):
        attend(b)
        one.push(b)
        if b == 3:
            for k in range(3, Z):
                grads.step(k)

    vec[...] = jnp.zeros_like(vec)

    def back(b):
        g = gall[pl.ds(2 * b, 2)].reshape(RB, D)
        gp = (dot(g, downw[...], NT) * slope[block(b)]).astype(bf16)
        gpre[block(b)] = gp
        gatt[block(b)] = dot(g, outwin[...], NT).astype(bf16)
        gs = dot(gp, wall[1].reshape(D, C), NT)
        n = normed[block(b)]
        vec[2:3] += jnp.sum(gs * n, axis=0, keepdims=True)
        vec[3:4] += jnp.sum(gs, axis=0, keepdims=True)
        vec[7:8] += jnp.sum(g.astype(f32), axis=0, keepdims=True)
        gsec[block(b)] = gs * gain_two
        sums = jnp.sum(gp.astype(f32), axis=0, keepdims=True)
        for i in range(C // 128):
            own_vec[1 + i : 2 + i] += sums[:, i * 128 : (i + 1) * 128]

    own_vec[...] = jnp.zeros_like(own_vec)
    for b in near:
        grads.got(2 * b + 1 - y)
        back(b)

    g_flat = gall[...].reshape(S, D)
    down_grad = dot(hidden[...], g_flat, TN).astype(bf16)
    q4 = C // 2
    for i in range(2):
        for j in range(2):
            g_own[i, j, half:] = down_grad[j * q4 : (j + 1) * q4, i * C : (i + 1) * C]
    gout_win[...] = dot(att_low[...], g_flat, TN).astype(bf16)
    for i in range(2):
        for j in range(2):
            g_own[i, j, :half] = gout_win[pl.ds(pl.multiple_of(off + j * half, 16), half), i * C : (i + 1) * C]
    for i in range(2):
        copies.send(g_own.at[i, 1 - c], co_buf.at[i], s_co.at[i], r_co.at[i], dp=cn)

    def matrix(m, left, right):
        g = dot(left[...], right[...], TN).astype(bf16).reshape(F, 2, half, C)
        for j in range(2):
            g_mat[m, j] = g[:, j].reshape(F * half, C)
        copies.send(g_mat.at[m, 1 - c], cbuf.at[m], s_c.at[m], r_c.at[m], dp=cn)

    def matrix_x(m):
        arrived(cbuf.at[m], r_c.at[m], dp=cn)
        add_rows(hbuf.at[m], [g_mat.at[m, c], cbuf.at[m]])
        copies.send(hbuf.at[m], xbuf.at[m], s_x.at[m], r_x.at[m], x != m, dp=xn)

    def matrix_spread(m):
        own = x == m

        @pl.when(own)
        def _():
            arrived(xbuf.at[m], r_x.at[m], dp=xn)
            add_rows(hbuf.at[m], [hbuf.at[m], xbuf.at[m]])
            here = pl.ds(pl.multiple_of(me * half, half), half)
            ret[m, c, here] = hbuf[m, here]

        for k, o in enumerate(others):
            there = pl.ds(pl.multiple_of(o * half, half), half)
            here = pl.ds(pl.multiple_of(me * half, half), half)
            copies.send(hbuf.at[m, there], ret.at[m, c, here], s_a.at[m, k], r_a.at[m, me], own, fsdp=o)

    def matrix_share(m):
        own = x == m
        for k, src in enumerate([me] + sources):
            piece = ret.at[m, c, pl.ds(pl.multiple_of(src * half, half), half)]
            if k == 0:

                @pl.when(jnp.logical_not(own))
                def _():
                    arrived(piece, r_a.at[m, src], dp=xn)
            else:
                arrived(piece, r_a.at[m, src], dp=xn)
            copies.send(piece, piece, s_cc.at[m, 0, k], r_a.at[m, src], own, dp=xn)
            copies.send(piece, piece, s_cc.at[m, 1, k], r_cc.at[m, src], dp=cn)

    matrix(1, second, gpre)
    one.step(0)
    for i in range(2):
        arrived(co_buf.at[i], r_co.at[i], dp=cn)
        add_rows(ho_buf.at[i], [g_own.at[i, c], co_buf.at[i]])
    copies.send(ho_buf.at[1 - x], xo_buf, s_xo, r_xo, dp=xn)
    matrix_x(1)

    def attend_back(b):
        kv = (b + 1) * RB
        rows = slice(b * RB, kv)
        ga, a = gatt[rows], att[rows]
        prod = ga.astype(f32) * a
        q_grad = None
        for h in range(2):
            delta = jnp.sum(jnp.where(head[h], prod, 0.0), axis=-1, keepdims=True)
            gah = jnp.where(head[h], ga, jnp.zeros((), bf16))
            qh = jnp.where(head[h], q_s[rows], jnp.zeros((), bf16))
            p = probs[h, rows, :kv]
            gp = dot(gah, v_s[:kv], NT)
            gs_f = p.astype(f32) * (gp - delta)
            last = jnp.where(seen(), gs_f[:, kv - RB :], 0.0).astype(bf16)
            gs = jnp.concatenate([gs_f[:, : kv - RB].astype(bf16), last], axis=1) if b else last
            dq = dot(gs, k_s[:kv], NN)
            q_grad = dq if h == 0 else jnp.where(head[0], q_grad, dq)
            gk[:kv] += dot(gs, qh, TN)
            gv[:kv] += dot(p, gah, TN)
        gq[rows] = q_grad

    def back_project(b):
        ct, s1, s2 = tabs[0, block(b)], tabs[1, block(b)], tabs[2, block(b)]
        dq = turn(gq[block(b)] * 0.125, ct, -s1, -s2)
        dk = turn(gk[block(b)], ct, -s1, -s2)
        for i, t in enumerate((dq, dk, gv[block(b)])):
            low = jnp.where(mine, t, 0.0).astype(bf16)
            gproj[block(b), i * 128 : (i + 1) * 128] = low
            own_vec[8 + i : 9 + i] += jnp.sum(low.astype(f32), axis=0, keepdims=True)
        gf = dot(gproj[block(b)], wall[0].reshape(D, C), NT)
        n = normed[block(b)]
        vec[0:1] += jnp.sum(gf * n, axis=0, keepdims=True)
        vec[1:2] += jnp.sum(gf, axis=0, keepdims=True)
        mixed[pl.ds(2 * b, 2)] = (gf * gain_one + gsec[block(b)]).astype(bf16).reshape(2, RB // 2, D)

    gk[...] = jnp.zeros_like(gk)
    gv[...] = jnp.zeros_like(gv)
    two = Collect(copies, mixed, yb.at[1], zb.at[1], sb.at[1], sems.at[1], mixed_out, Z, z, y)
    attend_back(3)
    back_project(3)
    two.push(3)
    one.step(3)
    attend_back(2)
    back_project(2)
    two.push(2)
    one.step(1)
    arrived(xo_buf, r_xo, dp=xn)
    owner = ret_own.at[x, c]
    add_rows(owner, [ho_buf.at[x], xo_buf])
    copies.send(owner, owner, s_fo.at[0], r_fo.at[0], dp=xn)
    copies.send(owner, owner, s_fo.at[1], r_fo.at[1], dp=cn)
    matrix_spread(1)
    attend_back(1)
    back_project(1)
    two.push(1)
    one.step(2)
    attend_back(0)
    back_project(0)
    two.push(0)
    matrix(0, first, gproj)
    two.step(3)
    two.step(2)
    matrix_x(0)
    two.step(1)
    two.step(0)
    matrix_share(1)

    vec[4:7] = exact(own_vec[8:16], window, NT)[0:3]
    pieces = [exact(vec[...], place_matrix(W, b * W, D), NT) for b in range(F)]
    for b in range(F):
        vecs[b, 0:4] = pieces[b][0:4]
        for j in range(3):
            m = 3 * b + j
            vecs[b, 4 + j : 5 + j] = pieces[m % F][4 + m // F : 5 + m // F]
        vecs[b, 7:8] = jnp.zeros((1, 128), f32)
    own_vec[0:1] = exact(vec[...], place_matrix(W, me * W, D), NT)[7:8]
    vbuf[me] = vecs[me]
    for k, o in enumerate(others):
        copies.send(vecs.at[o], vbuf.at[me], s_v.at[k], r_v.at[me], fsdp=o)
    matrix_spread(0)
    for src in sources:
        arrived(vbuf.at[src], r_v.at[src], dp=xn)
    total = vbuf[0]
    for g in range(1, F):
        total = total + vbuf[g]
    vtot[d, :8] = total
    vtot[d, 8:] = own_vec[0:8]
    for k, to in enumerate((xn, cn, dn)):
        copies.send(vtot.at[d], vtot.at[d], s_d.at[k], r_d.at[d], dp=to)
    one.finish()
    matrix_share(0)
    arrived(ret_own.at[1 - x, c], r_fo.at[0], dp=xn)
    copies.send(ret_own.at[1 - x, c], ret_own.at[1 - x, c], s_fo.at[2], r_fo.at[2], dp=cn)
    two.finish()
    for to in (xn, cn, dn):
        arrived(vtot.at[to], r_d.at[to], dp=to)
    vec_sum[...] = vtot[0] + vtot[1] + vtot[2] + vtot[3]
    arrived(ret_own.at[x, 1 - c], r_fo.at[1], dp=cn)
    arrived(ret_own.at[1 - x, 1 - c], r_fo.at[2], dp=cn)
    for m in range(2):
        for g in range(F):
            arrived(ret.at[m, 1 - c, pl.ds(g * half, half)], r_cc.at[m, g], dp=cn)
    copies.drain()


def layer(F, tok, cot, qkv, up, outw, downw, *vectors):
    rows, D = tok.shape
    W, FF = up.shape
    C = FF // F
    S, Z, half = rows * F, F // 2, W // 2
    own = (W + C) // 2
    dma = pltpu.SemaphoreType.DMA
    low = lambda *s: pltpu.VMEM(s, bf16)
    wide = lambda *s: pltpu.VMEM(s, f32)
    return pl.pallas_call(
        functools.partial(layer_kernel, F),
        out_shape=(
            jax.ShapeDtypeStruct((rows, D), f32),
            jax.ShapeDtypeStruct((rows, D), f32),
            jax.ShapeDtypeStruct((2, 2, F * half, C), bf16),
            jax.ShapeDtypeStruct((2, 2, own, C), bf16),
            jax.ShapeDtypeStruct((16, 128), f32),
            jax.ShapeDtypeStruct((16, D), f32),
        ),
        in_specs=[pl.BlockSpec(memory_space=pl.ANY)] * 6 + [vmem()] * 8,
        out_specs=(vmem(),) * 6,
        scratch_shapes=[
            low(F, rows, D), low(F, rows, D), wide(F, 16, 128), low(2, F, W, C), low(128, D), low(2, F, W, C),
            wide(F, 16, 128),
            wide(3, S, 128), wide(S, D), low(S, D), low(S, D), low(S, 128), low(S, 128), low(S, 128), low(2, S, S),
            wide(S, 128), low(S, 128), low(S, C), wide(S, C), low(F, rows, D), low(S, C), low(S, 128), wide(S, D),
            low(F, rows, D),
            low(S, 3 * 128), wide(S, 128), wide(S, 128), wide(S, 128), low(128, D), low(2, 2, F * half, C),
            low(2, 2, own, C), wide(8, D), wide(F, 8, 128), wide(16, 128),
            low(W, 3 * D), low(W, FF), low(W, D), low(C, D), wide(16, 128),
            low(2, Z, rows, D), low(2, Z, rows, D), low(2, Z, rows, D),
            low(2, F * half, C), low(2, F * half, C), low(2, F * half, C),
            low(2, own, C), low(2, own, C), low(own, C), wide(F, 8, 128), wide(4, 16, 128),
            dma((3, F)), dma((F,)), dma((3, F)), dma((F,)), dma((F,)), dma((F,)), dma((4, F)), dma((4, F)), dma, dma,
            dma((2, 4, Z)),
            dma((2,)), dma((2,)), dma((2,)), dma((2,)), dma((2, F)), dma((2, F)), dma((2, 2, F)), dma((2, F)),
            dma((2,)), dma((2,)), dma, dma, dma((3,)), dma((3,)), dma((F,)), dma((F,)), dma((3,)), dma((4,)),
            dma((6,)),
        ],
        compiler_params=pltpu.CompilerParams(
            collective_id=0, has_side_effects=True, vmem_limit_bytes=60 * 2**20
        ),
        name="layer",
    )(tok, cot, qkv, up, outw, downw, *vectors)


def finish_kernel(
    F, tok_in, cot_in, branch_in, mixed_in, ret_in, own_in, full, vec_sum, out, igrad, g_qkv, g_out, g_up, g_down,
    o0, o1, o2, o3, o_qkv, o_out, o_up, o_down, ret_own, ret, tok, cot, branch, mixed, sem,
):
    fetches = [
        pltpu.make_async_copy(src, dst, sem.at[i])
        for i, (src, dst) in enumerate(
            (
                (own_in, ret_own), (ret_in, ret), (tok_in, tok), (cot_in, cot), (branch_in, branch), (mixed_in, mixed)
            )
        )
    ]
    for fetch in fetches:
        fetch.start()
    W, D = g_out.shape
    C = ret.shape[3]
    for i, o in enumerate((o0, o1, o2, o3)):
        o[...] = vec_sum[i : i + 1, :W].reshape(W)
    o_qkv[...] = jnp.concatenate([vec_sum[4 + i : 5 + i, :W] for i in range(3)], axis=1).reshape(3 * W)
    o_out[...] = vec_sum[8:9, :W].reshape(W)
    o_down[...] = vec_sum[8:9, :W].reshape(W)
    o_up[...] = jnp.concatenate([vec_sum[9 + i : 10 + i] for i in range(C // 128)], axis=1).reshape(C)
    for fetch in fetches:
        fetch.wait()
    half = W // 2
    x = tok[...].astype(f32)
    center = x - jnp.mean(x, axis=-1, keepdims=True)
    inverse = lax.rsqrt(jnp.mean(center * center, axis=-1, keepdims=True) + epsilon)
    n = center * inverse
    out[...] = (x + branch[...] + full[4:5] + full[5:6]).astype(bf16)
    m = mixed[...]
    m = m - jnp.mean(m, axis=-1, keepdims=True) - n * jnp.mean(m * n, axis=-1, keepdims=True)
    igrad[...] = cot[...].astype(f32) + inverse * m
    row = lax.broadcasted_iota(jnp.int32, (128, D), 0)
    col = lax.broadcasted_iota(jnp.int32, (128, D), 1)
    for j in range(2):
        rows = slice(j * half, (j + 1) * half)
        for i in range(2):
            columns = slice(i * C, (i + 1) * C)
            g_out[rows, columns] = ret_own[i, j, :half].astype(f32)
            g_down[j * (C // 2) : (j + 1) * (C // 2), columns] = ret_own[i, j, half:].astype(f32)
        for g in range(F):
            g_up[rows, g * C : (g + 1) * C] = ret[1, j, g * half : (g + 1) * half].astype(f32)
    for i in range(3):
        total = jnp.zeros((W, D), f32)
        for g in range(F):
            s = g * W // HEAD * HEAD
            place = ((row + s == col) & (col >= g * W) & (col < (g + 1) * W)).astype(bf16)
            piece = jnp.concatenate(
                [ret[0, j, g * half : (g + 1) * half, i * 128 : (i + 1) * 128] for j in range(2)], axis=0
            )
            total = total + dot(piece, place, NN)
        g_qkv[:, i * D : (i + 1) * D] = total


def finish(F, tok, cot, branch, mixed, ret, ret_own, full, vec_sum):
    rows, D = tok.shape
    W = D // F
    C = ret.shape[3]
    return pl.pallas_call(
        functools.partial(finish_kernel, F),
        out_shape=(
            jax.ShapeDtypeStruct((rows, D), bf16),
            jax.ShapeDtypeStruct((rows, D), f32),
            jax.ShapeDtypeStruct((W, 3 * D), f32),
            jax.ShapeDtypeStruct((W, D), f32),
            jax.ShapeDtypeStruct((W, F * C), f32),
            jax.ShapeDtypeStruct((C, D), f32),
        )
        + tuple(jax.ShapeDtypeStruct((n,), f32) for n in (W, W, W, W, 3 * W, W, C, W)),
        in_specs=[pl.BlockSpec(memory_space=pl.ANY)] * 6 + [vmem()] * 2,
        out_specs=(vmem(),) * 14,
        scratch_shapes=[
            pltpu.VMEM(a.shape, a.dtype) for a in (ret_own, ret, tok, cot, branch, mixed)
        ]
        + [pltpu.SemaphoreType.DMA((6,))],
        compiler_params=pltpu.CompilerParams(vmem_limit_bytes=60 * 2**20),
        name="finish",
    )(tok, cot, branch, mixed, ret, ret_own, full, vec_sum)


def fast_body(
    tokens, ln1_gain, ln1_bias, ln2_gain, ln2_bias, qkv_weight, qkv_bias, out_weight, out_bias, up_weight, up_bias,
    down_weight, down_bias, cotangent,
):
    F = lax.axis_size("fsdp")
    branch, mixed, ret, ret_own, vec_sum, full = layer(
        F, tokens[0], cotangent[0], qkv_weight, up_weight, out_weight, down_weight,
        ln1_gain, ln1_bias, ln2_gain, ln2_bias, out_bias, down_bias, qkv_bias, up_bias,
    )
    out, igrad, g_qkv, g_out, g_up, g_down, o0, o1, o2, o3, o_qkv, o_out, o_up, o_down = finish(
        F, tokens[0], cotangent[0], branch, mixed, ret, ret_own, full, vec_sum
    )
    return (
        out[None], igrad[None], o0, o1, o2, o3, g_qkv, o_qkv, g_out, o_out, g_up, o_up, g_down, o_down
    )


def solution(mesh):
    row = P("fsdp", None)
    vec = P("fsdp")
    act = P("dp", "fsdp", None)
    fast = mesh.shape["fsdp"] == 8 and mesh.shape["dp"] == 4
    return jax.shard_map(
        fast_body if fast else body,
        mesh=mesh,
        in_specs=(act, vec, vec, vec, vec, row, vec, row, vec, row, vec, row, vec, act),
        out_specs=(act, act, vec, vec, vec, vec, row, vec, row, vec, row, vec, row, vec),
        check_vma=False,
    )
```

```python
import functools
import math

import jax
import jax.numpy as jnp
from jax import lax
from jax.experimental import pallas as pl
from jax.experimental.pallas import tpu as pltpu
from jax.sharding import PartitionSpec as P

HEADS = 12
HEAD = 64
ROT = 16

epsilon = 1e-05
inv_root_two = 1.0 / math.sqrt(2.0)
inv_root_twopi = 1.0 / math.sqrt(2.0 * math.pi)
bf16 = jnp.bfloat16
f32 = jnp.float32


def rotary(tensor, cosine, sine, direction):
    half = ROT // 2
    first = tensor[..., :half]
    second = tensor[..., half:ROT]
    return jnp.concatenate(
        [
            first * cosine - direction * second * sine,
            second * cosine + direction * first * sine,
            tensor[..., ROT:],
        ],
        axis=-1,
    )


def dot(a, b, dims):
    return lax.dot_general(a, b, ((dims[0], dims[1]), ((), ())), preferred_element_type=f32)


NN = ((1,), (0,))
NT = ((1,), (1,))
TN = ((0,), (0,))


def gather_rows(arrays):
    return [lax.all_gather(a, "fsdp", axis=0, tiled=True) for a in arrays]


def scatter_rows(a):
    F = lax.axis_size("fsdp")
    got = lax.all_to_all(a, "fsdp", 0, 0, tiled=True)
    return jnp.sum(got.reshape((F, a.shape[0] // F) + a.shape[1:]).astype(f32), axis=0)


def spread_weights(blocks):
    return lax.all_to_all(blocks, "fsdp", 0, 0, tiled=True)


def return_grads(blocks, own):
    n = lax.axis_size("dp")
    F, W, C = blocks.shape
    R, D = own.shape
    parts = jnp.swapaxes(blocks.reshape(F, n, W // n, C), 0, 1).reshape(n, F * (W // n), C)
    own_parts = own.reshape(n, R // n, D)
    if C == D:
        both = jnp.concatenate([parts, own_parts], axis=1)
        both = jnp.sum(lax.all_to_all(both, "dp", 0, 0, tiled=True).astype(f32), axis=0)
        part, own_part = both[: F * (W // n)].astype(bf16), both[F * (W // n) :].astype(bf16)
    else:
        part = jnp.sum(lax.all_to_all(parts, "dp", 0, 0, tiled=True).astype(f32), axis=0)
        own_part = jnp.sum(lax.all_to_all(own_parts, "dp", 0, 0, tiled=True).astype(f32), axis=0)
        part, own_part = part.astype(bf16), own_part.astype(bf16)
    part = lax.all_to_all(part, "fsdp", 0, 0, tiled=True)
    if C == D:
        whole = lax.all_gather(jnp.concatenate([part, own_part], axis=0), "dp", axis=0)
        part_all, own_all = whole[:, : F * (W // n)], whole[:, F * (W // n) :]
    else:
        part_all = lax.all_gather(part, "dp", axis=0)
        own_all = lax.all_gather(own_part, "dp", axis=0)
    part_all = jnp.swapaxes(part_all.reshape(n, F, W // n, C), 0, 1).reshape(F, W, C)
    return part_all, own_all.reshape(R, D)


def body(
    tokens,
    ln1_gain,
    ln1_bias,
    ln2_gain,
    ln2_bias,
    qkv_weight,
    qkv_bias,
    out_weight,
    out_bias,
    up_weight,
    up_bias,
    down_weight,
    down_bias,
    cotangent,
):
    rank = lax.axis_index("fsdp")
    F = lax.axis_size("fsdp")
    rows, D = tokens.shape[1:]
    W = D // F
    FFW = down_weight.shape[0]
    NH = max(-(-((g * W) % HEAD + W) // HEAD) for g in range(F))
    WIN = NH * HEAD
    starts = [min(g * W // HEAD, HEADS - NH) * HEAD for g in range(F)]
    start = jnp.minimum(rank * W // HEAD, HEADS - NH) * HEAD
    off = rank * W - start
    S = rows * F

    qkv3 = qkv_weight.reshape(W, 3, D)
    blocks = jnp.stack(
        [
            jnp.concatenate(
                [
                    qkv3[:, 0, s : s + WIN],
                    qkv3[:, 1, s : s + WIN],
                    qkv3[:, 2, s : s + WIN],
                    up_weight[:, g * FFW : (g + 1) * FFW],
                ],
                axis=1,
            )
            for g, s in enumerate(starts)
        ]
    )
    smalls = jnp.concatenate(
        [ln1_gain, ln1_bias, ln2_gain, ln2_bias, out_bias, down_bias, qkv_bias]
    )
    extra = -(-smalls.shape[0] // (16 * D)) * 16
    smalls = jnp.concatenate([smalls, jnp.zeros(extra * D - smalls.shape[0], bf16)])
    (both_all,) = gather_rows([jnp.concatenate([tokens[0], smalls.reshape(extra, D)], axis=0)])
    both_all = both_all.reshape(F, rows + extra, D)
    x_low = both_all[:, :rows].reshape(S, D)
    small_all = both_all[:, rows:].reshape(F, extra * D)
    wall = spread_weights(blocks).reshape(D, 3 * WIN + FFW)
    w_qkv = wall[:, : 3 * WIN]
    w_up = wall[:, 3 * WIN :]
    up_ring = [(i, (i + 1) % F) for i in range(F)]
    down_ring = [(i, (i - 1) % F) for i in range(F)]
    out_prev = lax.ppermute(out_weight, "fsdp", up_ring)
    out_next = lax.ppermute(out_weight, "fsdp", down_ring)
    (grad_out,) = gather_rows([cotangent[0]])
    out_three = jnp.concatenate(
        [out_prev, out_weight, out_next, jnp.zeros((WIN, D), bf16)], axis=0
    )
    w_out_win = lax.dynamic_slice_in_dim(out_three, W - off, WIN, 0)
    win_col = jnp.arange(WIN, dtype=jnp.int32)
    mine = (win_col >= off) & (win_col < off + W)
    small_all = small_all.astype(f32)
    gain_one, bias_one, gain_two, bias_two, b_out, b_down = [
        small_all[:, i * W : (i + 1) * W].reshape(D) for i in range(6)
    ]
    b_qkv = small_all[:, 6 * W : 9 * W].reshape(3, D)
    b_qkv = lax.dynamic_slice_in_dim(b_qkv, start, WIN, 1).reshape(3 * WIN)
    b_up = up_bias.astype(f32)

    x = x_low.astype(f32)
    center = x - jnp.mean(x, axis=-1, keepdims=True)
    inverse = lax.rsqrt(jnp.mean(center * center, axis=-1, keepdims=True) + epsilon)
    normed = center * inverse
    first_low = (normed * gain_one + bias_one).astype(bf16)
    second_low = (normed * gain_two + bias_two).astype(bf16)

    places = jnp.arange(S, dtype=f32)
    half = ROT // 2
    freq = 10000.0 ** (-(jnp.arange(half, dtype=f32) * 2.0) / ROT)
    angle = places[:, None] * freq[None, :]
    cosine = jnp.cos(angle)[:, None, :]
    sine = jnp.sin(angle)[:, None, :]

    proj = dot(first_low, w_qkv, NN) + b_qkv
    queries = (rotary(proj[:, :WIN].reshape(S, NH, HEAD), cosine, sine, 1.0) * 0.125).astype(bf16)
    keys = rotary(proj[:, WIN : 2 * WIN].reshape(S, NH, HEAD), cosine, sine, 1.0).astype(bf16)
    vals = proj[:, 2 * WIN :].astype(bf16).reshape(S, NH, HEAD)
    q_place = jnp.arange(S, dtype=jnp.int32)
    visible = (q_place[None, :] <= q_place[:, None])[None]
    scores = jnp.einsum("qhd,khd->hqk", queries, keys, preferred_element_type=f32)
    masked = jnp.where(visible, scores, -1e30)
    top = jnp.max(masked, axis=-1, keepdims=True)
    lse = top + jnp.log(jnp.sum(jnp.exp(masked - top), axis=-1, keepdims=True))
    probs = jnp.exp(masked - lse)
    probs_low = probs.astype(bf16)
    attended = jnp.einsum("hqk,khd->qhd", probs_low, vals, preferred_element_type=f32)
    att_low = jnp.where(mine, attended.reshape(S, WIN), 0.0).astype(bf16)

    hidden_pre = dot(second_low, w_up, NN) + b_up
    cdf = 0.5 * (1.0 + lax.erf(hidden_pre * inv_root_two))
    hidden_low = (hidden_pre * cdf).astype(bf16)
    part = dot(att_low, w_out_win, NN) + dot(hidden_low, down_weight, NN)
    branch = scatter_rows(part.astype(bf16))

    grad_hidden = dot(grad_out, down_weight, NT)
    slope = cdf + hidden_pre * jnp.exp(-0.5 * hidden_pre * hidden_pre) * inv_root_twopi
    grad_pre = (grad_hidden * slope).astype(bf16)
    grad_w_down = dot(hidden_low, grad_out, TN)
    grad_w_out_win = dot(att_low, grad_out, TN)
    grad_w_out = lax.dynamic_slice_in_dim(grad_w_out_win, off, W, 0)
    bias_total = jnp.sum(grad_out.astype(f32), axis=0)
    grad_b_up = jnp.sum(grad_pre.astype(f32), axis=0)
    grad_att = dot(grad_out, w_out_win, NT).astype(bf16).reshape(S, NH, HEAD)
    delta = jnp.transpose(jnp.sum(grad_att.astype(f32) * attended, axis=-1))[:, :, None]
    grad_probs = jnp.einsum("qhd,khd->hqk", grad_att, vals, preferred_element_type=f32)
    grad_scores = (probs * (grad_probs - delta)).astype(bf16)
    grad_q = jnp.einsum("hqk,khd->qhd", grad_scores, keys, preferred_element_type=f32)
    grad_k = jnp.einsum("hqk,qhd->khd", grad_scores, queries, preferred_element_type=f32)
    grad_v = jnp.einsum("hqk,qhd->khd", probs_low, grad_att, preferred_element_type=f32)
    grad_proj = jnp.stack(
        [
            rotary(grad_q * 0.125, cosine, sine, -1.0).reshape(S, WIN),
            rotary(grad_k, cosine, sine, -1.0).reshape(S, WIN),
            grad_v.reshape(S, WIN),
        ],
        axis=1,
    )
    grad_proj = jnp.where(mine, grad_proj, 0.0).astype(bf16).reshape(S, 3 * WIN)
    grad_w_qkv = dot(first_low, grad_proj, TN)
    grad_w_up = dot(second_low, grad_pre, TN)
    grad_b_qkv = jnp.sum(grad_proj.astype(f32), axis=0).reshape(3, WIN)
    grad_first = dot(grad_proj, w_qkv, NT)
    grad_second = dot(grad_pre, w_up, NT)
    vectors = [
        jnp.sum(grad_first * normed, axis=0),
        jnp.sum(grad_first, axis=0),
        jnp.sum(grad_second * normed, axis=0),
        jnp.sum(grad_second, axis=0),
    ]
    mixed = grad_first * gain_one + grad_second * gain_two
    b_full = lax.dynamic_update_slice_in_dim(jnp.zeros((3, D), f32), grad_b_qkv, start, 1)
    small_part = jnp.concatenate(
        [v.reshape(F, W) for v in vectors] + [b_full.reshape(F, 3 * W)], axis=1
    )
    mixed_mine = scatter_rows(mixed.astype(bf16))
    small_mine = scatter_rows(small_part)[0]
    own_small = jnp.concatenate(
        [small_mine, lax.dynamic_slice_in_dim(bias_total, rank * W, W, 0), grad_b_up]
    )
    pad = 8 * lax.axis_size("dp")
    own_rows = -(-(W + FFW + -(-own_small.shape[0] // D)) // pad) * pad
    n_small = own_rows - W - FFW
    own_small = jnp.concatenate([own_small, jnp.zeros(n_small * D - own_small.shape[0], f32)])

    grad_blocks = jnp.concatenate([grad_w_qkv, grad_w_up], axis=1).astype(bf16)
    grad_blocks = grad_blocks.reshape(F, W, 3 * WIN + FFW)
    own = jnp.concatenate(
        [grad_w_out, grad_w_down, own_small.reshape(n_small, D)], axis=0
    ).astype(bf16)
    returned, own = return_grads(grad_blocks, own)
    returned = returned.astype(f32)
    own = own.astype(f32)
    own_small = own[W + FFW :].reshape(n_small * D)
    pieces = [
        [returned[g, :, i * WIN + g * W - s : i * WIN + g * W - s + W] for g, s in enumerate(starts)]
        for i in range(3)
    ]
    out_w_qkv = jnp.concatenate(pieces[0] + pieces[1] + pieces[2], axis=1)
    out_w_up = jnp.concatenate([returned[g, :, 3 * WIN :] for g in range(F)], axis=1)

    here = rank * rows
    x_own = tokens[0].astype(f32)
    c_own = x_own - jnp.mean(x_own, axis=-1, keepdims=True)
    i_own = lax.rsqrt(jnp.mean(c_own * c_own, axis=-1, keepdims=True) + epsilon)
    n_own = c_own * i_own
    layer_output = (x_own + branch + b_out + b_down).astype(bf16)
    input_grad = cotangent[0].astype(f32) + i_own * (
        mixed_mine
        - jnp.mean(mixed_mine, axis=-1, keepdims=True)
        - n_own * jnp.mean(mixed_mine * n_own, axis=-1, keepdims=True)
    )
    g = [own_small[i * W : (i + 1) * W] for i in range(4)]
    bias_mine = own_small[7 * W : 8 * W]
    return (
        layer_output[None],
        input_grad[None],
        g[0],
        g[1],
        g[2],
        g[3],
        out_w_qkv,
        own_small[4 * W : 7 * W],
        own[:W],
        bias_mine,
        out_w_up,
        own_small[8 * W : 8 * W + FFW],
        own[W : W + FFW],
        bias_mine,
    )


class Copies:
    def __init__(self):
        self.later = []

    def send(self, src, dst, send_sem, recv_sem, when=None, **to):
        copy = pltpu.make_async_remote_copy(
            src_ref=src,
            dst_ref=dst,
            send_sem=send_sem,
            recv_sem=recv_sem,
            device_id=to,
            device_id_type=pl.DeviceIdType.MESH,
        )
        if when is None:
            copy.start()
        else:
            pl.when(when)(copy.start)
        self.later.append((copy, when))

    def drain(self):
        for copy, when in self.later:
            if when is None:
                copy.wait_send()
            else:
                pl.when(when)(copy.wait_send)
        self.later = []


def arrived(dst, recv_sem, **to):
    pltpu.make_async_remote_copy(
        src_ref=dst,
        dst_ref=dst,
        send_sem=recv_sem,
        recv_sem=recv_sem,
        device_id=to,
        device_id_type=pl.DeviceIdType.MESH,
    ).wait_recv()


def meet(peers):
    barrier = pltpu.get_barrier_semaphore()
    for to in peers:
        pl.semaphore_signal(barrier, inc=1, device_id=to, device_id_type=pl.DeviceIdType.MESH)
    pl.semaphore_wait(barrier, len(peers))


class Spread:
    def __init__(self, copies, buf, send_sem, recv_sem, Z, z, y):
        self.copies, self.buf, self.ss, self.rs = copies, buf, send_sem, recv_sem
        self.Z, self.z, self.y = Z, z, y

    def push(self, src, way, when=None):
        to = {0: src * 0 + (self.z * 2 + self.y + 2), 1: self.z * 2 + self.y - 2, 2: self.z * 2 + 1 - self.y}[way]
        self.copies.send(
            self.buf.at[src], self.buf.at[src], self.ss.at[way, src], self.rs.at[src], when, fsdp=to
        )

    def first(self):
        me = self.z * 2 + self.y
        self.push(me, 0, self.z + 1 < self.Z)
        self.push(me, 1, self.z > 0)
        self.push(me, 2)

    def got(self, src, when=None):
        def wait():
            arrived(self.buf.at[src], self.rs.at[src], fsdp=self.z * 2 + 1 - self.y)

        if when is None:
            wait()
        else:
            pl.when(when)(wait)

    def step(self, k):
        z, y = self.z, self.y
        low, high = jnp.maximum(z - k, 0) * 2 + y, jnp.minimum(z + k, self.Z - 1) * 2 + y
        has_low, has_high = z - k >= 0, z + k < self.Z
        self.got(low, has_low)
        self.push(low, 0, has_low & (z + 1 < self.Z))
        self.push(low, 2, has_low)
        self.got(high, has_high)
        self.push(high, 1, has_high & (z > 0))
        self.push(high, 2, has_high)

    def finish(self):
        for k in range(self.Z):
            self.got(k * 2 + 1 - self.y)


def vmem():
    return pl.BlockSpec(memory_space=pltpu.VMEM)


def add_rows(out, parts):
    step = 16
    for r in range(0, out.shape[0], step):
        total = parts[0][r : r + step].astype(f32)
        for p in parts[1:]:
            total = total + p[r : r + step].astype(f32)
        out[r : r + step] = total.astype(out.dtype)


class Collect:
    def __init__(self, copies, part, yb, zb, sb, sems, out, Z, z, y):
        self.__dict__.update(copies=copies, part=part, yb=yb, zb=zb, sb=sb, out=out, Z=Z, z=z, y=y)
        self.sy, self.ry, self.sz, self.rz = [sems.at[i] for i in range(4)]
        zb[z] = jnp.zeros(zb.shape[1:], zb.dtype)

    def push(self, t):
        self.copies.send(
            self.part.at[t * 2 + 1 - self.y], self.yb.at[t], self.sy.at[t], self.ry.at[t],
            fsdp=self.z * 2 + 1 - self.y,
        )

    def step(self, t):
        z, y = self.z, self.y
        away = t != z

        @pl.when(away)
        def _():
            arrived(self.yb.at[t], self.ry.at[t], fsdp=z * 2 + 1 - y)
            add_rows(self.sb.at[t], [self.part.at[t * 2 + y], self.yb.at[t]])

        self.copies.send(self.sb.at[t], self.zb.at[z], self.sz.at[t], self.rz.at[z], away, fsdp=t * 2 + y)

    def finish(self):
        z, y, Z = self.z, self.y, self.Z
        to = z * 2 + 1 - y
        arrived(self.yb.at[z], self.ry.at[z], fsdp=to)
        for k in range(1, Z):
            src = lax.rem(z + k, Z)
            arrived(self.zb.at[src], self.rz.at[src], fsdp=to)
        add_rows(self.out, [self.part.at[z * 2 + y], self.yb.at[z]] + [self.zb.at[k] for k in range(Z)])


def ln_rows(xall, normed, scale, b):
    x = xall[pl.ds(2 * b, 2)].reshape(RB, xall.shape[2]).astype(f32)
    center = x - jnp.mean(x, axis=-1, keepdims=True)
    inverse = lax.rsqrt(jnp.mean(center * center, axis=-1, keepdims=True) + epsilon)
    normed[block(b)] = center * inverse


RB = 256


def block(b):
    return pl.ds(pl.multiple_of(b * RB, RB), RB)


def turn(t, cosine, low_sine, high_sine):
    return t * cosine + pltpu.roll(t, 120, 1) * low_sine + pltpu.roll(t, 8, 1) * high_sine


def place_matrix(W, at, D):
    row = lax.broadcasted_iota(jnp.int32, (128, D), 0)
    col = lax.broadcasted_iota(jnp.int32, (128, D), 1)
    return ((col - at == row) & (row < W)).astype(f32)


def exact(a, b, dims):
    return lax.dot_general(
        a, b, ((dims[0], dims[1]), ((), ())), preferred_element_type=f32, precision=lax.Precision.HIGHEST
    )


def layer_kernel(
    F,
    tok, cot, qkv_in, up_in, outw_in, downw_in, v0, v1, v2, v3, v4, v5, qkv_bias, b_up,
    branch_out, mixed_out, ret, ret_own, vec_sum, full,
    xall, gall, sall, wall, outwin, wblk, placed,
    tabs, normed, first, second, q_s, k_s, v_s, probs, att, att_low, hidden, slope, part, gpre, gatt, gsec, mixed,
    gproj, gq, gk, gv, gout_win, g_mat, g_own, vec, vecs, own_vec,
    qkv, up, outw, downw, small, yb, zb, sb, cbuf, hbuf, xbuf, co_buf, ho_buf, xo_buf, vbuf, vtot,
    sx, rx, sg, rg, s_small, r_small, s_w, r_w, s_o, r_o, sems,
    s_c, r_c, s_x, r_x, s_a, r_a, s_cc, r_cc, s_co, r_co, s_xo, r_xo, s_fo, r_fo, s_v, r_v, s_d, r_d, s_in,
):
    me, d = lax.axis_index("fsdp"), lax.axis_index("dp")
    Z, z, y, x, c = F // 2, me // 2, me % 2, d // 2, d % 2
    W, D = outw.shape
    C = wall.shape[3]
    S = normed.shape[0]
    NB = S // RB
    half = W // 2
    others = [lax.rem(me + k, F) for k in range(1, F)]
    sources = [lax.rem(me + F - k, F) for k in range(1, F)]
    xn, cn, dn = d + 2 - 4 * x, d + 1 - 2 * c, (1 - x) * 2 + 1 - c
    fetches = [
        pltpu.make_async_copy(src, dst, s_in.at[i])
        for i, (src, dst) in enumerate(
            (
                (tok, xall.at[me]), (qkv_in, qkv), (up_in, up), (outw_in, outw), (cot, gall.at[me]), (downw_in, downw)
            )
        )
    ]
    for fetch in fetches:
        fetch.start()
    small[...] = jnp.zeros_like(small)
    for i, v in enumerate((v0, v1, v2, v3, v4, v5)):
        small[i : i + 1, :W] = v[...].astype(f32).reshape(1, W)
    shifts = qkv_bias[...].astype(f32).reshape(1, 3 * W)
    for i in range(3):
        small[6 + i : 7 + i, :W] = shifts[:, i * W : (i + 1) * W]
    meet([{"fsdp": o} for o in others] + [{"dp": xn}, {"dp": cn}, {"dp": dn}])
    copies = Copies()

    fetches[0].wait()
    tokens = Spread(copies, xall, sx, rx, Z, z, y)
    tokens.first()
    sall[me] = small[...]
    for k, o in enumerate(others):
        copies.send(small, sall.at[me], s_small.at[k], r_small.at[me], fsdp=o)
    for fetch in fetches[1:4]:
        fetch.wait()
    row = lax.broadcasted_iota(jnp.int32, (256, 128), 0)
    col = lax.broadcasted_iota(jnp.int32, (256, 128), 1)
    shift = (row == col + HEAD).astype(bf16)
    for g in range(F):
        s = g * W // HEAD * HEAD
        for i in range(3):
            at = i * D + s
            if s % 128 == 0:
                piece = qkv[:, at : at + 128]
            else:
                piece = dot(qkv[:, at - 64 : at + 192], shift, NN).astype(bf16)
            wblk[0, g, :, i * 128 : (i + 1) * 128] = piece
        wblk[1, g] = up[:, g * C : (g + 1) * C]
    mine_rows = pl.ds(pl.multiple_of(c * half, half), half)
    for k, o in enumerate(others):
        copies.send(wblk.at[x, o, mine_rows], wall.at[x, me, mine_rows], s_w.at[0, k], r_w.at[0, me], fsdp=o)
    wall[:, me] = wblk[:, me]
    outwin[pl.ds(pl.multiple_of(32 * y, 32), W), :] = outw[...]
    copies.send(
        outw.at[pl.ds(pl.multiple_of((W - 32) * (1 - y), 32), 32)],
        outwin.at[pl.ds(pl.multiple_of(W * y, 32), 32)],
        s_o, r_o, fsdp=z * 2 + 1 - y,
    )
    for fetch in fetches[4:]:
        fetch.wait()
    grads = Spread(copies, gall, sg, rg, Z, z, y)

    near = []
    for j in range(Z):
        at = jnp.int32(0)
        for i in range(Z):
            ranked = sorted(range(Z), key=lambda t: abs(t - i))
            at = jnp.where(z == i, ranked[j], at)
        near.append(at)
    tokens.step(1)
    tokens.step(2)
    for k, src in enumerate(sources):
        piece = wall.at[x, src, mine_rows]
        arrived(piece, r_w.at[0, src], dp=xn)
        copies.send(piece, piece, s_w.at[1, k], r_w.at[1, src], dp=xn)
        copies.send(piece, piece, s_w.at[2, k], r_w.at[2, src], dp=cn)
    grads.first()
    for k in range(3, Z):
        tokens.step(k)

    lane = lax.broadcasted_iota(jnp.int32, (RB, 128), 1)
    part_lane = lane % HEAD
    exponent = (part_lane[0:1] % (ROT // 2)).astype(f32) * (-2.0 * math.log(10000.0) / ROT)
    freq = jnp.exp(exponent)

    def tables(b, _):
        place = (lax.broadcasted_iota(jnp.int32, (RB, 128), 0) + b * RB).astype(f32)
        angle = place * freq
        sine = jnp.sin(angle)
        tabs[0, block(b)] = jnp.where(part_lane < ROT, jnp.cos(angle), 1.0)
        tabs[1, block(b)] = jnp.where(part_lane < ROT // 2, -sine, 0.0)
        tabs[2, block(b)] = jnp.where((part_lane >= ROT // 2) & (part_lane < ROT), sine, 0.0)
        return 0

    lax.fori_loop(0, NB, tables, 0)
    for k, src in enumerate(sources):
        piece = wall.at[1 - x, src, mine_rows]
        arrived(piece, r_w.at[1, src], dp=xn)
        copies.send(piece, piece, s_w.at[3, k], r_w.at[3, src], dp=cn)
    for src in sources:
        arrived(sall.at[src], r_small.at[src], dp=xn)
    for b in range(F):
        placed[b, 0:6] = sall[b, 0:6]
        for i in range(3):
            m = F * i + b
            placed[b, 6 + i : 7 + i] = sall[m // 3, 6 + m % 3 : 7 + m % 3]
        placed[b, 9:16] = jnp.zeros((7, 128), f32)
    total = jnp.zeros((16, D), f32)
    for b in range(F):
        total = total + dot(placed[b].astype(bf16), place_matrix(W, b * W, D).astype(bf16), NN)
    full[...] = total
    start = (me // 2) * (3 * HEAD) + HEAD * y
    window = (
        lax.broadcasted_iota(jnp.int32, (D, 128), 0) - start == lax.broadcasted_iota(jnp.int32, (D, 128), 1)
    ).astype(f32)
    b_qkv = dot(total.astype(bf16), window.astype(bf16), NN)
    gain_one, bias_one, gain_two, bias_two = [total[i : i + 1] for i in range(4)]
    off = 32 * y
    mine = ((lane >= off) & (lane < off + W))[0:1]

    def norm(b):
        ln_rows(xall, normed, None, b)
        n = normed[block(b)]
        first[block(b)] = (n * gain_one + bias_one).astype(bf16)
        second[block(b)] = (n * gain_two + bias_two).astype(bf16)

    up_shift = b_up[...].astype(f32).reshape(1, C)
    head = [lane // HEAD == h for h in range(2)]

    def project(b):
        p = dot(first[block(b)], wall[0].reshape(D, C), NN)
        ct, s1, s2 = tabs[0, block(b)], tabs[1, block(b)], tabs[2, block(b)]
        q = turn(p[:, :128] + b_qkv[6:7], ct, s1, s2) * 0.125
        q_s[block(b)] = q.astype(bf16)
        k_s[block(b)] = turn(p[:, 128:256] + b_qkv[7:8], ct, s1, s2).astype(bf16)
        v_s[block(b)] = (p[:, 256:] + b_qkv[8:9]).astype(bf16)
        u = dot(second[block(b)], wall[1].reshape(D, C), NN) + up_shift
        cdf = 0.5 * (1.0 + lax.erf(u * inv_root_two))
        hidden[block(b)] = (u * cdf).astype(bf16)
        slope[block(b)] = cdf + u * jnp.exp(-0.5 * u * u) * inv_root_twopi

    other_rows = pl.ds(pl.multiple_of((1 - c) * half, half), half)
    for j, b in enumerate(near):
        tokens.got(2 * b + 1 - y)
        norm(b)
        if j == 1:
            grads.step(1)
            for src in sources:
                arrived(wall.at[x, src, other_rows], r_w.at[2, src], dp=cn)
                arrived(wall.at[1 - x, src, other_rows], r_w.at[3, src], dp=cn)
            arrived(outwin.at[pl.ds(pl.multiple_of(W * (1 - y), 32), 32)], r_o, fsdp=z * 2 + 1 - y)
            project(near[0])
        if j:
            project(b)
    grads.step(2)

    def seen():
        r = lax.broadcasted_iota(jnp.int32, (RB, RB), 0)
        return lax.broadcasted_iota(jnp.int32, (RB, RB), 1) <= r

    def attend(b):
        kv = (b + 1) * RB
        rows = slice(b * RB, kv)
        halves = []
        for h in range(2):
            q = jnp.where(head[h], q_s[rows], jnp.zeros((), bf16))
            s = dot(q, k_s[:kv], NT)
            last = jnp.where(seen(), s[:, kv - RB :], -1e30)
            top = jnp.max(last, axis=-1, keepdims=True)
            if b:
                top = jnp.maximum(top, jnp.max(s[:, : kv - RB], axis=-1, keepdims=True))
            e_last = jnp.exp(last - top)
            norm = jnp.sum(e_last, axis=-1, keepdims=True)
            if b:
                e_rest = jnp.exp(s[:, : kv - RB] - top)
                norm = norm + jnp.sum(e_rest, axis=-1, keepdims=True)
            inv = 1.0 / norm
            probs[h, rows, kv - RB : kv] = (e_last * inv).astype(bf16)
            if b:
                probs[h, rows, : kv - RB] = (e_rest * inv).astype(bf16)
            halves.append(dot(probs[h, rows, :kv], v_s[:kv], NN))
        a = jnp.where(head[0], halves[0], halves[1])
        att[rows] = a
        att_low[rows] = jnp.where(mine, a, 0.0).astype(bf16)
        p = dot(att_low[rows], outwin[...], NN) + dot(hidden[rows], downw[...], NN)
        part[2 * b : 2 * b + 2] = p.astype(bf16).reshape(2, RB // 2, D)

    one = Collect(copies, part, yb.at[0], zb.at[0], sb.at[0], sems.at[0], branch_out, Z, z, y)
    for b in range(NB):
        attend(b)
        if b == 1:
            for k in range(3, Z):
                grads.step(k)
    far = near[::-1]
    for b in far:
        one.push(b)

    vec[...] = jnp.zeros_like(vec)

    def back(b):
        g = gall[pl.ds(2 * b, 2)].reshape(RB, D)
        gp = (dot(g, downw[...], NT) * slope[block(b)]).astype(bf16)
        gpre[block(b)] = gp
        gatt[block(b)] = dot(g, outwin[...], NT).astype(bf16)
        gs = dot(gp, wall[1].reshape(D, C), NT)
        n = normed[block(b)]
        vec[2:3] += jnp.sum(gs * n, axis=0, keepdims=True)
        vec[3:4] += jnp.sum(gs, axis=0, keepdims=True)
        vec[7:8] += jnp.sum(g.astype(f32), axis=0, keepdims=True)
        gsec[block(b)] = gs * gain_two
        sums = jnp.sum(gp.astype(f32), axis=0, keepdims=True)
        for i in range(C // 128):
            own_vec[1 + i : 2 + i] += sums[:, i * 128 : (i + 1) * 128]

    own_vec[...] = jnp.zeros_like(own_vec)
    for b in near:
        grads.got(2 * b + 1 - y)
        back(b)

    g_flat = gall[...].reshape(S, D)
    down_grad = dot(hidden[...], g_flat, TN).astype(bf16)
    q4 = C // 2
    for i in range(2):
        for j in range(2):
            g_own[i, j, half:] = down_grad[j * q4 : (j + 1) * q4, i * C : (i + 1) * C]
    gout_win[...] = dot(att_low[...], g_flat, TN).astype(bf16)
    for i in range(2):
        for j in range(2):
            g_own[i, j, :half] = gout_win[pl.ds(pl.multiple_of(off + j * half, 16), half), i * C : (i + 1) * C]
    for i in range(2):
        copies.send(g_own.at[i, 1 - c], co_buf.at[i], s_co.at[i], r_co.at[i], dp=cn)

    def matrix(m, left, right):
        g = dot(left[...], right[...], TN).astype(bf16).reshape(F, 2, half, C)
        for j in range(2):
            g_mat[m, j] = g[:, j].reshape(F * half, C)
        copies.send(g_mat.at[m, 1 - c], cbuf.at[m], s_c.at[m], r_c.at[m], dp=cn)

    def matrix_x(m):
        arrived(cbuf.at[m], r_c.at[m], dp=cn)
        add_rows(hbuf.at[m], [g_mat.at[m, c], cbuf.at[m]])
        copies.send(hbuf.at[m], xbuf.at[m], s_x.at[m], r_x.at[m], x != m, dp=xn)

    def matrix_spread(m):
        own = x == m

        @pl.when(own)
        def _():
            arrived(xbuf.at[m], r_x.at[m], dp=xn)
            add_rows(hbuf.at[m], [hbuf.at[m], xbuf.at[m]])
            here = pl.ds(pl.multiple_of(me * half, half), half)
            ret[m, c, here] = hbuf[m, here]

        for k, o in enumerate(others):
            there = pl.ds(pl.multiple_of(o * half, half), half)
            here = pl.ds(pl.multiple_of(me * half, half), half)
            copies.send(hbuf.at[m, there], ret.at[m, c, here], s_a.at[m, k], r_a.at[m, me], own, fsdp=o)

    def matrix_share(m, by_owner):
        act = (x == m) == by_owner
        for k, src in enumerate([me] + sources):
            piece = ret.at[m, c, pl.ds(pl.multiple_of(src * half, half), half)]
            if k or not by_owner:

                @pl.when(act)
                def _():
                    arrived(piece, r_a.at[m, src], dp=xn)

            if by_owner:
                copies.send(piece, piece, s_cc.at[m, 0, k], r_a.at[m, src], act, dp=xn)
            copies.send(piece, piece, s_cc.at[m, 1, k], r_cc.at[m, src], act, dp=cn)

    matrix(1, second, gpre)
    one.step(far[0])
    for i in range(2):
        arrived(co_buf.at[i], r_co.at[i], dp=cn)
        add_rows(ho_buf.at[i], [g_own.at[i, c], co_buf.at[i]])
    copies.send(ho_buf.at[1 - x], xo_buf, s_xo, r_xo, dp=xn)
    matrix_x(1)

    def attend_back(b):
        kv = (b + 1) * RB
        rows = slice(b * RB, kv)
        ga, a = gatt[rows], att[rows]
        prod = ga.astype(f32) * a
        q_grad = None
        for h in range(2):
            delta = jnp.sum(jnp.where(head[h], prod, 0.0), axis=-1, keepdims=True)
            gah = jnp.where(head[h], ga, jnp.zeros((), bf16))
            qh = jnp.where(head[h], q_s[rows], jnp.zeros((), bf16))
            p = probs[h, rows, :kv]
            gp = dot(gah, v_s[:kv], NT)
            gs_f = p.astype(f32) * (gp - delta)
            last = jnp.where(seen(), gs_f[:, kv - RB :], 0.0).astype(bf16)
            gs = jnp.concatenate([gs_f[:, : kv - RB].astype(bf16), last], axis=1) if b else last
            dq = dot(gs, k_s[:kv], NN)
            q_grad = dq if h == 0 else jnp.where(head[0], q_grad, dq)
            gk[:kv] += dot(gs, qh, TN)
            gv[:kv] += dot(p, gah, TN)
        gq[rows] = q_grad

    def back_project(b):
        ct, s1, s2 = tabs[0, block(b)], tabs[1, block(b)], tabs[2, block(b)]
        dq = turn(gq[block(b)] * 0.125, ct, -s1, -s2)
        dk = turn(gk[block(b)], ct, -s1, -s2)
        for i, t in enumerate((dq, dk, gv[block(b)])):
            low = jnp.where(mine, t, 0.0).astype(bf16)
            gproj[block(b), i * 128 : (i + 1) * 128] = low
            own_vec[8 + i : 9 + i] += jnp.sum(low.astype(f32), axis=0, keepdims=True)

    def back_norm(b):
        gf = dot(gproj[block(b)], wall[0].reshape(D, C), NT)
        n = normed[block(b)]
        vec[0:1] += jnp.sum(gf * n, axis=0, keepdims=True)
        vec[1:2] += jnp.sum(gf, axis=0, keepdims=True)
        mixed[pl.ds(2 * b, 2)] = (gf * gain_one + gsec[block(b)]).astype(bf16).reshape(2, RB // 2, D)

    gk[...] = jnp.zeros_like(gk)
    gv[...] = jnp.zeros_like(gv)
    two = Collect(copies, mixed, yb.at[1], zb.at[1], sb.at[1], sems.at[1], mixed_out, Z, z, y)
    attend_back(3)
    attend_back(2)
    one.step(far[1])
    arrived(xo_buf, r_xo, dp=xn)
    owner = ret_own.at[x, c]
    add_rows(owner, [ho_buf.at[x], xo_buf])
    copies.send(owner, owner, s_fo.at[0], r_fo.at[0], dp=xn)
    copies.send(owner, owner, s_fo.at[1], r_fo.at[1], dp=cn)
    matrix_spread(1)
    attend_back(1)
    attend_back(0)
    for b in range(NB):
        back_project(b)
    matrix(0, first, gproj)
    for j, b in enumerate(far):
        back_norm(b)
        two.push(b)
        if j == 1:
            matrix_x(0)
    matrix_share(1, True)
    one.step(far[2])
    two.step(far[0])

    vec[4:7] = exact(own_vec[8:16], window, NT)[0:3]
    pieces = [exact(vec[...], place_matrix(W, b * W, D), NT) for b in range(F)]
    for b in range(F):
        vecs[b, 0:4] = pieces[b][0:4]
        for j in range(3):
            m = 3 * b + j
            vecs[b, 4 + j : 5 + j] = pieces[m % F][4 + m // F : 5 + m // F]
        vecs[b, 7:8] = jnp.zeros((1, 128), f32)
    own_vec[0:1] = exact(vec[...], place_matrix(W, me * W, D), NT)[7:8]
    vbuf[me] = vecs[me]
    for k, o in enumerate(others):
        copies.send(vecs.at[o], vbuf.at[me], s_v.at[k], r_v.at[me], fsdp=o)
    matrix_spread(0)
    two.step(far[1])
    two.step(far[2])
    for src in sources:
        arrived(vbuf.at[src], r_v.at[src], dp=xn)
    total = vbuf[0]
    for g in range(1, F):
        total = total + vbuf[g]
    vtot[d, :8] = total
    vtot[d, 8:] = own_vec[0:8]
    for k, to in enumerate((xn, cn, dn)):
        copies.send(vtot.at[d], vtot.at[d], s_d.at[k], r_d.at[d], dp=to)
    one.finish()
    matrix_share(0, True)
    matrix_share(1, False)
    matrix_share(0, False)
    arrived(ret_own.at[1 - x, c], r_fo.at[0], dp=xn)
    copies.send(ret_own.at[1 - x, c], ret_own.at[1 - x, c], s_fo.at[2], r_fo.at[2], dp=cn)
    two.finish()
    for to in (xn, cn, dn):
        arrived(vtot.at[to], r_d.at[to], dp=to)
    vec_sum[...] = vtot[0] + vtot[1] + vtot[2] + vtot[3]
    arrived(ret_own.at[x, 1 - c], r_fo.at[1], dp=cn)
    arrived(ret_own.at[1 - x, 1 - c], r_fo.at[2], dp=cn)
    for m in range(2):
        for g in range(F):
            arrived(ret.at[m, 1 - c, pl.ds(g * half, half)], r_cc.at[m, g], dp=cn)
    copies.drain()


def layer(F, tok, cot, qkv, up, outw, downw, *vectors):
    rows, D = tok.shape
    W, FF = up.shape
    C = FF // F
    S, Z, half = rows * F, F // 2, W // 2
    own = (W + C) // 2
    dma = pltpu.SemaphoreType.DMA
    low = lambda *s: pltpu.VMEM(s, bf16)
    wide = lambda *s: pltpu.VMEM(s, f32)
    return pl.pallas_call(
        functools.partial(layer_kernel, F),
        out_shape=(
            jax.ShapeDtypeStruct((rows, D), f32),
            jax.ShapeDtypeStruct((rows, D), f32),
            jax.ShapeDtypeStruct((2, 2, F * half, C), bf16),
            jax.ShapeDtypeStruct((2, 2, own, C), bf16),
            jax.ShapeDtypeStruct((16, 128), f32),
            jax.ShapeDtypeStruct((16, D), f32),
        ),
        in_specs=[pl.BlockSpec(memory_space=pl.ANY)] * 6 + [vmem()] * 8,
        out_specs=(vmem(),) * 6,
        scratch_shapes=[
            low(F, rows, D), low(F, rows, D), wide(F, 16, 128), low(2, F, W, C), low(128, D), low(2, F, W, C),
            wide(F, 16, 128),
            wide(3, S, 128), wide(S, D), low(S, D), low(S, D), low(S, 128), low(S, 128), low(S, 128), low(2, S, S),
            wide(S, 128), low(S, 128), low(S, C), wide(S, C), low(F, rows, D), low(S, C), low(S, 128), wide(S, D),
            low(F, rows, D),
            low(S, 3 * 128), wide(S, 128), wide(S, 128), wide(S, 128), low(128, D), low(2, 2, F * half, C),
            low(2, 2, own, C), wide(8, D), wide(F, 8, 128), wide(16, 128),
            low(W, 3 * D), low(W, FF), low(W, D), low(C, D), wide(16, 128),
            low(2, Z, rows, D), low(2, Z, rows, D), low(2, Z, rows, D),
            low(2, F * half, C), low(2, F * half, C), low(2, F * half, C),
            low(2, own, C), low(2, own, C), low(own, C), wide(F, 8, 128), wide(4, 16, 128),
            dma((3, F)), dma((F,)), dma((3, F)), dma((F,)), dma((F,)), dma((F,)), dma((4, F)), dma((4, F)), dma, dma,
            dma((2, 4, Z)),
            dma((2,)), dma((2,)), dma((2,)), dma((2,)), dma((2, F)), dma((2, F)), dma((2, 2, F)), dma((2, F)),
            dma((2,)), dma((2,)), dma, dma, dma((3,)), dma((3,)), dma((F,)), dma((F,)), dma((3,)), dma((4,)),
            dma((6,)),
        ],
        compiler_params=pltpu.CompilerParams(
            collective_id=0, has_side_effects=True, vmem_limit_bytes=60 * 2**20
        ),
        name="layer",
    )(tok, cot, qkv, up, outw, downw, *vectors)


def finish_kernel(
    F, tok_in, cot_in, branch_in, mixed_in, ret_in, own_in, full, vec_sum, out, igrad, g_qkv, g_out, g_up, g_down,
    o0, o1, o2, o3, o_qkv, o_out, o_up, o_down, ret_own, ret, tok, cot, branch, mixed,
    w_out, w_igrad, w_qkv, w_out_grad, w_up, w_down, sem, out_sem,
):
    fetches = [
        pltpu.make_async_copy(src, dst, sem.at[i])
        for i, (src, dst) in enumerate(
            (
                (own_in, ret_own), (ret_in, ret), (tok_in, tok), (cot_in, cot), (branch_in, branch), (mixed_in, mixed)
            )
        )
    ]
    for fetch in fetches:
        fetch.start()
    W, D = g_out.shape
    C = ret.shape[3]
    for i, o in enumerate((o0, o1, o2, o3)):
        o[...] = vec_sum[i : i + 1, :W].reshape(W)
    o_qkv[...] = jnp.concatenate([vec_sum[4 + i : 5 + i, :W] for i in range(3)], axis=1).reshape(3 * W)
    o_out[...] = vec_sum[8:9, :W].reshape(W)
    o_down[...] = vec_sum[8:9, :W].reshape(W)
    o_up[...] = jnp.concatenate([vec_sum[9 + i : 10 + i] for i in range(C // 128)], axis=1).reshape(C)
    outs = (w_out, w_igrad, w_qkv, w_out_grad, w_up, w_down)
    writes = [
        pltpu.make_async_copy(src, dst, out_sem.at[i])
        for i, (src, dst) in enumerate(zip(outs, (out, igrad, g_qkv, g_out, g_up, g_down)))
    ]
    half = W // 2
    fetches[0].wait()
    for j in range(2):
        rows = slice(j * half, (j + 1) * half)
        for i in range(2):
            columns = slice(i * C, (i + 1) * C)
            w_down[j * (C // 2) : (j + 1) * (C // 2), columns] = ret_own[i, j, half:].astype(f32)
            w_out_grad[rows, columns] = ret_own[i, j, :half].astype(f32)
    writes[5].start()
    writes[3].start()
    fetches[1].wait()
    for j in range(2):
        rows = slice(j * half, (j + 1) * half)
        for g in range(F):
            w_up[rows, g * C : (g + 1) * C] = ret[1, j, g * half : (g + 1) * half].astype(f32)
    writes[4].start()
    row = lax.broadcasted_iota(jnp.int32, (128, D), 0)
    col = lax.broadcasted_iota(jnp.int32, (128, D), 1)
    totals = [jnp.zeros((W, D), f32)] * 3
    for g in range(F):
        s = g * W // HEAD * HEAD
        place = ((row + s == col) & (col >= g * W) & (col < (g + 1) * W)).astype(bf16)
        for i in range(3):
            piece = jnp.concatenate(
                [ret[0, j, g * half : (g + 1) * half, i * 128 : (i + 1) * 128] for j in range(2)], axis=0
            )
            totals[i] = totals[i] + dot(piece, place, NN)
    for i in range(3):
        w_qkv[:, i * D : (i + 1) * D] = totals[i]
    writes[2].start()
    for fetch in fetches[2:]:
        fetch.wait()
    x = tok[...].astype(f32)
    center = x - jnp.mean(x, axis=-1, keepdims=True)
    inverse = lax.rsqrt(jnp.mean(center * center, axis=-1, keepdims=True) + epsilon)
    n = center * inverse
    w_out[...] = (x + branch[...] + full[4:5] + full[5:6]).astype(bf16)
    writes[0].start()
    m = mixed[...]
    m = m - jnp.mean(m, axis=-1, keepdims=True) - n * jnp.mean(m * n, axis=-1, keepdims=True)
    w_igrad[...] = cot[...].astype(f32) + inverse * m
    writes[1].start()
    for write in writes:
        write.wait()


def finish(F, tok, cot, branch, mixed, ret, ret_own, full, vec_sum):
    rows, D = tok.shape
    W = D // F
    C = ret.shape[3]
    big = (
        jax.ShapeDtypeStruct((rows, D), bf16),
        jax.ShapeDtypeStruct((rows, D), f32),
        jax.ShapeDtypeStruct((W, 3 * D), f32),
        jax.ShapeDtypeStruct((W, D), f32),
        jax.ShapeDtypeStruct((W, F * C), f32),
        jax.ShapeDtypeStruct((C, D), f32),
    )
    anywhere = pl.BlockSpec(memory_space=pl.ANY)
    return pl.pallas_call(
        functools.partial(finish_kernel, F),
        out_shape=big
        + tuple(jax.ShapeDtypeStruct((n,), f32) for n in (W, W, W, W, 3 * W, W, C, W)),
        in_specs=[anywhere] * 6 + [vmem()] * 2,
        out_specs=(anywhere,) * 6 + (vmem(),) * 8,
        scratch_shapes=[
            pltpu.VMEM(a.shape, a.dtype) for a in (ret_own, ret, tok, cot, branch, mixed) + big
        ]
        + [pltpu.SemaphoreType.DMA((6,))] * 2,
        compiler_params=pltpu.CompilerParams(vmem_limit_bytes=60 * 2**20),
        name="finish",
    )(tok, cot, branch, mixed, ret, ret_own, full, vec_sum)


def fast_body(
    tokens, ln1_gain, ln1_bias, ln2_gain, ln2_bias, qkv_weight, qkv_bias, out_weight, out_bias, up_weight, up_bias,
    down_weight, down_bias, cotangent,
):
    F = lax.axis_size("fsdp")
    branch, mixed, ret, ret_own, vec_sum, full = layer(
        F, tokens[0], cotangent[0], qkv_weight, up_weight, out_weight, down_weight,
        ln1_gain, ln1_bias, ln2_gain, ln2_bias, out_bias, down_bias, qkv_bias, up_bias,
    )
    out, igrad, g_qkv, g_out, g_up, g_down, o0, o1, o2, o3, o_qkv, o_out, o_up, o_down = finish(
        F, tokens[0], cotangent[0], branch, mixed, ret, ret_own, full, vec_sum
    )
    return (
        out[None], igrad[None], o0, o1, o2, o3, g_qkv, o_qkv, g_out, o_out, g_up, o_up, g_down, o_down
    )


def solution(mesh):
    row = P("fsdp", None)
    vec = P("fsdp")
    act = P("dp", "fsdp", None)
    fast = mesh.shape["fsdp"] == 8 and mesh.shape["dp"] == 4
    return jax.shard_map(
        fast_body if fast else body,
        mesh=mesh,
        in_specs=(act, vec, vec, vec, vec, row, vec, row, vec, row, vec, row, vec, act),
        out_specs=(act, act, vec, vec, vec, vec, row, vec, row, vec, row, vec, row, vec),
        check_vma=False,
    )
```

```python
import functools
import math

import jax
import jax.numpy as jnp
from jax import lax
from jax.experimental import pallas as pl
from jax.experimental.pallas import tpu as pltpu
from jax.sharding import PartitionSpec as P

HEADS = 12
HEAD = 64
ROT = 16

epsilon = 1e-05
inv_root_two = 1.0 / math.sqrt(2.0)
inv_root_twopi = 1.0 / math.sqrt(2.0 * math.pi)
bf16 = jnp.bfloat16
f32 = jnp.float32


def rotary(tensor, cosine, sine, direction):
    half = ROT // 2
    first = tensor[..., :half]
    second = tensor[..., half:ROT]
    return jnp.concatenate(
        [
            first * cosine - direction * second * sine,
            second * cosine + direction * first * sine,
            tensor[..., ROT:],
        ],
        axis=-1,
    )


def dot(a, b, dims):
    return lax.dot_general(a, b, ((dims[0], dims[1]), ((), ())), preferred_element_type=f32)


NN = ((1,), (0,))
NT = ((1,), (1,))
TN = ((0,), (0,))


def gather_rows(arrays):
    return [lax.all_gather(a, "fsdp", axis=0, tiled=True) for a in arrays]


def scatter_rows(a):
    F = lax.axis_size("fsdp")
    got = lax.all_to_all(a, "fsdp", 0, 0, tiled=True)
    return jnp.sum(got.reshape((F, a.shape[0] // F) + a.shape[1:]).astype(f32), axis=0)


def spread_weights(blocks):
    return lax.all_to_all(blocks, "fsdp", 0, 0, tiled=True)


def return_grads(blocks, own):
    n = lax.axis_size("dp")
    F, W, C = blocks.shape
    R, D = own.shape
    parts = jnp.swapaxes(blocks.reshape(F, n, W // n, C), 0, 1).reshape(n, F * (W // n), C)
    own_parts = own.reshape(n, R // n, D)
    if C == D:
        both = jnp.concatenate([parts, own_parts], axis=1)
        both = jnp.sum(lax.all_to_all(both, "dp", 0, 0, tiled=True).astype(f32), axis=0)
        part, own_part = both[: F * (W // n)].astype(bf16), both[F * (W // n) :].astype(bf16)
    else:
        part = jnp.sum(lax.all_to_all(parts, "dp", 0, 0, tiled=True).astype(f32), axis=0)
        own_part = jnp.sum(lax.all_to_all(own_parts, "dp", 0, 0, tiled=True).astype(f32), axis=0)
        part, own_part = part.astype(bf16), own_part.astype(bf16)
    part = lax.all_to_all(part, "fsdp", 0, 0, tiled=True)
    if C == D:
        whole = lax.all_gather(jnp.concatenate([part, own_part], axis=0), "dp", axis=0)
        part_all, own_all = whole[:, : F * (W // n)], whole[:, F * (W // n) :]
    else:
        part_all = lax.all_gather(part, "dp", axis=0)
        own_all = lax.all_gather(own_part, "dp", axis=0)
    part_all = jnp.swapaxes(part_all.reshape(n, F, W // n, C), 0, 1).reshape(F, W, C)
    return part_all, own_all.reshape(R, D)


def body(
    tokens,
    ln1_gain,
    ln1_bias,
    ln2_gain,
    ln2_bias,
    qkv_weight,
    qkv_bias,
    out_weight,
    out_bias,
    up_weight,
    up_bias,
    down_weight,
    down_bias,
    cotangent,
):
    rank = lax.axis_index("fsdp")
    F = lax.axis_size("fsdp")
    rows, D = tokens.shape[1:]
    W = D // F
    FFW = down_weight.shape[0]
    NH = max(-(-((g * W) % HEAD + W) // HEAD) for g in range(F))
    WIN = NH * HEAD
    starts = [min(g * W // HEAD, HEADS - NH) * HEAD for g in range(F)]
    start = jnp.minimum(rank * W // HEAD, HEADS - NH) * HEAD
    off = rank * W - start
    S = rows * F

    qkv3 = qkv_weight.reshape(W, 3, D)
    blocks = jnp.stack(
        [
            jnp.concatenate(
                [
                    qkv3[:, 0, s : s + WIN],
                    qkv3[:, 1, s : s + WIN],
                    qkv3[:, 2, s : s + WIN],
                    up_weight[:, g * FFW : (g + 1) * FFW],
                ],
                axis=1,
            )
            for g, s in enumerate(starts)
        ]
    )
    smalls = jnp.concatenate(
        [ln1_gain, ln1_bias, ln2_gain, ln2_bias, out_bias, down_bias, qkv_bias]
    )
    extra = -(-smalls.shape[0] // (16 * D)) * 16
    smalls = jnp.concatenate([smalls, jnp.zeros(extra * D - smalls.shape[0], bf16)])
    (both_all,) = gather_rows([jnp.concatenate([tokens[0], smalls.reshape(extra, D)], axis=0)])
    both_all = both_all.reshape(F, rows + extra, D)
    x_low = both_all[:, :rows].reshape(S, D)
    small_all = both_all[:, rows:].reshape(F, extra * D)
    wall = spread_weights(blocks).reshape(D, 3 * WIN + FFW)
    w_qkv = wall[:, : 3 * WIN]
    w_up = wall[:, 3 * WIN :]
    up_ring = [(i, (i + 1) % F) for i in range(F)]
    down_ring = [(i, (i - 1) % F) for i in range(F)]
    out_prev = lax.ppermute(out_weight, "fsdp", up_ring)
    out_next = lax.ppermute(out_weight, "fsdp", down_ring)
    (grad_out,) = gather_rows([cotangent[0]])
    out_three = jnp.concatenate(
        [out_prev, out_weight, out_next, jnp.zeros((WIN, D), bf16)], axis=0
    )
    w_out_win = lax.dynamic_slice_in_dim(out_three, W - off, WIN, 0)
    win_col = jnp.arange(WIN, dtype=jnp.int32)
    mine = (win_col >= off) & (win_col < off + W)
    small_all = small_all.astype(f32)
    gain_one, bias_one, gain_two, bias_two, b_out, b_down = [
        small_all[:, i * W : (i + 1) * W].reshape(D) for i in range(6)
    ]
    b_qkv = small_all[:, 6 * W : 9 * W].reshape(3, D)
    b_qkv = lax.dynamic_slice_in_dim(b_qkv, start, WIN, 1).reshape(3 * WIN)
    b_up = up_bias.astype(f32)

    x = x_low.astype(f32)
    center = x - jnp.mean(x, axis=-1, keepdims=True)
    inverse = lax.rsqrt(jnp.mean(center * center, axis=-1, keepdims=True) + epsilon)
    normed = center * inverse
    first_low = (normed * gain_one + bias_one).astype(bf16)
    second_low = (normed * gain_two + bias_two).astype(bf16)

    places = jnp.arange(S, dtype=f32)
    half = ROT // 2
    freq = 10000.0 ** (-(jnp.arange(half, dtype=f32) * 2.0) / ROT)
    angle = places[:, None] * freq[None, :]
    cosine = jnp.cos(angle)[:, None, :]
    sine = jnp.sin(angle)[:, None, :]

    proj = dot(first_low, w_qkv, NN) + b_qkv
    queries = (rotary(proj[:, :WIN].reshape(S, NH, HEAD), cosine, sine, 1.0) * 0.125).astype(bf16)
    keys = rotary(proj[:, WIN : 2 * WIN].reshape(S, NH, HEAD), cosine, sine, 1.0).astype(bf16)
    vals = proj[:, 2 * WIN :].astype(bf16).reshape(S, NH, HEAD)
    q_place = jnp.arange(S, dtype=jnp.int32)
    visible = (q_place[None, :] <= q_place[:, None])[None]
    scores = jnp.einsum("qhd,khd->hqk", queries, keys, preferred_element_type=f32)
    masked = jnp.where(visible, scores, -1e30)
    top = jnp.max(masked, axis=-1, keepdims=True)
    lse = top + jnp.log(jnp.sum(jnp.exp(masked - top), axis=-1, keepdims=True))
    probs = jnp.exp(masked - lse)
    probs_low = probs.astype(bf16)
    attended = jnp.einsum("hqk,khd->qhd", probs_low, vals, preferred_element_type=f32)
    att_low = jnp.where(mine, attended.reshape(S, WIN), 0.0).astype(bf16)

    hidden_pre = dot(second_low, w_up, NN) + b_up
    cdf = 0.5 * (1.0 + lax.erf(hidden_pre * inv_root_two))
    hidden_low = (hidden_pre * cdf).astype(bf16)
    part = dot(att_low, w_out_win, NN) + dot(hidden_low, down_weight, NN)
    branch = scatter_rows(part.astype(bf16))

    grad_hidden = dot(grad_out, down_weight, NT)
    slope = cdf + hidden_pre * jnp.exp(-0.5 * hidden_pre * hidden_pre) * inv_root_twopi
    grad_pre = (grad_hidden * slope).astype(bf16)
    grad_w_down = dot(hidden_low, grad_out, TN)
    grad_w_out_win = dot(att_low, grad_out, TN)
    grad_w_out = lax.dynamic_slice_in_dim(grad_w_out_win, off, W, 0)
    bias_total = jnp.sum(grad_out.astype(f32), axis=0)
    grad_b_up = jnp.sum(grad_pre.astype(f32), axis=0)
    grad_att = dot(grad_out, w_out_win, NT).astype(bf16).reshape(S, NH, HEAD)
    delta = jnp.transpose(jnp.sum(grad_att.astype(f32) * attended, axis=-1))[:, :, None]
    grad_probs = jnp.einsum("qhd,khd->hqk", grad_att, vals, preferred_element_type=f32)
    grad_scores = (probs * (grad_probs - delta)).astype(bf16)
    grad_q = jnp.einsum("hqk,khd->qhd", grad_scores, keys, preferred_element_type=f32)
    grad_k = jnp.einsum("hqk,qhd->khd", grad_scores, queries, preferred_element_type=f32)
    grad_v = jnp.einsum("hqk,qhd->khd", probs_low, grad_att, preferred_element_type=f32)
    grad_proj = jnp.stack(
        [
            rotary(grad_q * 0.125, cosine, sine, -1.0).reshape(S, WIN),
            rotary(grad_k, cosine, sine, -1.0).reshape(S, WIN),
            grad_v.reshape(S, WIN),
        ],
        axis=1,
    )
    grad_proj = jnp.where(mine, grad_proj, 0.0).astype(bf16).reshape(S, 3 * WIN)
    grad_w_qkv = dot(first_low, grad_proj, TN)
    grad_w_up = dot(second_low, grad_pre, TN)
    grad_b_qkv = jnp.sum(grad_proj.astype(f32), axis=0).reshape(3, WIN)
    grad_first = dot(grad_proj, w_qkv, NT)
    grad_second = dot(grad_pre, w_up, NT)
    vectors = [
        jnp.sum(grad_first * normed, axis=0),
        jnp.sum(grad_first, axis=0),
        jnp.sum(grad_second * normed, axis=0),
        jnp.sum(grad_second, axis=0),
    ]
    mixed = grad_first * gain_one + grad_second * gain_two
    b_full = lax.dynamic_update_slice_in_dim(jnp.zeros((3, D), f32), grad_b_qkv, start, 1)
    small_part = jnp.concatenate(
        [v.reshape(F, W) for v in vectors] + [b_full.reshape(F, 3 * W)], axis=1
    )
    mixed_mine = scatter_rows(mixed.astype(bf16))
    small_mine = scatter_rows(small_part)[0]
    own_small = jnp.concatenate(
        [small_mine, lax.dynamic_slice_in_dim(bias_total, rank * W, W, 0), grad_b_up]
    )
    pad = 8 * lax.axis_size("dp")
    own_rows = -(-(W + FFW + -(-own_small.shape[0] // D)) // pad) * pad
    n_small = own_rows - W - FFW
    own_small = jnp.concatenate([own_small, jnp.zeros(n_small * D - own_small.shape[0], f32)])

    grad_blocks = jnp.concatenate([grad_w_qkv, grad_w_up], axis=1).astype(bf16)
    grad_blocks = grad_blocks.reshape(F, W, 3 * WIN + FFW)
    own = jnp.concatenate(
        [grad_w_out, grad_w_down, own_small.reshape(n_small, D)], axis=0
    ).astype(bf16)
    returned, own = return_grads(grad_blocks, own)
    returned = returned.astype(f32)
    own = own.astype(f32)
    own_small = own[W + FFW :].reshape(n_small * D)
    pieces = [
        [returned[g, :, i * WIN + g * W - s : i * WIN + g * W - s + W] for g, s in enumerate(starts)]
        for i in range(3)
    ]
    out_w_qkv = jnp.concatenate(pieces[0] + pieces[1] + pieces[2], axis=1)
    out_w_up = jnp.concatenate([returned[g, :, 3 * WIN :] for g in range(F)], axis=1)

    here = rank * rows
    x_own = tokens[0].astype(f32)
    c_own = x_own - jnp.mean(x_own, axis=-1, keepdims=True)
    i_own = lax.rsqrt(jnp.mean(c_own * c_own, axis=-1, keepdims=True) + epsilon)
    n_own = c_own * i_own
    layer_output = (x_own + branch + b_out + b_down).astype(bf16)
    input_grad = cotangent[0].astype(f32) + i_own * (
        mixed_mine
        - jnp.mean(mixed_mine, axis=-1, keepdims=True)
        - n_own * jnp.mean(mixed_mine * n_own, axis=-1, keepdims=True)
    )
    g = [own_small[i * W : (i + 1) * W] for i in range(4)]
    bias_mine = own_small[7 * W : 8 * W]
    return (
        layer_output[None],
        input_grad[None],
        g[0],
        g[1],
        g[2],
        g[3],
        out_w_qkv,
        own_small[4 * W : 7 * W],
        own[:W],
        bias_mine,
        out_w_up,
        own_small[8 * W : 8 * W + FFW],
        own[W : W + FFW],
        bias_mine,
    )


class Copies:
    def __init__(self):
        self.later = []

    def send(self, src, dst, send_sem, recv_sem, when=None, **to):
        copy = pltpu.make_async_remote_copy(
            src_ref=src,
            dst_ref=dst,
            send_sem=send_sem,
            recv_sem=recv_sem,
            device_id=to,
            device_id_type=pl.DeviceIdType.MESH,
        )
        if when is None:
            copy.start()
        else:
            pl.when(when)(copy.start)
        self.later.append((copy, when))

    def drain(self):
        for copy, when in self.later:
            if when is None:
                copy.wait_send()
            else:
                pl.when(when)(copy.wait_send)
        self.later = []


def arrived(dst, recv_sem, **to):
    pltpu.make_async_remote_copy(
        src_ref=dst,
        dst_ref=dst,
        send_sem=recv_sem,
        recv_sem=recv_sem,
        device_id=to,
        device_id_type=pl.DeviceIdType.MESH,
    ).wait_recv()


def meet(peers):
    barrier = pltpu.get_barrier_semaphore()
    for to in peers:
        pl.semaphore_signal(barrier, inc=1, device_id=to, device_id_type=pl.DeviceIdType.MESH)
    pl.semaphore_wait(barrier, len(peers))


class Spread:
    def __init__(self, copies, buf, send_sem, recv_sem, Z, z, y):
        self.copies, self.buf, self.ss, self.rs = copies, buf, send_sem, recv_sem
        self.Z, self.z, self.y = Z, z, y

    def push(self, src, way, when=None):
        to = {0: src * 0 + (self.z * 2 + self.y + 2), 1: self.z * 2 + self.y - 2, 2: self.z * 2 + 1 - self.y}[way]
        self.copies.send(
            self.buf.at[src], self.buf.at[src], self.ss.at[way, src], self.rs.at[src], when, fsdp=to
        )

    def first(self):
        me = self.z * 2 + self.y
        self.push(me, 0, self.z + 1 < self.Z)
        self.push(me, 1, self.z > 0)
        self.push(me, 2)

    def got(self, src, when=None):
        def wait():
            arrived(self.buf.at[src], self.rs.at[src], fsdp=self.z * 2 + 1 - self.y)

        if when is None:
            wait()
        else:
            pl.when(when)(wait)

    def step(self, k):
        z, y = self.z, self.y
        low, high = jnp.maximum(z - k, 0) * 2 + y, jnp.minimum(z + k, self.Z - 1) * 2 + y
        has_low, has_high = z - k >= 0, z + k < self.Z
        self.got(low, has_low)
        self.push(low, 0, has_low & (z + 1 < self.Z))
        self.push(low, 2, has_low)
        self.got(high, has_high)
        self.push(high, 1, has_high & (z > 0))
        self.push(high, 2, has_high)

    def finish(self):
        for k in range(self.Z):
            self.got(k * 2 + 1 - self.y)


def vmem():
    return pl.BlockSpec(memory_space=pltpu.VMEM)


def add_rows(out, parts):
    step = 16
    for r in range(0, out.shape[0], step):
        total = parts[0][r : r + step].astype(f32)
        for p in parts[1:]:
            total = total + p[r : r + step].astype(f32)
        out[r : r + step] = total.astype(out.dtype)


class Collect:
    def __init__(self, copies, part, yb, zb, sb, sems, out, Z, z, y):
        self.__dict__.update(copies=copies, part=part, yb=yb, zb=zb, sb=sb, out=out, Z=Z, z=z, y=y)
        self.sy, self.ry, self.sz, self.rz = [sems.at[i] for i in range(4)]
        zb[z] = jnp.zeros(zb.shape[1:], zb.dtype)

    def push(self, t):
        self.copies.send(
            self.part.at[t * 2 + 1 - self.y], self.yb.at[t], self.sy.at[t], self.ry.at[t],
            fsdp=self.z * 2 + 1 - self.y,
        )

    def step(self, t):
        z, y = self.z, self.y
        away = t != z

        @pl.when(away)
        def _():
            arrived(self.yb.at[t], self.ry.at[t], fsdp=z * 2 + 1 - y)
            add_rows(self.sb.at[t], [self.part.at[t * 2 + y], self.yb.at[t]])

        self.copies.send(self.sb.at[t], self.zb.at[z], self.sz.at[t], self.rz.at[z], away, fsdp=t * 2 + y)

    def finish(self):
        z, y, Z = self.z, self.y, self.Z
        to = z * 2 + 1 - y
        arrived(self.yb.at[z], self.ry.at[z], fsdp=to)
        for k in range(1, Z):
            src = lax.rem(z + k, Z)
            arrived(self.zb.at[src], self.rz.at[src], fsdp=to)
        add_rows(self.out, [self.part.at[z * 2 + y], self.yb.at[z]] + [self.zb.at[k] for k in range(Z)])


def ln_rows(xall, normed, scale, b):
    x = xall[pl.ds(2 * b, 2)].reshape(RB, xall.shape[2]).astype(f32)
    center = x - jnp.mean(x, axis=-1, keepdims=True)
    inverse = lax.rsqrt(jnp.mean(center * center, axis=-1, keepdims=True) + epsilon)
    normed[block(b)] = center * inverse


RB = 256


def block(b):
    return pl.ds(pl.multiple_of(b * RB, RB), RB)


def turn(t, cosine, low_sine, high_sine):
    return t * cosine + pltpu.roll(t, 120, 1) * low_sine + pltpu.roll(t, 8, 1) * high_sine


def place_matrix(W, at, D):
    row = lax.broadcasted_iota(jnp.int32, (128, D), 0)
    col = lax.broadcasted_iota(jnp.int32, (128, D), 1)
    return ((col - at == row) & (row < W)).astype(f32)


def exact(a, b, dims):
    return lax.dot_general(
        a, b, ((dims[0], dims[1]), ((), ())), preferred_element_type=f32, precision=lax.Precision.HIGHEST
    )


def layer_kernel(
    F,
    tok, cot, qkv_in, up_in, outw_in, downw_in, v0, v1, v2, v3, v4, v5, qkv_bias, b_up,
    branch_out, mixed_out, ret, ret_own, vec_sum, full,
    xall, gall, sall, wall, outwin, wblk, placed,
    tabs, normed, first, second, q_s, k_s, v_s, probs, att, att_low, hidden, slope, part, gpre, gatt, gsec, mixed,
    gproj, gq, gk, gv, gout_win, g_mat, g_own, vec, vecs, own_vec,
    qkv, up, outw, downw, small, yb, zb, sb, cbuf, hbuf, xbuf, co_buf, ho_buf, xo_buf, vbuf, vtot,
    sx, rx, sg, rg, s_small, r_small, s_w, r_w, s_o, r_o, sems,
    s_c, r_c, s_x, r_x, s_a, r_a, s_cc, r_cc, s_co, r_co, s_xo, r_xo, s_fo, r_fo, s_v, r_v, s_d, r_d, s_in,
):
    me, d = lax.axis_index("fsdp"), lax.axis_index("dp")
    Z, z, y, x, c = F // 2, me // 2, me % 2, d // 2, d % 2
    W, D = outw.shape
    C = wall.shape[3]
    S = normed.shape[0]
    NB = S // RB
    half = W // 2
    others = [lax.rem(me + k, F) for k in range(1, F)]
    sources = [lax.rem(me + F - k, F) for k in range(1, F)]
    xn, cn, dn = d + 2 - 4 * x, d + 1 - 2 * c, (1 - x) * 2 + 1 - c
    fetches = [
        pltpu.make_async_copy(src, dst, s_in.at[i])
        for i, (src, dst) in enumerate(
            (
                (tok, xall.at[me]), (qkv_in, qkv), (up_in, up), (outw_in, outw), (cot, gall.at[me]), (downw_in, downw)
            )
        )
    ]
    for fetch in fetches:
        fetch.start()
    small[...] = jnp.zeros_like(small)
    for i, v in enumerate((v0, v1, v2, v3, v4, v5)):
        small[i : i + 1, :W] = v[...].astype(f32).reshape(1, W)
    shifts = qkv_bias[...].astype(f32).reshape(1, 3 * W)
    for i in range(3):
        small[6 + i : 7 + i, :W] = shifts[:, i * W : (i + 1) * W]
    meet([{"fsdp": o} for o in others] + [{"dp": xn}, {"dp": cn}, {"dp": dn}])
    copies = Copies()

    fetches[0].wait()
    tokens = Spread(copies, xall, sx, rx, Z, z, y)
    tokens.first()
    sall[me] = small[...]
    for k, o in enumerate(others):
        copies.send(small, sall.at[me], s_small.at[k], r_small.at[me], fsdp=o)
    for fetch in fetches[1:4]:
        fetch.wait()
    row = lax.broadcasted_iota(jnp.int32, (256, 128), 0)
    col = lax.broadcasted_iota(jnp.int32, (256, 128), 1)
    shift = (row == col + HEAD).astype(bf16)
    for g in range(F):
        s = g * W // HEAD * HEAD
        for i in range(3):
            at = i * D + s
            if s % 128 == 0:
                piece = qkv[:, at : at + 128]
            else:
                piece = dot(qkv[:, at - 64 : at + 192], shift, NN).astype(bf16)
            wblk[0, g, :, i * 128 : (i + 1) * 128] = piece
        wblk[1, g] = up[:, g * C : (g + 1) * C]
    mine_rows = pl.ds(pl.multiple_of(c * half, half), half)
    for k, o in enumerate(others):
        copies.send(wblk.at[x, o, mine_rows], wall.at[x, me, mine_rows], s_w.at[0, k], r_w.at[0, me], fsdp=o)
    wall[:, me] = wblk[:, me]
    outwin[pl.ds(pl.multiple_of(32 * y, 32), W), :] = outw[...]
    copies.send(
        outw.at[pl.ds(pl.multiple_of((W - 32) * (1 - y), 32), 32)],
        outwin.at[pl.ds(pl.multiple_of(W * y, 32), 32)],
        s_o, r_o, fsdp=z * 2 + 1 - y,
    )
    for fetch in fetches[4:]:
        fetch.wait()
    grads = Spread(copies, gall, sg, rg, Z, z, y)

    near = []
    for j in range(Z):
        at = jnp.int32(0)
        for i in range(Z):
            ranked = sorted(range(Z), key=lambda t: abs(t - i))
            at = jnp.where(z == i, ranked[j], at)
        near.append(at)
    tokens.step(1)
    tokens.step(2)
    for k, src in enumerate(sources):
        piece = wall.at[x, src, mine_rows]
        arrived(piece, r_w.at[0, src], dp=xn)
        copies.send(piece, piece, s_w.at[1, k], r_w.at[1, src], dp=xn)
        copies.send(piece, piece, s_w.at[2, k], r_w.at[2, src], dp=cn)
    grads.first()
    for k in range(3, Z):
        tokens.step(k)

    lane = lax.broadcasted_iota(jnp.int32, (RB, 128), 1)
    part_lane = lane % HEAD
    exponent = (part_lane[0:1] % (ROT // 2)).astype(f32) * (-2.0 * math.log(10000.0) / ROT)
    freq = jnp.exp(exponent)

    def tables(b, _):
        place = (lax.broadcasted_iota(jnp.int32, (RB, 128), 0) + b * RB).astype(f32)
        angle = place * freq
        sine = jnp.sin(angle)
        tabs[0, block(b)] = jnp.where(part_lane < ROT, jnp.cos(angle), 1.0)
        tabs[1, block(b)] = jnp.where(part_lane < ROT // 2, -sine, 0.0)
        tabs[2, block(b)] = jnp.where((part_lane >= ROT // 2) & (part_lane < ROT), sine, 0.0)
        return 0

    lax.fori_loop(0, NB, tables, 0)
    for k, src in enumerate(sources):
        piece = wall.at[1 - x, src, mine_rows]
        arrived(piece, r_w.at[1, src], dp=xn)
        copies.send(piece, piece, s_w.at[3, k], r_w.at[3, src], dp=cn)
    for src in sources:
        arrived(sall.at[src], r_small.at[src], dp=xn)
    for b in range(F):
        placed[b, 0:6] = sall[b, 0:6]
        for i in range(3):
            m = F * i + b
            placed[b, 6 + i : 7 + i] = sall[m // 3, 6 + m % 3 : 7 + m % 3]
        placed[b, 9:16] = jnp.zeros((7, 128), f32)
    total = jnp.zeros((16, D), f32)
    for b in range(F):
        total = total + dot(placed[b].astype(bf16), place_matrix(W, b * W, D).astype(bf16), NN)
    full[...] = total
    start = (me // 2) * (3 * HEAD) + HEAD * y
    window = (
        lax.broadcasted_iota(jnp.int32, (D, 128), 0) - start == lax.broadcasted_iota(jnp.int32, (D, 128), 1)
    ).astype(f32)
    b_qkv = dot(total.astype(bf16), window.astype(bf16), NN)
    gain_one, bias_one, gain_two, bias_two = [total[i : i + 1] for i in range(4)]
    off = 32 * y
    mine = ((lane >= off) & (lane < off + W))[0:1]

    def norm(b):
        ln_rows(xall, normed, None, b)
        n = normed[block(b)]
        first[block(b)] = (n * gain_one + bias_one).astype(bf16)
        second[block(b)] = (n * gain_two + bias_two).astype(bf16)

    up_shift = b_up[...].astype(f32).reshape(1, C)
    head = [lane // HEAD == h for h in range(2)]

    def project(b):
        p = dot(first[block(b)], wall[0].reshape(D, C), NN)
        ct, s1, s2 = tabs[0, block(b)], tabs[1, block(b)], tabs[2, block(b)]
        q = turn(p[:, :128] + b_qkv[6:7], ct, s1, s2) * 0.125
        q_s[block(b)] = q.astype(bf16)
        k_s[block(b)] = turn(p[:, 128:256] + b_qkv[7:8], ct, s1, s2).astype(bf16)
        v_s[block(b)] = (p[:, 256:] + b_qkv[8:9]).astype(bf16)
        u = dot(second[block(b)], wall[1].reshape(D, C), NN) + up_shift
        cdf = 0.5 * (1.0 + lax.erf(u * inv_root_two))
        hidden[block(b)] = (u * cdf).astype(bf16)
        slope[block(b)] = cdf + u * jnp.exp(-0.5 * u * u) * inv_root_twopi

    other_rows = pl.ds(pl.multiple_of((1 - c) * half, half), half)
    for j, b in enumerate(near):
        tokens.got(2 * b + 1 - y)
        norm(b)
        if j == 1:
            grads.step(1)
            for src in sources:
                arrived(wall.at[x, src, other_rows], r_w.at[2, src], dp=cn)
                arrived(wall.at[1 - x, src, other_rows], r_w.at[3, src], dp=cn)
            arrived(outwin.at[pl.ds(pl.multiple_of(W * (1 - y), 32), 32)], r_o, fsdp=z * 2 + 1 - y)
            project(near[0])
        if j:
            project(b)
    grads.step(2)

    def seen():
        r = lax.broadcasted_iota(jnp.int32, (RB, RB), 0)
        return lax.broadcasted_iota(jnp.int32, (RB, RB), 1) <= r

    def attend(b):
        kv = (b + 1) * RB
        rows = slice(b * RB, kv)
        halves = []
        for h in range(2):
            q = jnp.where(head[h], q_s[rows], jnp.zeros((), bf16))
            s = dot(q, k_s[:kv], NT)
            last = jnp.where(seen(), s[:, kv - RB :], -1e30)
            top = jnp.max(last, axis=-1, keepdims=True)
            if b:
                top = jnp.maximum(top, jnp.max(s[:, : kv - RB], axis=-1, keepdims=True))
            e_last = jnp.exp(last - top)
            norm = jnp.sum(e_last, axis=-1, keepdims=True)
            if b:
                e_rest = jnp.exp(s[:, : kv - RB] - top)
                norm = norm + jnp.sum(e_rest, axis=-1, keepdims=True)
            inv = 1.0 / norm
            probs[h, rows, kv - RB : kv] = (e_last * inv).astype(bf16)
            if b:
                probs[h, rows, : kv - RB] = (e_rest * inv).astype(bf16)
            halves.append(dot(probs[h, rows, :kv], v_s[:kv], NN))
        a = jnp.where(head[0], halves[0], halves[1])
        att[rows] = a
        att_low[rows] = jnp.where(mine, a, 0.0).astype(bf16)
        p = dot(att_low[rows], outwin[...], NN) + dot(hidden[rows], downw[...], NN)
        part[2 * b : 2 * b + 2] = p.astype(bf16).reshape(2, RB // 2, D)

    one = Collect(copies, part, yb.at[0], zb.at[0], sb.at[0], sems.at[0], branch_out, Z, z, y)
    for b in range(NB):
        attend(b)
        if b == 1:
            for k in range(3, Z):
                grads.step(k)
    far = near[::-1]
    for b in far:
        one.push(b)

    vec[...] = jnp.zeros_like(vec)

    def back(b):
        g = gall[pl.ds(2 * b, 2)].reshape(RB, D)
        gp = (dot(g, downw[...], NT) * slope[block(b)]).astype(bf16)
        gpre[block(b)] = gp
        gatt[block(b)] = dot(g, outwin[...], NT).astype(bf16)
        gs = dot(gp, wall[1].reshape(D, C), NT)
        n = normed[block(b)]
        vec[2:3] += jnp.sum(gs * n, axis=0, keepdims=True)
        vec[3:4] += jnp.sum(gs, axis=0, keepdims=True)
        vec[7:8] += jnp.sum(g.astype(f32), axis=0, keepdims=True)
        gsec[block(b)] = gs * gain_two
        sums = jnp.sum(gp.astype(f32), axis=0, keepdims=True)
        for i in range(C // 128):
            own_vec[1 + i : 2 + i] += sums[:, i * 128 : (i + 1) * 128]

    own_vec[...] = jnp.zeros_like(own_vec)
    for b in near:
        grads.got(2 * b + 1 - y)
        back(b)

    g_flat = gall[...].reshape(S, D)
    down_grad = dot(hidden[...], g_flat, TN).astype(bf16)
    q4 = C // 2
    for i in range(2):
        for j in range(2):
            g_own[i, j, half:] = down_grad[j * q4 : (j + 1) * q4, i * C : (i + 1) * C]
    gout_win[...] = dot(att_low[...], g_flat, TN).astype(bf16)
    for i in range(2):
        for j in range(2):
            g_own[i, j, :half] = gout_win[pl.ds(pl.multiple_of(off + j * half, 16), half), i * C : (i + 1) * C]
    for i in range(2):
        copies.send(g_own.at[i, 1 - c], co_buf.at[i], s_co.at[i], r_co.at[i], dp=cn)

    def matrix(m, left, right):
        g = dot(left[...], right[...], TN).astype(bf16).reshape(F, 2, half, C)
        for j in range(2):
            g_mat[m, j] = g[:, j].reshape(F * half, C)
        copies.send(g_mat.at[m, 1 - c], cbuf.at[m], s_c.at[m], r_c.at[m], dp=cn)

    def matrix_x(m):
        arrived(cbuf.at[m], r_c.at[m], dp=cn)
        add_rows(hbuf.at[m], [g_mat.at[m, c], cbuf.at[m]])
        copies.send(hbuf.at[m], xbuf.at[m], s_x.at[m], r_x.at[m], x != m, dp=xn)

    def matrix_spread(m):
        own = x == m

        @pl.when(own)
        def _():
            arrived(xbuf.at[m], r_x.at[m], dp=xn)
            add_rows(hbuf.at[m], [hbuf.at[m], xbuf.at[m]])
            here = pl.ds(pl.multiple_of(me * half, half), half)
            ret[m, c, here] = hbuf[m, here]

        for k, o in enumerate(others):
            there = pl.ds(pl.multiple_of(o * half, half), half)
            here = pl.ds(pl.multiple_of(me * half, half), half)
            copies.send(hbuf.at[m, there], ret.at[m, c, here], s_a.at[m, k], r_a.at[m, me], own, fsdp=o)

    def matrix_share(m, by_owner):
        act = (x == m) == by_owner
        for k, src in enumerate([me] + sources):
            piece = ret.at[m, c, pl.ds(pl.multiple_of(src * half, half), half)]
            if k or not by_owner:

                @pl.when(act)
                def _():
                    arrived(piece, r_a.at[m, src], dp=xn)

            if by_owner:
                copies.send(piece, piece, s_cc.at[m, 0, k], r_a.at[m, src], act, dp=xn)
            copies.send(piece, piece, s_cc.at[m, 1, k], r_cc.at[m, src], act, dp=cn)

    matrix(1, second, gpre)
    one.step(far[0])
    for i in range(2):
        arrived(co_buf.at[i], r_co.at[i], dp=cn)
        add_rows(ho_buf.at[i], [g_own.at[i, c], co_buf.at[i]])
    copies.send(ho_buf.at[1 - x], xo_buf, s_xo, r_xo, dp=xn)
    matrix_x(1)

    def attend_back(b):
        kv = (b + 1) * RB
        rows = slice(b * RB, kv)
        ga, a = gatt[rows], att[rows]
        prod = ga.astype(f32) * a
        q_grad = None
        for h in range(2):
            delta = jnp.sum(jnp.where(head[h], prod, 0.0), axis=-1, keepdims=True)
            gah = jnp.where(head[h], ga, jnp.zeros((), bf16))
            qh = jnp.where(head[h], q_s[rows], jnp.zeros((), bf16))
            p = probs[h, rows, :kv]
            gp = dot(gah, v_s[:kv], NT)
            gs_f = p.astype(f32) * (gp - delta)
            last = jnp.where(seen(), gs_f[:, kv - RB :], 0.0).astype(bf16)
            gs = jnp.concatenate([gs_f[:, : kv - RB].astype(bf16), last], axis=1) if b else last
            dq = dot(gs, k_s[:kv], NN)
            q_grad = dq if h == 0 else jnp.where(head[0], q_grad, dq)
            gk[:kv] += dot(gs, qh, TN)
            gv[:kv] += dot(p, gah, TN)
        gq[rows] = q_grad

    def back_project(b):
        ct, s1, s2 = tabs[0, block(b)], tabs[1, block(b)], tabs[2, block(b)]
        dq = turn(gq[block(b)] * 0.125, ct, -s1, -s2)
        dk = turn(gk[block(b)], ct, -s1, -s2)
        for i, t in enumerate((dq, dk, gv[block(b)])):
            low = jnp.where(mine, t, 0.0).astype(bf16)
            gproj[block(b), i * 128 : (i + 1) * 128] = low
            own_vec[8 + i : 9 + i] += jnp.sum(low.astype(f32), axis=0, keepdims=True)

    def back_norm(b):
        gf = dot(gproj[block(b)], wall[0].reshape(D, C), NT)
        n = normed[block(b)]
        vec[0:1] += jnp.sum(gf * n, axis=0, keepdims=True)
        vec[1:2] += jnp.sum(gf, axis=0, keepdims=True)
        mixed[pl.ds(2 * b, 2)] = (gf * gain_one + gsec[block(b)]).astype(bf16).reshape(2, RB // 2, D)

    gk[...] = jnp.zeros_like(gk)
    gv[...] = jnp.zeros_like(gv)
    two = Collect(copies, mixed, yb.at[1], zb.at[1], sb.at[1], sems.at[1], mixed_out, Z, z, y)
    attend_back(3)
    attend_back(2)
    one.step(far[1])
    arrived(xo_buf, r_xo, dp=xn)
    owner = ret_own.at[x, c]
    add_rows(owner, [ho_buf.at[x], xo_buf])
    copies.send(owner, owner, s_fo.at[0], r_fo.at[0], dp=xn)
    copies.send(owner, owner, s_fo.at[1], r_fo.at[1], dp=cn)
    matrix_spread(1)
    attend_back(1)
    attend_back(0)
    for b in range(NB):
        back_project(b)
    matrix(0, first, gproj)
    for j, b in enumerate(far):
        back_norm(b)
        two.push(b)
    matrix_x(0)
    one.step(far[2])
    two.step(far[0])

    vec[4:7] = exact(own_vec[8:16], window, NT)[0:3]
    pieces = [exact(vec[...], place_matrix(W, b * W, D), NT) for b in range(F)]
    for b in range(F):
        vecs[b, 0:4] = pieces[b][0:4]
        for j in range(3):
            m = 3 * b + j
            vecs[b, 4 + j : 5 + j] = pieces[m % F][4 + m // F : 5 + m // F]
        vecs[b, 7:8] = jnp.zeros((1, 128), f32)
    own_vec[0:1] = exact(vec[...], place_matrix(W, me * W, D), NT)[7:8]
    vbuf[me] = vecs[me]
    for k, o in enumerate(others):
        copies.send(vecs.at[o], vbuf.at[me], s_v.at[k], r_v.at[me], fsdp=o)
    matrix_spread(0)
    two.step(far[1])
    matrix_share(1, True)
    two.step(far[2])
    for src in sources:
        arrived(vbuf.at[src], r_v.at[src], dp=xn)
    total = vbuf[0]
    for g in range(1, F):
        total = total + vbuf[g]
    vtot[d, :8] = total
    vtot[d, 8:] = own_vec[0:8]
    for k, to in enumerate((xn, cn, dn)):
        copies.send(vtot.at[d], vtot.at[d], s_d.at[k], r_d.at[d], dp=to)
    one.finish()
    matrix_share(0, True)
    matrix_share(1, False)
    matrix_share(0, False)
    arrived(ret_own.at[1 - x, c], r_fo.at[0], dp=xn)
    copies.send(ret_own.at[1 - x, c], ret_own.at[1 - x, c], s_fo.at[2], r_fo.at[2], dp=cn)
    two.finish()
    for to in (xn, cn, dn):
        arrived(vtot.at[to], r_d.at[to], dp=to)
    vec_sum[...] = vtot[0] + vtot[1] + vtot[2] + vtot[3]
    arrived(ret_own.at[x, 1 - c], r_fo.at[1], dp=cn)
    arrived(ret_own.at[1 - x, 1 - c], r_fo.at[2], dp=cn)
    for m in range(2):
        for g in range(F):
            arrived(ret.at[m, 1 - c, pl.ds(g * half, half)], r_cc.at[m, g], dp=cn)
    copies.drain()


def layer(F, tok, cot, qkv, up, outw, downw, *vectors):
    rows, D = tok.shape
    W, FF = up.shape
    C = FF // F
    S, Z, half = rows * F, F // 2, W // 2
    own = (W + C) // 2
    dma = pltpu.SemaphoreType.DMA
    low = lambda *s: pltpu.VMEM(s, bf16)
    wide = lambda *s: pltpu.VMEM(s, f32)
    return pl.pallas_call(
        functools.partial(layer_kernel, F),
        out_shape=(
            jax.ShapeDtypeStruct((rows, D), f32),
            jax.ShapeDtypeStruct((rows, D), f32),
            jax.ShapeDtypeStruct((2, 2, F * half, C), bf16),
            jax.ShapeDtypeStruct((2, 2, own, C), bf16),
            jax.ShapeDtypeStruct((16, 128), f32),
            jax.ShapeDtypeStruct((16, D), f32),
        ),
        in_specs=[pl.BlockSpec(memory_space=pl.ANY)] * 6 + [vmem()] * 8,
        out_specs=(vmem(),) * 6,
        scratch_shapes=[
            low(F, rows, D), low(F, rows, D), wide(F, 16, 128), low(2, F, W, C), low(128, D), low(2, F, W, C),
            wide(F, 16, 128),
            wide(3, S, 128), wide(S, D), low(S, D), low(S, D), low(S, 128), low(S, 128), low(S, 128), low(2, S, S),
            wide(S, 128), low(S, 128), low(S, C), wide(S, C), low(F, rows, D), low(S, C), low(S, 128), wide(S, D),
            low(F, rows, D),
            low(S, 3 * 128), wide(S, 128), wide(S, 128), wide(S, 128), low(128, D), low(2, 2, F * half, C),
            low(2, 2, own, C), wide(8, D), wide(F, 8, 128), wide(16, 128),
            low(W, 3 * D), low(W, FF), low(W, D), low(C, D), wide(16, 128),
            low(2, Z, rows, D), low(2, Z, rows, D), low(2, Z, rows, D),
            low(2, F * half, C), low(2, F * half, C), low(2, F * half, C),
            low(2, own, C), low(2, own, C), low(own, C), wide(F, 8, 128), wide(4, 16, 128),
            dma((3, F)), dma((F,)), dma((3, F)), dma((F,)), dma((F,)), dma((F,)), dma((4, F)), dma((4, F)), dma, dma,
            dma((2, 4, Z)),
            dma((2,)), dma((2,)), dma((2,)), dma((2,)), dma((2, F)), dma((2, F)), dma((2, 2, F)), dma((2, F)),
            dma((2,)), dma((2,)), dma, dma, dma((3,)), dma((3,)), dma((F,)), dma((F,)), dma((3,)), dma((4,)),
            dma((6,)),
        ],
        compiler_params=pltpu.CompilerParams(
            collective_id=0, has_side_effects=True, vmem_limit_bytes=60 * 2**20
        ),
        name="layer",
    )(tok, cot, qkv, up, outw, downw, *vectors)


def finish_kernel(
    F, tok_in, cot_in, branch_in, mixed_in, ret_in, own_in, full, vec_sum, out, igrad, g_qkv, g_out, g_up, g_down,
    o0, o1, o2, o3, o_qkv, o_out, o_up, o_down, ret_own, ret, tok, cot, branch, mixed,
    w_out, w_igrad, w_qkv, w_out_grad, w_up, w_down, sem, out_sem,
):
    fetches = [
        pltpu.make_async_copy(src, dst, sem.at[i])
        for i, (src, dst) in enumerate(
            (
                (own_in, ret_own), (ret_in, ret), (tok_in, tok), (cot_in, cot), (branch_in, branch), (mixed_in, mixed)
            )
        )
    ]
    for fetch in fetches:
        fetch.start()
    W, D = g_out.shape
    C = ret.shape[3]
    for i, o in enumerate((o0, o1, o2, o3)):
        o[...] = vec_sum[i : i + 1, :W].reshape(W)
    o_qkv[...] = jnp.concatenate([vec_sum[4 + i : 5 + i, :W] for i in range(3)], axis=1).reshape(3 * W)
    o_out[...] = vec_sum[8:9, :W].reshape(W)
    o_down[...] = vec_sum[8:9, :W].reshape(W)
    o_up[...] = jnp.concatenate([vec_sum[9 + i : 10 + i] for i in range(C // 128)], axis=1).reshape(C)
    outs = (w_out, w_igrad, w_qkv, w_out_grad, w_up, w_down)
    writes = [
        pltpu.make_async_copy(src, dst, out_sem.at[i])
        for i, (src, dst) in enumerate(zip(outs, (out, igrad, g_qkv, g_out, g_up, g_down)))
    ]
    half = W // 2
    fetches[0].wait()
    for j in range(2):
        rows = slice(j * half, (j + 1) * half)
        for i in range(2):
            columns = slice(i * C, (i + 1) * C)
            w_down[j * (C // 2) : (j + 1) * (C // 2), columns] = ret_own[i, j, half:].astype(f32)
            w_out_grad[rows, columns] = ret_own[i, j, :half].astype(f32)
    writes[5].start()
    writes[3].start()
    fetches[1].wait()
    for j in range(2):
        rows = slice(j * half, (j + 1) * half)
        for g in range(F):
            w_up[rows, g * C : (g + 1) * C] = ret[1, j, g * half : (g + 1) * half].astype(f32)
    writes[4].start()
    row = lax.broadcasted_iota(jnp.int32, (128, D), 0)
    col = lax.broadcasted_iota(jnp.int32, (128, D), 1)
    totals = [jnp.zeros((W, D), f32)] * 3
    for g in range(F):
        s = g * W // HEAD * HEAD
        place = ((row + s == col) & (col >= g * W) & (col < (g + 1) * W)).astype(bf16)
        for i in range(3):
            piece = jnp.concatenate(
                [ret[0, j, g * half : (g + 1) * half, i * 128 : (i + 1) * 128] for j in range(2)], axis=0
            )
            totals[i] = totals[i] + dot(piece, place, NN)
    for i in range(3):
        w_qkv[:, i * D : (i + 1) * D] = totals[i]
    writes[2].start()
    for fetch in fetches[2:]:
        fetch.wait()
    x = tok[...].astype(f32)
    center = x - jnp.mean(x, axis=-1, keepdims=True)
    inverse = lax.rsqrt(jnp.mean(center * center, axis=-1, keepdims=True) + epsilon)
    n = center * inverse
    w_out[...] = (x + branch[...] + full[4:5] + full[5:6]).astype(bf16)
    writes[0].start()
    m = mixed[...]
    m = m - jnp.mean(m, axis=-1, keepdims=True) - n * jnp.mean(m * n, axis=-1, keepdims=True)
    w_igrad[...] = cot[...].astype(f32) + inverse * m
    writes[1].start()
    for write in writes:
        write.wait()


def finish(F, tok, cot, branch, mixed, ret, ret_own, full, vec_sum):
    rows, D = tok.shape
    W = D // F
    C = ret.shape[3]
    big = (
        jax.ShapeDtypeStruct((rows, D), bf16),
        jax.ShapeDtypeStruct((rows, D), f32),
        jax.ShapeDtypeStruct((W, 3 * D), f32),
        jax.ShapeDtypeStruct((W, D), f32),
        jax.ShapeDtypeStruct((W, F * C), f32),
        jax.ShapeDtypeStruct((C, D), f32),
    )
    anywhere = pl.BlockSpec(memory_space=pl.ANY)
    return pl.pallas_call(
        functools.partial(finish_kernel, F),
        out_shape=big
        + tuple(jax.ShapeDtypeStruct((n,), f32) for n in (W, W, W, W, 3 * W, W, C, W)),
        in_specs=[anywhere] * 6 + [vmem()] * 2,
        out_specs=(anywhere,) * 6 + (vmem(),) * 8,
        scratch_shapes=[
            pltpu.VMEM(a.shape, a.dtype) for a in (ret_own, ret, tok, cot, branch, mixed) + big
        ]
        + [pltpu.SemaphoreType.DMA((6,))] * 2,
        compiler_params=pltpu.CompilerParams(vmem_limit_bytes=60 * 2**20),
        name="finish",
    )(tok, cot, branch, mixed, ret, ret_own, full, vec_sum)


def fast_body(
    tokens, ln1_gain, ln1_bias, ln2_gain, ln2_bias, qkv_weight, qkv_bias, out_weight, out_bias, up_weight, up_bias,
    down_weight, down_bias, cotangent,
):
    F = lax.axis_size("fsdp")
    branch, mixed, ret, ret_own, vec_sum, full = layer(
        F, tokens[0], cotangent[0], qkv_weight, up_weight, out_weight, down_weight,
        ln1_gain, ln1_bias, ln2_gain, ln2_bias, out_bias, down_bias, qkv_bias, up_bias,
    )
    out, igrad, g_qkv, g_out, g_up, g_down, o0, o1, o2, o3, o_qkv, o_out, o_up, o_down = finish(
        F, tokens[0], cotangent[0], branch, mixed, ret, ret_own, full, vec_sum
    )
    return (
        out[None], igrad[None], o0, o1, o2, o3, g_qkv, o_qkv, g_out, o_out, g_up, o_up, g_down, o_down
    )


def solution(mesh):
    row = P("fsdp", None)
    vec = P("fsdp")
    act = P("dp", "fsdp", None)
    fast = mesh.shape["fsdp"] == 8 and mesh.shape["dp"] == 4
    return jax.shard_map(
        fast_body if fast else body,
        mesh=mesh,
        in_specs=(act, vec, vec, vec, vec, row, vec, row, vec, row, vec, row, vec, act),
        out_specs=(act, act, vec, vec, vec, vec, row, vec, row, vec, row, vec, row, vec),
        check_vma=False,
    )
```
